32 devices in a mesh: groups: 1, context: 8 (over y, x, core), span: 4 (over z).
Axes of the slice: x: 2, y: 2, z: 4, core: 2. Of those that a mesh axis runs over, the one named last changes fastest.
Arguments:
- raw_tokens: bfloat16 [1536, 2048], P(('groups', 'context'), 'span'), may hold values from -6 to 6
- keep: int32 [8, 32], P(('groups', 'context')), may hold values from -1 to 191, as said below
- attn_gain: float32 [2048], replicated, may hold values from 0.25 to 1.75
- query_weight: bfloat16 [2048, 4608], P(None, 'span'), may hold values from -5 to 5
- latent_weight: bfloat16 [2048, 576], P(None, 'span'), may hold values from -0.5 to 0.5
- kv_gain: float32 [512], replicated, may hold values from 0.25 to 1.75
- out_weight: bfloat16 [4096, 2048], P('span', 'context'), may hold values from -0.25 to 0.25
- moe_gain: float32 [2048], replicated, may hold values from 0.25 to 1.75
- expert_ids: int32 [256, 6], P(('groups', 'context', 'span')), may hold values from 0 to 15, all different within a row; in each aligned block of 8 rows (0 to 7, 8 to 15, ...) at most 6 rows name the same one
- gate_values: float32 [256, 6], P(('groups', 'context', 'span')), may hold values from 0.05 to 0.5
- expert_slot: int32 [16], replicated, may hold values from 0 to 15, each once
- expert_in: bfloat16 [32, 2, 2048, 704], P(('context', 'span')), may hold values from -0.125 to 0.125
- expert_out: bfloat16 [32, 704, 2048], P(('context', 'span')), may hold values from -0.15625 to 0.15625
Outputs:
- layer_out: bfloat16 [256, 2048], P(('groups', 'context', 'span'))
- latent_cache: bfloat16 [256, 576], P(('groups', 'context'))
The draws below stay inside these ranges and needn't reach their ends.
Inputs may be any that keep to these rules, and one draw needn't show every extreme that they name: `keep`: row c lists the kept positions among the 192 raw tokens of span c in increasing order, then -1 in the empty entries; every span keeps 32 // 2 or more, and in every draw some span keeps 32. `expert_ids`: in each aligned block of 8 rows (the rows of one device) no expert is named more than 6 times, a bound that some block reaches. `expert_slot`: each stored slot holds exactly one routed expert.
All inputs are finite; a program needn't handle non-finite values.
Results may differ from the reference program's by a relative error of at most 0.013.
Values may be sent and summed in bfloat16 or wider, within the bound.
No kernel may reach another device: no remote copies, remote signals or barrier semaphores. Data moves between devices by JAX's collectives and lax.ppermute only.
A program may use at most 64 MiB of HBM per device.

```python
import math
import jax
import jax.numpy as jnp
import numpy as np
from jax import lax

D = 2048
HEADS = 8
KV_RANK = 512
ROPE = 64
LATENT = 576
HID = 1408
HALF = 704
EXPERTS = 16
TOP = 6
ROWS_DEV = 8
KEEP_C = 32
RAW_C = 192
TOKENS = 256
CAP = 6
N_CONTEXT = 8


def latent_base(key):
    return jax.random.truncated_normal(jax.random.fold_in(key, 11), -4.0, 4.0, (D, LATENT), jnp.float32) / math.sqrt(D)


def draw_latent_weight(key, part):
    return latent_base(key).astype(jnp.bfloat16)


def draw_query_weight(key, part):
    drawn = jax.random.truncated_normal(jax.random.fold_in(key, 23), -4.0, 4.0, (D, HEADS, LATENT), jnp.float32) / math.sqrt(D)
    return drawn.reshape(D, HEADS * LATENT).astype(jnp.bfloat16)


def draw_keep(key, part):
    span_keys = jax.random.split(jax.random.fold_in(key, 3), N_CONTEXT)
    orders = jax.vmap(lambda sub: jax.random.permutation(sub, RAW_C))(span_keys)[:, :KEEP_C].astype(jnp.int32)
    counts = jax.random.randint(jax.random.fold_in(key, 5), (N_CONTEXT,), KEEP_C // 2, KEEP_C + 1).astype(jnp.int32)
    fullest = jax.random.randint(jax.random.fold_in(key, 7), (), 0, N_CONTEXT).astype(jnp.int32)
    counts = jnp.where(jnp.arange(N_CONTEXT, dtype=jnp.int32) == fullest, KEEP_C, counts)
    entry = jnp.arange(KEEP_C, dtype=jnp.int32)[None, :]
    chosen = jnp.where(entry < counts[:, None], orders, RAW_C)
    chosen = jnp.sort(chosen, axis=1)
    return jnp.where(chosen >= RAW_C, -1, chosen).astype(jnp.int32)


def steps_of(rng, dims, cuts, low, top_value):
    def one(position, shards_of):
        heights = jax.random.uniform(jax.random.fold_in(jax.random.fold_in(rng, 6), position), (shards_of,), jnp.float32, low / len(cuts), top_value / len(cuts))
        return jnp.repeat(jnp.exp(heights), dims[position] // shards_of).reshape((-1,) + (1,) * (len(dims) - position - 1))

    level = one(*cuts[0])
    for cut in cuts[1:]:
        level = level * one(*cut)
    return level


def routed_block(key, own, number, rows, count, top, limit, skew):
    ranking = jax.random.permutation(key, count)
    heavy_load, ordinary = portions_of(count, rows * top, limit, skew, True), portions_of(count, rows * top, limit, skew, False)
    places = jnp.arange(count)

    def named(lengths, offset_by):
        used = int((lengths > 0).sum())
        fixed = max(1, used // 4)
        passed = fixed + (places - fixed + offset_by * (used - fixed)) % max(1, count - fixed)
        return jnp.zeros((count,), jnp.int32).at[ranking[jnp.where(places < fixed, places, passed)]].set(jnp.asarray(lengths, jnp.int32))

    lengths = jnp.where(number % 4 == 0, named(heavy_load, number // 4), named(ordinary, number - number // 4 - 1))
    mixed = jax.random.permutation(jax.random.fold_in(own, 3), count)
    giver, sink = mixed[0:count // 2 * 2:2], mixed[1:count // 2 * 2:2]
    room = jnp.minimum(lengths[giver] - 1, limit - lengths[sink]) // 2
    room = jnp.where((giver == ranking[0]) | (sink == ranking[0]) | (lengths[sink] == 0), 0, jnp.maximum(room, 0))
    passed = jax.random.randint(jax.random.fold_in(own, 4), (count // 2,), 0, 1 << 20) % (room + 1)
    lengths = lengths.at[giver].add(-passed).at[sink].add(passed)
    members = jnp.searchsorted(jnp.cumsum(lengths), jnp.arange(rows * top), side="right").astype(jnp.int32)
    listing = members.reshape(top, rows).T
    listing = listing[jax.random.permutation(jax.random.fold_in(own, 1), rows)]
    offset_by = jax.random.randint(jax.random.fold_in(own, 2), (rows, 1), 0, top)
    return jnp.take_along_axis(listing, (jnp.arange(top)[None, :] + offset_by) % top, axis=1)


def portions_of(number_of, total, limit, slope, full):
    portions = [(1 << 20) // math.isqrt(rank ** slope) + 1 for rank in range(1, number_of + 1)]
    largest = limit if full else min(limit, max(-(-total // number_of), total * portions[0] // sum(portions)))
    least = 1 if total - largest >= number_of - 1 else 0
    holding, spare = [largest] + [least] * (number_of - 1), total - largest - least * (number_of - 1)
    while spare > 0:
        candidates = [i for i in range(1, number_of) if holding[i] < largest] or [i for i in range(1, number_of) if holding[i] < limit]
        whole, budget = sum([portions[i] for i in candidates]), spare
        for i in candidates:
            addition = min(limit - holding[i], max(1, budget * portions[i] // whole), spare)
            holding[i] = holding[i] + addition
            spare = spare - addition
    return np.array(holding)


def bell_draw(own_key, extent, width, bound, cuts=(), kind=jnp.bfloat16):
    entries = width * jax.random.normal(own_key, extent, jnp.float32)
    if cuts:
        entries = entries * steps_of(own_key, extent, cuts, -0.22, 0.18)
    return jnp.clip(entries, -bound, bound).astype(kind)


def setup_inputs(seed: int = 0, part: int = 0) -> dict:
    arg_keys = jax.random.split(jax.random.key(seed), 14)
    own_keys = jax.random.split(jax.random.fold_in(arg_keys[13], part), 14)
    raw_tokens = bell_draw(own_keys[0], (N_CONTEXT * RAW_C, D), 1.0, 6.0, ((0, 8), (1, 4)))
    keep = draw_keep(jax.random.fold_in(jax.random.fold_in(arg_keys[13], part), 71), part)
    attn_gain = jnp.clip(1.0 + 0.15 * jax.random.normal(arg_keys[2], (D,), jnp.float32), 0.25, 1.75)
    query_weight = draw_query_weight(jax.random.fold_in(arg_keys[13], 71), part)
    latent_weight = draw_latent_weight(jax.random.fold_in(arg_keys[13], 71), part)
    kv_gain = jnp.clip(1.0 + 0.15 * jax.random.normal(arg_keys[5], (KV_RANK,), jnp.float32), 0.25, 1.75)
    out_weight = bell_draw(arg_keys[6], (HEADS * KV_RANK, D), KV_RANK ** -0.5, 0.25, ((0, 4), (1, 8)))
    moe_gain = jnp.clip(1.0 + 0.15 * jax.random.normal(arg_keys[7], (D,), jnp.float32), 0.25, 1.75)
    expert_ids_keys = jax.random.split(jax.random.fold_in(own_keys[8], 1), TOKENS // ROWS_DEV)
    expert_ids_turns = jax.random.permutation(jax.random.fold_in(own_keys[8], 3), TOKENS // ROWS_DEV)
    expert_ids = jax.vmap(lambda own, number: routed_block(jax.random.fold_in(own_keys[8], 2), own, number, ROWS_DEV, EXPERTS, TOP, CAP, 2))(expert_ids_keys, expert_ids_turns).reshape((TOKENS, TOP))
    gate_values = jnp.clip(jnp.exp(math.log(0.5) - 2.3025851 * jax.random.uniform(own_keys[9], (TOKENS, TOP), jnp.float32) ** steps_of(own_keys[9], (TOKENS, TOP), ((0, 32),), -0.2, 0.2)), 0.05, 0.5)
    expert_slot = jax.random.permutation(arg_keys[10], EXPERTS).astype(jnp.int32)
    expert_in = bell_draw(arg_keys[11], (2 * EXPERTS, 2, D, HALF), D ** -0.5, 0.125, ((0, 32),))
    expert_out = bell_draw(arg_keys[12], (2 * EXPERTS, HALF, D), HID ** -0.5, 0.15625, ((0, 32),))
    return dict(raw_tokens=raw_tokens, keep=keep, attn_gain=attn_gain, query_weight=query_weight, latent_weight=latent_weight, kv_gain=kv_gain, out_weight=out_weight, moe_gain=moe_gain, expert_ids=expert_ids, gate_values=gate_values, expert_slot=expert_slot, expert_in=expert_in, expert_out=expert_out)


EPS = 1e-06
THETA = 50000.0
SCALE = 192.0 ** (-0.5)

def rms_scale(values, gain):
    values = values.astype(jnp.float32)
    factor = lax.rsqrt(lax.optimization_barrier(jnp.mean(values * values, axis=-1, keepdims=True)) + EPS)
    return values * factor * gain.astype(jnp.float32)

def rotary_tables(positions, rotary_width):
    half = rotary_width // 2
    freqs = THETA ** (-2.0 * jnp.arange(half, dtype=jnp.float32) / rotary_width)
    angles = positions.astype(jnp.float32)[:, None] * freqs[None, :]
    return (jnp.cos(angles), jnp.sin(angles))

def rotate(values, cosine, sine):
    half = values.shape[-1] // 2
    first = values[..., :half]
    second = values[..., half:]
    return jnp.concatenate([first * cosine - second * sine, second * cosine + first * sine], axis=-1)

def reference(raw_tokens, keep, attn_gain, query_weight, latent_weight, kv_gain, out_weight, moe_gain, expert_ids, gate_values, expert_slot, expert_in, expert_out):
    slot_count = N_CONTEXT * KEEP_C
    span_ids = jnp.arange(N_CONTEXT, dtype=jnp.int32)[:, None]
    live = (keep >= 0).reshape(slot_count)
    positions = (span_ids * RAW_C + jnp.maximum(keep, 0)).reshape(slot_count).astype(jnp.int32)
    compact = jnp.take(raw_tokens, positions, axis=0)
    compact = jnp.where(live[:, None], compact, jnp.zeros_like(compact))
    normed = rms_scale(compact, attn_gain).astype(jnp.bfloat16)
    cosine, sine = rotary_tables(positions, ROPE)
    query = jnp.dot(normed, query_weight, preferred_element_type=jnp.float32).reshape(slot_count, HEADS, LATENT)
    query = jnp.concatenate([query[..., :KV_RANK], rotate(query[..., KV_RANK:], cosine[:, None, :], sine[:, None, :])], axis=-1).astype(jnp.bfloat16)
    latent = jnp.dot(normed, latent_weight, preferred_element_type=jnp.float32)
    latent_cache = jnp.concatenate([rms_scale(latent[:, :KV_RANK], kv_gain), rotate(latent[:, KV_RANK:], cosine, sine)], axis=-1).astype(jnp.bfloat16)
    order = jnp.arange(slot_count, dtype=jnp.int32)
    allowed = (order[None, :] <= order[:, None]) & live[None, :]
    values = latent_cache[:, :KV_RANK]

    def one_head(head_query):
        scores = jnp.dot(head_query, latent_cache.T, preferred_element_type=jnp.float32) * SCALE
        scores = jnp.where(allowed, scores, -jnp.inf)
        highest = lax.optimization_barrier(jnp.max(scores, axis=1, keepdims=True))
        weights = jnp.where(allowed, jnp.exp(scores - highest), 0.0)
        denominator = lax.optimization_barrier(jnp.sum(weights, axis=1, keepdims=True))
        summed = jnp.dot(weights.astype(jnp.bfloat16), values, preferred_element_type=jnp.float32)
        return (summed / denominator).astype(jnp.bfloat16)
    mixed = lax.map(one_head, jnp.swapaxes(query, 0, 1))
    heads_out = jnp.einsum('hqd,hdm->qm', mixed.astype(jnp.float32), out_weight.reshape(HEADS, KV_RANK, D).astype(jnp.float32))
    resid = compact.astype(jnp.float32) + heads_out
    moe_in = rms_scale(resid, moe_gain).astype(jnp.bfloat16)
    blocks = slot_count // ROWS_DEV
    slots = jnp.take(expert_slot, expert_ids, axis=0).astype(jnp.int32).reshape(blocks, ROWS_DEV * TOP)
    member = (slots[:, :, None] == jnp.arange(EXPERTS, dtype=jnp.int32)[None, None, :]).astype(jnp.int32)
    place = lax.optimization_barrier(jnp.sum((jnp.cumsum(member, axis=1) - member) * member, axis=2))
    target = (slots * CAP + place).reshape(blocks, ROWS_DEV, TOP)
    block_rows = moe_in.reshape(blocks, ROWS_DEV, D).astype(jnp.float32)
    gates = gate_values.reshape(blocks, ROWS_DEV, TOP).astype(jnp.float32)
    pieces_in = expert_in.reshape(EXPERTS, 2, 2, D, HALF)
    pieces_out = expert_out.reshape(EXPERTS, 2, HALF, D)
    capacity_ids = jnp.arange(CAP, dtype=jnp.int32)

    def one_expert(routed, operands):
        stored, weights_in, weights_out = operands
        hits = target[:, :, :, None] == (stored * CAP + capacity_ids)[None, None, None, :]
        select = lax.optimization_barrier(jnp.sum(hits.astype(jnp.float32), axis=2))
        buffer = jnp.einsum('brc,brd->bcd', select, block_rows, precision=lax.Precision.HIGHEST).astype(jnp.bfloat16).reshape(blocks * CAP, D)
        result = jnp.zeros((blocks * CAP, D), jnp.float32)
        for half in range(2):
            gate = jnp.dot(buffer, weights_in[half, 0], preferred_element_type=jnp.float32)
            upper = jnp.dot(buffer, weights_in[half, 1], preferred_element_type=jnp.float32)
            hidden = (jax.nn.silu(gate) * upper).astype(jnp.bfloat16)
            part = jnp.dot(hidden, weights_out[half], preferred_element_type=jnp.float32).astype(jnp.bfloat16)
            result = result + part.astype(jnp.float32)
        result = result.reshape(blocks, CAP, D)
        combine = lax.optimization_barrier(jnp.sum(jnp.where(hits, gates[:, :, :, None], 0.0), axis=2))
        routed = routed + jnp.einsum('brc,bcd->brd', combine, result, precision=lax.Precision.HIGHEST)
        return (routed, None)
    start = jnp.zeros((blocks, ROWS_DEV, D), jnp.float32)
    routed, _ = lax.scan(one_expert, start, (jnp.arange(EXPERTS, dtype=jnp.int32), pieces_in, pieces_out))
    routed = routed.reshape(slot_count, D)
    layer_out = jnp.where(live[:, None], resid + routed, 0.0).astype(jnp.bfloat16)
    return (layer_out, latent_cache)
```

```python
import jax
import jax.numpy as jnp
from jax import lax
from jax.sharding import PartitionSpec as P

EPS = 1e-06
THETA = 50000.0
SCALE = 192.0 ** (-0.5)
NEGATIVE = -1e30
LANES = 128


def rms_scale(values, gain):
    values = values.astype(jnp.float32)
    factor = lax.rsqrt(jnp.mean(values * values, axis=-1, keepdims=True) + EPS)
    return values * factor * gain


def rotary_tables(positions, rotary_width):
    half = rotary_width // 2
    freqs = THETA ** (-2.0 * jnp.arange(half, dtype=jnp.float32) / rotary_width)
    angles = positions.astype(jnp.float32)[:, None] * freqs[None, :]
    return (jnp.cos(angles), jnp.sin(angles))


def rotate(values, cosine, sine):
    half = values.shape[-1] // 2
    first = values[..., :half]
    second = values[..., half:]
    return jnp.concatenate(
        [first * cosine - second * sine, second * cosine + first * sine], axis=-1
    )


def partner(values, axis, mask):
    count = lax.axis_size(axis)
    return lax.ppermute(values, axis, [(i, i ^ mask) for i in range(count)])


def natural(parts, index):
    bit = 1
    while bit < len(parts):
        swap = (index & bit) != 0
        parts = [jnp.where(swap, parts[k ^ bit], parts[k]) for k in range(len(parts))]
        bit *= 2
    return parts


def per_device(
    raw_tokens,
    keep,
    attn_gain,
    query_weight,
    latent_weight,
    kv_gain,
    out_weight,
    moe_gain,
    expert_ids,
    gate_values,
    expert_slot,
    expert_in,
    expert_out,
):
    kv_rank = kv_gain.shape[0]
    spans = lax.axis_size("span")
    contexts = lax.axis_size("context")
    latent_part_width = latent_weight.shape[1]
    latent_width = latent_part_width * spans
    model_width = attn_gain.shape[0]
    keep_count = keep.shape[1]
    raw_rows = raw_tokens.shape[0]
    heads_here = query_weight.shape[1] // latent_width
    rows_dev = expert_ids.shape[0]
    experts = expert_slot.shape[0]
    context_index = lax.axis_index("context")
    span_index = lax.axis_index("span")
    evens = list(range(0, contexts, 2))
    order = evens + [i + 1 for i in evens]

    listing = keep[0]
    live = listing >= 0
    clamped = jnp.maximum(listing, 0)
    positions = context_index * raw_rows + clamped
    picked = jnp.take(raw_tokens, clamped, axis=0)
    picked = jnp.where(live[:, None], picked, jnp.zeros_like(picked))
    parts = [picked] + [partner(picked, "span", k) for k in range(1, spans)]
    weights_even = [out_weight] + [partner(out_weight, "context", i) for i in evens[1:]]
    weights_odd = [partner(w, "context", 1) for w in weights_even]
    head_weights = weights_even + weights_odd
    compact = jnp.concatenate(natural(parts, span_index), axis=1)
    normed = rms_scale(compact, attn_gain).astype(jnp.bfloat16)
    cosine, sine = rotary_tables(positions, latent_width - kv_rank)

    expert_range = jnp.arange(experts, dtype=jnp.int32)
    chosen = expert_ids[:, :, None] == expert_range[None, None, :]
    slots = jnp.sum(jnp.where(chosen, expert_slot[None, None, :], 0), axis=-1)
    gates = jnp.sum(
        jnp.where(slots[:, :, None] == expert_range[None, None, :], gate_values[:, :, None], 0.0),
        axis=1,
    )
    latent_part = jnp.dot(normed, latent_weight, preferred_element_type=jnp.float32)
    width = max(latent_part_width, experts)
    sent = jnp.concatenate(
        [
            jnp.pad(latent_part, ((0, 0), (0, width - latent_part_width))),
            jnp.pad(gates, ((0, 0), (0, width - experts))),
        ],
        axis=0,
    )
    parts = [sent] + [partner(sent, "span", k) for k in range(1, spans)]
    parts = natural(parts, span_index)
    latent = jnp.concatenate([p[:keep_count, :latent_part_width] for p in parts], axis=1)
    span_gates = jnp.concatenate([p[keep_count:, :experts] for p in parts], axis=0)
    query = jnp.dot(normed, query_weight, preferred_element_type=jnp.float32).reshape(
        keep_count, heads_here, latent_width
    )
    query = jnp.concatenate(
        [query[..., :kv_rank], rotate(query[..., kv_rank:], cosine[:, None, :], sine[:, None, :])],
        axis=-1,
    ).astype(jnp.bfloat16)
    cached = jnp.concatenate(
        [rms_scale(latent[:, :kv_rank], kv_gain), rotate(latent[:, kv_rank:], cosine, sine)],
        axis=-1,
    ).astype(jnp.bfloat16)

    gates_high = span_gates.astype(jnp.bfloat16)
    gates_low = (span_gates - gates_high.astype(jnp.float32)).astype(jnp.bfloat16)
    sent = jnp.concatenate(
        [cached, gates_high, gates_low, live.astype(jnp.bfloat16)[:, None]], axis=1
    )
    used = sent.shape[1]
    sent = jnp.pad(sent, ((0, 0), (0, -used % LANES)))
    mine = jnp.concatenate([sent] + [partner(sent, "context", i) for i in evens[1:]], axis=0)
    theirs = partner(mine, "context", 1)
    rows_all = jnp.concatenate([mine, theirs], axis=0)
    key_rows = rows_all[:, :latent_width]
    all_gates = rows_all[:, latent_width : latent_width + experts].astype(jnp.float32) + rows_all[
        :, latent_width + experts : latent_width + 2 * experts
    ].astype(jnp.float32)
    key_live = rows_all[:, used - 1] > 0
    local = jnp.arange(keep_count, dtype=jnp.int32)
    key_ids = jnp.concatenate([(context_index ^ i) * keep_count + local for i in order])
    query_ids = context_index * keep_count + local
    allowed = (key_ids[None, :] <= query_ids[:, None]) & key_live[None, :]
    scores = jnp.einsum("qhd,kd->hqk", query, key_rows, preferred_element_type=jnp.float32) * SCALE
    scores = jnp.where(allowed[None], scores, NEGATIVE)
    highest = jnp.max(scores, axis=-1)
    weights = jnp.where(allowed[None], jnp.exp(scores - highest[..., None]), 0.0)
    denominator = jnp.sum(weights, axis=-1)
    summed = jnp.einsum(
        "hqk,kd->qhd",
        weights.astype(jnp.bfloat16),
        key_rows[:, :kv_rank],
        preferred_element_type=jnp.float32,
    )
    mixed = (
        (summed / denominator.T[..., None])
        .astype(jnp.bfloat16)
        .reshape(keep_count, heads_here * kv_rank)
    )

    partial = jnp.concatenate(
        [
            jnp.dot(mixed, w, preferred_element_type=jnp.float32).astype(jnp.bfloat16)
            for w in head_weights
        ],
        axis=1,
    )
    attended = partial.astype(jnp.float32)
    for k in range(1, spans):
        attended = attended + partner(partial, "span", k).astype(jnp.float32)
    block = model_width // contexts
    pieces = [None] * contexts
    for at, i in enumerate(order):
        pieces[i] = attended[:, at * block : (at + 1) * block]
    attended = jnp.concatenate(natural(pieces, context_index), axis=1)
    resid = compact.astype(jnp.float32) + attended
    moe_in = rms_scale(resid, moe_gain).astype(jnp.bfloat16)

    mine = jnp.concatenate([moe_in] + [partner(moe_in, "context", i) for i in evens[1:]], axis=0)
    theirs = partner(mine, "context", 1)
    piece = context_index * spans + span_index
    here = expert_range[None, :] == piece // 2
    scale = jnp.sum(jnp.where(here, all_gates, 0.0), axis=1, keepdims=True)
    rows = jnp.concatenate([mine, theirs], axis=0)
    gate = jnp.dot(rows, expert_in[0, 0], preferred_element_type=jnp.float32)
    upper = jnp.dot(rows, expert_in[0, 1], preferred_element_type=jnp.float32)
    hidden = (jax.nn.silu(gate) * upper).astype(jnp.bfloat16)
    done = jnp.dot(hidden, expert_out[0], preferred_element_type=jnp.float32)
    done = jnp.where(scale > 0, done * scale, 0.0)

    half = mine.shape[0]
    back = partner(done[half:].astype(jnp.bfloat16), "context", 1)
    level = (done[:half] + back.astype(jnp.float32)).reshape(len(evens), keep_count, model_width)
    total = level[0]
    for at, i in enumerate(evens[1:], 1):
        total = total + partner(level[at].astype(jnp.bfloat16), "context", i).astype(jnp.float32)
    total = total.reshape(spans, rows_dev, model_width)
    routed = lax.dynamic_index_in_dim(total, span_index, 0, keepdims=False)
    for k in range(1, spans):
        away = lax.dynamic_index_in_dim(total, span_index ^ k, 0, keepdims=False)
        routed = routed + partner(away.astype(jnp.bfloat16), "span", k).astype(jnp.float32)
    own = lax.dynamic_slice_in_dim(resid, span_index * rows_dev, rows_dev, 0)
    row_live = lax.dynamic_slice_in_dim(live, span_index * rows_dev, rows_dev, 0)
    layer_out = jnp.where(row_live[:, None], own + routed, 0.0).astype(jnp.bfloat16)
    return (layer_out, cached)


def solution(mesh):
    placed = (
        P(("groups", "context"), "span"),
        P(("groups", "context"), None),
        P(),
        P(None, "span"),
        P(None, "span"),
        P(),
        P("span", "context"),
        P(),
        P(("groups", "context", "span"), None),
        P(("groups", "context", "span"), None),
        P(),
        P(("context", "span"), None, None, None),
        P(("context", "span"), None, None),
    )
    return jax.shard_map(
        per_device,
        mesh=mesh,
        in_specs=placed,
        out_specs=(P(("groups", "context", "span"), None), P(("groups", "context"), None)),
        check_vma=False,
    )
```

```python
import functools

import jax
import jax.numpy as jnp
from jax import lax
from jax.experimental import pallas as pl
from jax.experimental.pallas import tpu as pltpu
from jax.sharding import PartitionSpec as P

EPS = 1e-06
THETA = 50000.0
SCALE = 192.0 ** (-0.5)
NEGATIVE = -1e30
LANES = 128
F32 = jnp.float32
BF16 = jnp.bfloat16
MIB = 1 << 20


VM = pl.BlockSpec(memory_space=pltpu.VMEM)
SM = pl.BlockSpec(memory_space=pltpu.SMEM)
HBM = pl.BlockSpec(memory_space=pl.ANY)


def up(count, unit=LANES):
    return -(-count // unit) * unit


def shape(dims, dtype):
    return jax.ShapeDtypeStruct(tuple(dims), dtype)


def call(kernel, name, outs, in_specs, args, scratch=(), flops=0, moved=0, limit=16):
    single = not isinstance(outs, (list, tuple))
    return pl.pallas_call(
        kernel,
        out_shape=outs,
        in_specs=in_specs,
        out_specs=VM if single else [VM] * len(outs),
        scratch_shapes=list(scratch),
        name=name,
        compiler_params=pltpu.CompilerParams(vmem_limit_bytes=limit * MIB),
        cost_estimate=pl.CostEstimate(flops=flops, bytes_accessed=moved, transcendentals=0),
    )(*args)


def nt(left, right):
    return lax.dot_general(left, right, (((1,), (1,)), ((), ())), preferred_element_type=F32)


def nn(left, right):
    return jnp.dot(left, right, preferred_element_type=F32)


def partner(values, axis, mask):
    count = lax.axis_size(axis)
    return lax.ppermute(values, axis, [(i, i ^ mask) for i in range(count)])


def natural(parts, index):
    bit = 1
    while bit < len(parts):
        swap = (index & bit) != 0
        parts = [jnp.where(swap, parts[k ^ bit], parts[k]) for k in range(len(parts))]
        bit *= 2
    return parts


def pick_kernel(keep_ref, raw_ref, out_ref):
    rows = lax.broadcasted_iota(jnp.int32, (raw_ref.shape[0], keep_ref.shape[1]), 0)
    hits = jnp.where(rows == keep_ref[...], 1.0, 0.0).astype(BF16)
    out_ref[...] = lax.dot_general(
        hits, raw_ref[...], (((0,), (0,)), ((), ())), preferred_element_type=F32
    ).astype(BF16)


def latent_kernel(spans, *refs):
    at_ref, slot_ref = refs[:2]
    parts = refs[2 : 2 + spans]
    gain_ref, weight_ref, ids_ref, gates_ref, compact_ref, normed_ref, sent_ref = refs[2 + spans :]
    rows, block = parts[0].shape
    experts = slot_ref.shape[0]
    values = [p[...].astype(F32) for p in parts]
    square = sum(jnp.sum(v * v, axis=1, keepdims=True) for v in values)
    factor = lax.rsqrt(square / (spans * block) + EPS)
    for k in range(spans):
        at = pl.ds(pl.multiple_of((at_ref[1] ^ k) * block, block), block)
        compact_ref[:, at] = parts[k][...]
        normed_ref[:, at] = (values[k] * factor * gain_ref[:, at]).astype(BF16)
    ids = ids_ref[...]
    slots = jnp.zeros_like(ids)
    for e in range(experts):
        slots = jnp.where(ids == e, slot_ref[e], slots)
    width = sent_ref.shape[1]
    lane = lax.broadcasted_iota(jnp.int32, (ids.shape[0], width), 1)
    gates = jnp.zeros((ids.shape[0], width), F32)
    for t in range(ids.shape[1]):
        gates = gates + jnp.where(lane == slots[:, t : t + 1], gates_ref[:, t : t + 1], 0.0)
    sent_ref[0:rows, :] = jnp.zeros((rows, width), F32)
    sent_ref[0:rows, 0 : weight_ref.shape[0]] = nt(normed_ref[...], weight_ref[...])
    sent_ref[rows:, :] = gates


def rotated(values, cosine, sine):
    half = values.shape[1] // 2
    swapped = jnp.concatenate([values[:, half:], values[:, :half]], axis=1)
    return values * cosine + swapped * sine


def query_kernel(heads, kv_rank, normed_ref, weight_ref, cos_ref, sin_ref, out_ref, buf, sem):
    rows = normed_ref.shape[0]
    latent = weight_ref.shape[1] // heads
    steps = buf.shape[0]
    deep = buf.shape[1]
    copies = [
        pltpu.make_async_copy(weight_ref.at[pl.ds(n * deep, deep), :], buf.at[n], sem.at[n])
        for n in range(steps)
    ]
    for copy in copies:
        copy.start()
    total = jnp.zeros((rows, weight_ref.shape[1]), F32)
    for n in range(steps):
        copies[n].wait()
        total = total + nn(normed_ref[:, n * deep : (n + 1) * deep], buf[n])
    out_ref[...] = jnp.zeros(out_ref.shape, BF16)
    for h in range(heads):
        one = total[:, h * latent : (h + 1) * latent]
        out_ref[h * rows : (h + 1) * rows, 0:kv_rank] = one[:, :kv_rank].astype(BF16)
        out_ref[h * rows : (h + 1) * rows, kv_rank:latent] = rotated(
            one[:, kv_rank:], cos_ref[...], sin_ref[...]
        ).astype(BF16)


def cache_kernel(spans, width, experts, *refs):
    at_ref = refs[0]
    parts = refs[1 : 1 + spans]
    live_ref, gain_ref, cos_ref, sin_ref, cached_ref, sent_ref = refs[1 + spans :]
    rows = live_ref.shape[0]
    kv_rank = gain_ref.shape[1]
    values = natural([p[...] for p in parts], at_ref[1])
    latent = jnp.concatenate([v[:rows, :width] for v in values], axis=1)
    gates = jnp.concatenate([v[rows:, :experts] for v in values], axis=0)
    nope = latent[:, :kv_rank]
    factor = lax.rsqrt(jnp.mean(nope * nope, axis=1, keepdims=True) + EPS)
    nope = nope * factor * gain_ref[...]
    rope = rotated(latent[:, kv_rank:], cos_ref[...], sin_ref[...])
    cached_ref[:, :kv_rank] = nope.astype(BF16)
    cached_ref[:, kv_rank:] = rope.astype(BF16)
    high = gates.astype(BF16).astype(F32)
    used = rope.shape[1] + 2 * experts + 1
    tail = [rope, high, gates - high, live_ref[...]]
    rest = sent_ref.shape[1] - kv_rank - used
    if rest:
        tail.append(jnp.zeros((rows, rest), F32))
    sent_ref[:, :kv_rank] = nope.astype(BF16)
    sent_ref[:, kv_rank:] = jnp.concatenate(tail, axis=1).astype(BF16)


def attend_kernel(heads, kv_rank, flag_lane, blocks, at_ref, query_ref, mine_ref, theirs_ref, *refs):
    weights = refs[:blocks]
    out_ref, buf, sem = refs[blocks:]
    copies = [pltpu.make_async_copy(weights[n], buf.at[n], sem.at[n]) for n in range(blocks)]
    for copy in copies:
        copy.start()
    count = query_ref.shape[0] // heads
    here = at_ref[0]
    keys = jnp.concatenate([mine_ref[...], theirs_ref[...]], axis=0)
    total = keys.shape[0]
    width = keys.shape[1]
    lane = lax.broadcasted_iota(jnp.int32, (8, width), 1)
    flags = nt(jnp.where(lane == flag_lane, 1.0, 0.0).astype(BF16), keys)[0:1, :]
    row = lax.broadcasted_iota(jnp.int32, (count, total), 0)
    col = lax.broadcasted_iota(jnp.int32, (count, total), 1)
    half = blocks // 2
    at = col // count
    which = jnp.where(at < half, 2 * at, 2 * (at - half) + 1)
    key_ids = (which ^ here) * count + col % count
    allowed = (key_ids <= here * count + row) & (flags > 0)
    mixed = []
    for h in range(heads):
        scores = nt(query_ref[h * count : (h + 1) * count, :], keys) * SCALE
        scores = jnp.where(allowed, scores, NEGATIVE)
        highest = jnp.max(scores, axis=1, keepdims=True)
        weight = jnp.where(allowed, jnp.exp(scores - highest), 0.0)
        denominator = jnp.sum(weight, axis=1, keepdims=True)
        summed = nn(weight.astype(BF16), keys[:, :kv_rank])
        mixed.append((summed / denominator).astype(BF16))
    mixed = jnp.concatenate(mixed, axis=1)
    block = buf.shape[2]
    for n in range(blocks):
        i = 2 * n if n < half else 2 * (n - half) + 1
        copies[n].wait()
        place = pl.ds(pl.multiple_of((here ^ i) * block, block), block)
        out_ref[:, place] = nn(mixed, buf[n]).astype(BF16)


def resid_kernel(spans, *refs):
    parts = refs[:spans]
    compact_ref, gain_ref, resid_ref, out_ref = refs[spans:]
    resid = compact_ref[...].astype(F32) + sum(p[...].astype(F32) for p in parts)
    factor = lax.rsqrt(jnp.mean(resid * resid, axis=1, keepdims=True) + EPS)
    resid_ref[...] = resid
    out_ref[...] = (resid * factor * gain_ref[...]).astype(BF16)


def expert_kernel(
    first_lane,
    tail_at,
    experts,
    cuts,
    columns,
    at_ref,
    mine_ref,
    theirs_ref,
    mine_tail_ref,
    theirs_tail_ref,
    in_ref,
    out_weight_ref,
    near_ref,
    far_ref,
    in_buf,
    out_buf,
    act_ref,
    sem,
):
    copies = []
    for n, (start, size) in enumerate(cuts):
        copies.append(
            [
                pltpu.make_async_copy(
                    in_ref.at[j, pl.ds(start, size), :],
                    in_buf.at[j, pl.ds(start, size), :],
                    sem.at[2 * n + j],
                )
                for j in range(2)
            ]
        )
    last = pltpu.make_async_copy(out_weight_ref, out_buf, sem.at[2 * len(cuts)])
    for pair in copies:
        for copy in pair:
            copy.start()
    last.start()
    rows = jnp.concatenate([mine_ref[...], theirs_ref[...]], axis=0)
    tail = jnp.concatenate([mine_tail_ref[:, tail_at:], theirs_tail_ref[:, tail_at:]], axis=0)
    tail = tail.astype(F32)
    lane = lax.broadcasted_iota(jnp.int32, tail.shape, 1) - first_lane
    slot = at_ref[2]
    scale = jnp.sum(
        jnp.where((lane == slot) | (lane == slot + experts), tail, 0.0), axis=1, keepdims=True
    )
    for n, (start, size) in enumerate(cuts):
        for copy in copies[n]:
            copy.wait()
        gate = nt(rows, in_buf[0, start : start + size, :])
        upper = nt(rows, in_buf[1, start : start + size, :])
        act_ref[:, start : start + size] = (gate / (1.0 + jnp.exp(-gate)) * upper).astype(BF16)
    last.wait()
    half = mine_ref.shape[0]
    width = out_buf.shape[1] // columns
    for n in range(columns):
        span = slice(n * width, (n + 1) * width)
        done = nn(act_ref[...], out_buf[:, span])
        done = jnp.where(scale > 0, done * scale, 0.0).astype(BF16)
        near_ref[:, span] = done[:half]
        far_ref[:, span] = done[half:]


def level_kernel(near_ref, back_ref, *outs):
    rows = outs[0].shape[0]
    for n, out in enumerate(outs):
        at = slice(n * rows, (n + 1) * rows)
        out[...] = (near_ref[at, :].astype(F32) + back_ref[at, :].astype(F32)).astype(out.dtype)


def rows_kernel(spans, *refs):
    at_ref = refs[0]
    parts, outs, buf = refs[1 : -spans - 1], refs[-spans - 1 : -1], refs[-1]
    total = parts[0][...]
    for p in parts[1:]:
        total = total + p[...].astype(F32)
    buf[...] = total
    count = outs[0].shape[0]
    for k, out in enumerate(outs):
        at = pl.ds(pl.multiple_of((at_ref[1] ^ k) * count, count), count)
        out[...] = buf[at, :].astype(out.dtype)


def last_kernel(spans, *refs):
    at_ref = refs[0]
    parts = refs[1 : 1 + spans]
    resid_ref, live_ref, out_ref = refs[1 + spans :]
    count = out_ref.shape[0]
    routed = sum(p[...].astype(F32) for p in parts)
    at = pl.ds(pl.multiple_of(at_ref[1] * count, count), count)
    total = resid_ref[at, :] + routed
    out_ref[...] = jnp.where(live_ref[at, :] > 0, total, 0.0).astype(BF16)


def per_device(
    raw_tokens,
    keep,
    attn_gain,
    query_weight,
    latent_weight,
    kv_gain,
    out_weight,
    moe_gain,
    expert_ids,
    gate_values,
    expert_slot,
    expert_in,
    expert_out,
):
    kv_rank = kv_gain.shape[0]
    spans = lax.axis_size("span")
    contexts = lax.axis_size("context")
    part_width = latent_weight.shape[1]
    latent_width = part_width * spans
    rope = latent_width - kv_rank
    model = attn_gain.shape[0]
    kept = keep.shape[1]
    raw_rows = raw_tokens.shape[0]
    heads = query_weight.shape[1] // latent_width
    rows_dev = expert_ids.shape[0]
    experts = expert_slot.shape[0]
    hidden = expert_in.shape[3]
    context_index = lax.axis_index("context")
    span_index = lax.axis_index("span")
    evens = list(range(0, contexts, 2))
    piece = context_index * spans + span_index
    at = jnp.stack([context_index, span_index, piece // 2]).astype(jnp.int32)

    picked = call(
        pick_kernel, "pick", shape((kept, raw_tokens.shape[1]), BF16), [VM, VM], (keep, raw_tokens)
    )
    parts = [picked] + [partner(picked, "span", k) for k in range(1, spans)]
    weights_even = [out_weight] + [partner(out_weight, "context", i) for i in evens[1:]]
    weights_odd = [partner(w, "context", 1) for w in weights_even]
    live = (keep[0] >= 0).astype(F32)[:, None]
    positions = (context_index * raw_rows + jnp.maximum(keep[0], 0)).astype(F32)[:, None]
    freqs = THETA ** (-2.0 * jnp.arange(rope // 2, dtype=F32) / rope)
    angles = positions * freqs[None, :]
    cosine, sine = jnp.cos(angles), jnp.sin(angles)
    cosine = jnp.concatenate([cosine, cosine], axis=1)
    sine = jnp.concatenate([-sine, sine], axis=1)

    sent_width = up(max(part_width, experts))
    compact, normed, sent = call(
        functools.partial(latent_kernel, spans),
        "latent",
        [
            shape((kept, model), BF16),
            shape((kept, model), BF16),
            shape((kept + rows_dev, sent_width), F32),
        ],
        [SM, SM] + [VM] * (spans + 4),
        (at, expert_slot, *parts, attn_gain[None], latent_weight.T, expert_ids, gate_values),
        flops=2 * kept * latent_weight.size,
        moved=2 * latent_weight.size,
    )
    parts = [sent] + [partner(sent, "span", k) for k in range(1, spans)]
    steps = 8
    query = call(
        functools.partial(query_kernel, heads, kv_rank),
        "query",
        shape((heads * kept, up(latent_width + 2 * experts + 1)), BF16),
        [VM, HBM, VM, VM],
        (normed, query_weight, cosine, sine),
        scratch=[
            pltpu.VMEM((steps, model // steps, query_weight.shape[1]), BF16),
            pltpu.SemaphoreType.DMA((steps,)),
        ],
        flops=2 * kept * query_weight.size,
        moved=2 * query_weight.size,
    )
    cached, sent = call(
        functools.partial(cache_kernel, spans, part_width, experts),
        "cache",
        [shape((kept, latent_width), BF16), shape((kept, up(latent_width + 2 * experts + 1)), BF16)],
        [SM] + [VM] * (spans + 4),
        (at, *parts, live, kv_gain[None], cosine, sine),
    )

    mine_keys = jnp.concatenate([sent] + [partner(sent, "context", i) for i in evens[1:]], axis=0)
    their_keys = partner(mine_keys, "context", 1)
    partial = call(
        functools.partial(
            attend_kernel, heads, kv_rank, latent_width + 2 * experts, contexts
        ),
        "attend",
        shape((kept, model), BF16),
        [SM, VM, VM, VM] + [HBM] * contexts,
        (at, query, mine_keys, their_keys, *weights_even, *weights_odd),
        scratch=[
            pltpu.VMEM((contexts, *out_weight.shape), BF16),
            pltpu.SemaphoreType.DMA((contexts,)),
        ],
        flops=2 * kept * contexts * out_weight.size,
        moved=2 * contexts * out_weight.size,
    )

    resid, moe_in = call(
        functools.partial(resid_kernel, spans),
        "resid",
        [shape((kept, model), F32), shape((kept, model), BF16)],
        [VM] * (spans + 2),
        (partial, *[partner(partial, "span", k) for k in range(1, spans)], compact, moe_gain[None]),
    )

    mine = jnp.concatenate([moe_in] + [partner(moe_in, "context", i) for i in evens[1:]], axis=0)
    theirs = partner(mine, "context", 1)
    half = mine.shape[0]
    cuts, start = [], 0
    while start < hidden:
        size = min(2 * LANES, hidden - start)
        cuts.append((start, size))
        start += size
    near, far = call(
        functools.partial(expert_kernel, latent_width - kv_rank, kv_rank, experts, cuts, 4),
        "expert",
        [shape((half, model), BF16), shape((half, model), BF16)],
        [SM, VM, VM, VM, VM, HBM, HBM],
        (at, mine, theirs, mine_keys, their_keys, jnp.swapaxes(expert_in[0], 1, 2), expert_out[0]),
        scratch=[
            pltpu.VMEM((2, hidden, model), BF16),
            pltpu.VMEM((hidden, model), BF16),
            pltpu.VMEM((2 * half, hidden), BF16),
            pltpu.SemaphoreType.DMA((2 * len(cuts) + 1,)),
        ],
        flops=6 * 2 * half * hidden * model,
        moved=6 * hidden * model,
        limit=40,
    )

    levels = call(
        level_kernel,
        "level",
        [shape((kept, model), F32)] + [shape((kept, model), BF16)] * (len(evens) - 1),
        [VM, VM],
        (near, partner(far, "context", 1)),
    )
    got = [partner(level, "context", i) for level, i in zip(levels[1:], evens[1:])]
    rows = call(
        functools.partial(rows_kernel, spans),
        "rows",
        [shape((rows_dev, model), F32)] + [shape((rows_dev, model), BF16)] * (spans - 1),
        [SM] + [VM] * len(levels),
        (at, levels[0], *got),
        scratch=[pltpu.VMEM((kept, model), F32)],
    )
    got = [partner(rows[k], "span", k) for k in range(1, spans)]
    layer_out = call(
        functools.partial(last_kernel, spans),
        "last",
        shape((rows_dev, model), BF16),
        [SM] + [VM] * (spans + 2),
        (at, rows[0], *got, resid, live),
    )
    return (layer_out, cached)


def solution(mesh):
    placed = (
        P(("groups", "context"), "span"),
        P(("groups", "context"), None),
        P(),
        P(None, "span"),
        P(None, "span"),
        P(),
        P("span", "context"),
        P(),
        P(("groups", "context", "span"), None),
        P(("groups", "context", "span"), None),
        P(),
        P(("context", "span"), None, None, None),
        P(("context", "span"), None, None),
    )
    return jax.shard_map(
        per_device,
        mesh=mesh,
        in_specs=placed,
        out_specs=(P(("groups", "context", "span"), None), P(("groups", "context"), None)),
        check_vma=False,
    )
```

```python
import functools
import math

import jax
import jax.numpy as jnp
from jax import lax
from jax.experimental import pallas as pl
from jax.experimental.pallas import tpu as pltpu
from jax.sharding import PartitionSpec as P

EPS = 1e-06
THETA = 50000.0
SCALE = 192.0 ** (-0.5)
NEGATIVE = -1e30
LANES = 128
F32 = jnp.float32
BF16 = jnp.bfloat16
MIB = 1 << 20


VM = pl.BlockSpec(memory_space=pltpu.VMEM)
SM = pl.BlockSpec(memory_space=pltpu.SMEM)
ANY = pl.BlockSpec(memory_space=pl.ANY)
HBM = pl.BlockSpec(memory_space=pltpu.HBM)


def up(count, unit=LANES):
    return -(-count // unit) * unit


def shape(dims, dtype):
    return jax.ShapeDtypeStruct(tuple(dims), dtype)


def call(kernel, name, outs, in_specs, args, scratch=(), flops=0, moved=0, limit=16):
    single = not isinstance(outs, (list, tuple))
    return pl.pallas_call(
        kernel,
        out_shape=outs,
        in_specs=in_specs,
        out_specs=VM if single else [VM] * len(outs),
        scratch_shapes=list(scratch),
        name=name,
        compiler_params=pltpu.CompilerParams(vmem_limit_bytes=limit * MIB),
        cost_estimate=pl.CostEstimate(flops=flops, bytes_accessed=moved, transcendentals=0),
    )(*args)


def nt(left, right):
    return lax.dot_general(left, right, (((1,), (1,)), ((), ())), preferred_element_type=F32)


def nn(left, right):
    return jnp.dot(left, right, preferred_element_type=F32)


def partner(values, axis, mask):
    count = lax.axis_size(axis)
    return lax.ppermute(values, axis, [(i, i ^ mask) for i in range(count)])


def natural(parts, index):
    bit = 1
    while bit < len(parts):
        swap = (index & bit) != 0
        parts = [jnp.where(swap, parts[k ^ bit], parts[k]) for k in range(len(parts))]
        bit *= 2
    return parts


def pick_kernel(
    keep_hbm,
    raw_hbm,
    weight_hbm,
    gain_hbm,
    ids_hbm,
    gates_hbm,
    slot_hbm,
    out_ref,
    weight_ref,
    gain_ref,
    dense_ref,
    keep_ref,
    raw_ref,
    ids_ref,
    gates_ref,
    slot_ref,
    sem,
):
    pairs = [
        (keep_hbm, keep_ref),
        (raw_hbm, raw_ref),
        (ids_hbm, ids_ref),
        (gates_hbm, gates_ref),
        (slot_hbm, slot_ref),
        (gain_hbm, gain_ref),
        (weight_hbm, weight_ref),
    ]
    copies = [pltpu.make_async_copy(a, b, sem.at[n]) for n, (a, b) in enumerate(pairs)]
    for copy in copies:
        copy.start()
    copies[0].wait()
    copies[1].wait()
    rows = lax.broadcasted_iota(jnp.int32, (raw_ref.shape[0], keep_ref.shape[1]), 0)
    hits = jnp.where(rows == keep_ref[...], 1.0, 0.0).astype(BF16)
    out_ref[...] = lax.dot_general(
        hits, raw_ref[...], (((0,), (0,)), ((), ())), preferred_element_type=F32
    ).astype(BF16)
    for copy in copies[2:]:
        copy.wait()
    ids = ids_ref[...]
    slots = jnp.zeros_like(ids)
    for e in range(slot_ref.shape[0]):
        slots = jnp.where(ids == e, slot_ref[e], slots)
    lane = lax.broadcasted_iota(jnp.int32, dense_ref.shape, 1)
    gates = jnp.zeros(dense_ref.shape, F32)
    for t in range(ids.shape[1]):
        gates = gates + jnp.where(lane == slots[:, t : t + 1], gates_ref[:, t : t + 1], 0.0)
    dense_ref[...] = gates


def latent_kernel(spans, *refs):
    at_ref = refs[0]
    parts = refs[1 : 1 + spans]
    gain_ref, weight_ref, dense_ref, compact_ref, normed_ref, sent_ref = refs[1 + spans :]
    rows, block = parts[0].shape
    values = [p[...].astype(F32) for p in parts]
    square = sum(jnp.sum(v * v, axis=1, keepdims=True) for v in values)
    factor = lax.rsqrt(square / (spans * block) + EPS)
    for k in range(spans):
        at = pl.ds(pl.multiple_of((at_ref[1] ^ k) * block, block), block)
        compact_ref[:, at] = parts[k][...]
        normed_ref[:, at] = (values[k] * factor * gain_ref[:, at]).astype(BF16)
    sent_ref[0:rows, :] = jnp.zeros((rows, sent_ref.shape[1]), F32)
    sent_ref[0:rows, 0 : weight_ref.shape[0]] = nt(normed_ref[...], weight_ref[...])
    sent_ref[rows:, :] = dense_ref[...]


def rotated(values, cosine, sine):
    half = values.shape[1] // 2
    swapped = jnp.concatenate([values[:, half:], values[:, :half]], axis=1)
    return values * cosine + swapped * sine


def query_kernel(
    heads,
    raw_rows,
    at_ref,
    normed_ref,
    weight_ref,
    keep_hbm,
    kv_hbm,
    moe_hbm,
    out_ref,
    cos_ref,
    sin_ref,
    live_ref,
    kv_ref,
    moe_ref,
    buf,
    keep_ref,
    sem,
):
    rows = normed_ref.shape[0]
    latent = weight_ref.shape[1] // heads
    steps = buf.shape[0]
    deep = buf.shape[1]
    small = [(keep_hbm, keep_ref), (kv_hbm, kv_ref), (moe_hbm, moe_ref)]
    small = [pltpu.make_async_copy(a, b, sem.at[steps + n]) for n, (a, b) in enumerate(small)]
    copies = [
        pltpu.make_async_copy(weight_ref.at[pl.ds(n * deep, deep), :], buf.at[n], sem.at[n])
        for n in range(steps)
    ]
    for copy in small + copies:
        copy.start()
    small[0].wait()
    diagonal = lax.broadcasted_iota(jnp.int32, (rows, rows), 0) == lax.broadcasted_iota(
        jnp.int32, (rows, rows), 1
    )
    listing = jnp.sum(
        jnp.where(diagonal, keep_ref[...].astype(F32), 0.0), axis=1, keepdims=True
    )
    live_ref[...] = jnp.where(listing >= 0, 1.0, 0.0)
    positions = (at_ref[0] * raw_rows).astype(F32) + jnp.maximum(listing, 0.0)
    rope = cos_ref.shape[1]
    half = rope // 2
    lane = lax.broadcasted_iota(jnp.int32, (rows, rope), 1)
    first = lane < half
    place = jnp.where(first, lane, lane - half).astype(F32)
    angles = positions * jnp.exp(place * (-2.0 / rope * math.log(THETA)))
    cos_ref[...] = jnp.cos(angles)
    sine = jnp.sin(angles)
    sin_ref[...] = jnp.where(first, -sine, sine)
    total = jnp.zeros((rows, weight_ref.shape[1]), F32)
    for n in range(steps):
        copies[n].wait()
        total = total + nn(normed_ref[:, n * deep : (n + 1) * deep], buf[n])
    kv_rank = latent - rope
    out_ref[...] = jnp.zeros(out_ref.shape, BF16)
    for h in range(heads):
        one = total[:, h * latent : (h + 1) * latent]
        out_ref[h * rows : (h + 1) * rows, 0:kv_rank] = one[:, :kv_rank].astype(BF16)
        out_ref[h * rows : (h + 1) * rows, kv_rank:latent] = rotated(
            one[:, kv_rank:], cos_ref[...], sin_ref[...]
        ).astype(BF16)
    for copy in small[1:]:
        copy.wait()


def cache_kernel(spans, width, experts, *refs):
    at_ref = refs[0]
    parts = refs[1 : 1 + spans]
    live_ref, gain_ref, cos_ref, sin_ref, cached_ref, sent_ref = refs[1 + spans :]
    rows = live_ref.shape[0]
    kv_rank = gain_ref.shape[1]
    values = natural([p[...] for p in parts], at_ref[1])
    latent = jnp.concatenate([v[:rows, :width] for v in values], axis=1)
    gates = jnp.concatenate([v[rows:, :experts] for v in values], axis=0)
    nope = latent[:, :kv_rank]
    factor = lax.rsqrt(jnp.mean(nope * nope, axis=1, keepdims=True) + EPS)
    nope = nope * factor * gain_ref[...]
    rope = rotated(latent[:, kv_rank:], cos_ref[...], sin_ref[...])
    cached_ref[:, :kv_rank] = nope.astype(BF16)
    cached_ref[:, kv_rank:] = rope.astype(BF16)
    high = gates.astype(BF16).astype(F32)
    used = rope.shape[1] + 2 * experts + 1
    tail = [rope, high, gates - high, live_ref[...]]
    rest = sent_ref.shape[1] - kv_rank - used
    if rest:
        tail.append(jnp.zeros((rows, rest), F32))
    sent_ref[:, :kv_rank] = nope.astype(BF16)
    sent_ref[:, kv_rank:] = jnp.concatenate(tail, axis=1).astype(BF16)


def attend_kernel(heads, kv_rank, flag_lane, blocks, at_ref, query_ref, mine_ref, theirs_ref, *refs):
    weights = refs[:blocks]
    out_ref, buf, sem = refs[blocks:]
    copies = [pltpu.make_async_copy(weights[n], buf.at[n], sem.at[n]) for n in range(blocks)]
    for copy in copies:
        copy.start()
    count = query_ref.shape[0] // heads
    here = at_ref[0]
    keys = jnp.concatenate([mine_ref[...], theirs_ref[...]], axis=0)
    total = keys.shape[0]
    width = keys.shape[1]
    lane = lax.broadcasted_iota(jnp.int32, (8, width), 1)
    flags = nt(jnp.where(lane == flag_lane, 1.0, 0.0).astype(BF16), keys)[0:1, :]
    row = lax.broadcasted_iota(jnp.int32, (count, total), 0)
    col = lax.broadcasted_iota(jnp.int32, (count, total), 1)
    half = blocks // 2
    at = col // count
    which = jnp.where(at < half, 2 * at, 2 * (at - half) + 1)
    key_ids = (which ^ here) * count + col % count
    allowed = (key_ids <= here * count + row) & (flags > 0)
    mixed = []
    for h in range(heads):
        scores = nt(query_ref[h * count : (h + 1) * count, :], keys) * SCALE
        scores = jnp.where(allowed, scores, NEGATIVE)
        highest = jnp.max(scores, axis=1, keepdims=True)
        weight = jnp.where(allowed, jnp.exp(scores - highest), 0.0)
        denominator = jnp.sum(weight, axis=1, keepdims=True)
        summed = nn(weight.astype(BF16), keys[:, :kv_rank])
        mixed.append((summed / denominator).astype(BF16))
    mixed = jnp.concatenate(mixed, axis=1)
    block = buf.shape[2]
    for n in range(blocks):
        i = 2 * n if n < half else 2 * (n - half) + 1
        copies[n].wait()
        place = pl.ds(pl.multiple_of((here ^ i) * block, block), block)
        out_ref[:, place] = nn(mixed, buf[n]).astype(BF16)


def resid_kernel(spans, *refs):
    at_ref = refs[0]
    parts = refs[1 : 1 + spans]
    compact_ref, gain_ref, own_ref, out_ref, buf = refs[1 + spans :]
    resid = compact_ref[...].astype(F32) + sum(p[...].astype(F32) for p in parts)
    factor = lax.rsqrt(jnp.mean(resid * resid, axis=1, keepdims=True) + EPS)
    out_ref[...] = (resid * factor * gain_ref[...]).astype(BF16)
    buf[...] = resid
    count = own_ref.shape[0]
    own_ref[...] = buf[pl.ds(pl.multiple_of(at_ref[1] * count, count), count), :]


def expert_kernel(
    first_lane,
    tail_at,
    experts,
    cuts,
    columns,
    at_ref,
    mine_ref,
    theirs_ref,
    mine_tail_ref,
    theirs_tail_ref,
    in_ref,
    out_weight_ref,
    near_ref,
    far_ref,
    act_ref,
):
    rows = jnp.concatenate([mine_ref[...], theirs_ref[...]], axis=0)
    tail = jnp.concatenate([mine_tail_ref[:, tail_at:], theirs_tail_ref[:, tail_at:]], axis=0)
    tail = tail.astype(F32)
    lane = lax.broadcasted_iota(jnp.int32, tail.shape, 1) - first_lane
    slot = at_ref[2]
    scale = jnp.sum(
        jnp.where((lane == slot) | (lane == slot + experts), tail, 0.0), axis=1, keepdims=True
    )
    for start, size in cuts:
        gate = nt(rows, in_ref[0, start : start + size, :])
        upper = nt(rows, in_ref[1, start : start + size, :])
        act_ref[:, start : start + size] = (gate / (1.0 + jnp.exp(-gate)) * upper).astype(BF16)
    half = mine_ref.shape[0]
    width = out_weight_ref.shape[1] // columns
    for n in range(columns):
        span = slice(n * width, (n + 1) * width)
        done = nn(act_ref[...], out_weight_ref[:, span])
        done = jnp.where(scale > 0, done * scale, 0.0).astype(BF16)
        near_ref[:, span] = done[:half]
        far_ref[:, span] = done[half:]


def level_kernel(near_ref, back_ref, *outs):
    rows = outs[0].shape[0]
    for n, out in enumerate(outs):
        at = slice(n * rows, (n + 1) * rows)
        out[...] = (near_ref[at, :].astype(F32) + back_ref[at, :].astype(F32)).astype(out.dtype)


def rows_kernel(spans, *refs):
    at_ref = refs[0]
    parts, outs, buf = refs[1 : -spans - 1], refs[-spans - 1 : -1], refs[-1]
    total = parts[0][...]
    for p in parts[1:]:
        total = total + p[...].astype(F32)
    buf[...] = total
    count = outs[0].shape[0]
    for k, out in enumerate(outs):
        at = pl.ds(pl.multiple_of((at_ref[1] ^ k) * count, count), count)
        out[...] = buf[at, :].astype(out.dtype)


def last_kernel(spans, *refs):
    at_ref = refs[0]
    parts = refs[1 : 1 + spans]
    own_ref, live_ref, out_ref = refs[1 + spans :]
    count = out_ref.shape[0]
    routed = sum(p[...].astype(F32) for p in parts)
    at = pl.ds(pl.multiple_of(at_ref[1] * count, count), count)
    total = own_ref[...] + routed
    out_ref[...] = jnp.where(live_ref[at, :] > 0, total, 0.0).astype(BF16)


def per_device(
    raw_tokens,
    keep,
    attn_gain,
    query_weight,
    latent_weight,
    kv_gain,
    out_weight,
    moe_gain,
    expert_ids,
    gate_values,
    expert_slot,
    expert_in,
    expert_out,
):
    kv_rank = kv_gain.shape[0]
    spans = lax.axis_size("span")
    contexts = lax.axis_size("context")
    part_width = latent_weight.shape[1]
    latent_width = part_width * spans
    rope = latent_width - kv_rank
    model = attn_gain.shape[0]
    kept = keep.shape[1]
    raw_rows = raw_tokens.shape[0]
    heads = query_weight.shape[1] // latent_width
    rows_dev = expert_ids.shape[0]
    experts = expert_slot.shape[0]
    hidden = expert_in.shape[3]
    context_index = lax.axis_index("context")
    span_index = lax.axis_index("span")
    evens = list(range(0, contexts, 2))
    piece = context_index * spans + span_index
    at = jnp.stack([context_index, span_index, piece // 2]).astype(jnp.int32)

    sent_width = up(max(part_width, experts))
    picked, near_weight, gain, dense = call(
        pick_kernel,
        "pick",
        [
            shape((kept, raw_tokens.shape[1]), BF16),
            shape((part_width, model), BF16),
            shape((1, model), F32),
            shape((rows_dev, sent_width), F32),
        ],
        [HBM] * 7,
        (keep, raw_tokens, latent_weight.T, attn_gain[None], expert_ids, gate_values, expert_slot),
        scratch=[
            pltpu.VMEM(keep.shape, jnp.int32),
            pltpu.VMEM(raw_tokens.shape, BF16),
            pltpu.VMEM(expert_ids.shape, jnp.int32),
            pltpu.VMEM(gate_values.shape, F32),
            pltpu.SMEM(expert_slot.shape, jnp.int32),
            pltpu.SemaphoreType.DMA((7,)),
        ],
        limit=4,
    )
    parts = [picked] + [partner(picked, "span", k) for k in range(1, spans)]
    weights_even = [out_weight] + [partner(out_weight, "context", i) for i in evens[1:]]
    weights_odd = [partner(w, "context", 1) for w in weights_even]

    compact, normed, sent = call(
        functools.partial(latent_kernel, spans),
        "latent",
        [
            shape((kept, model), BF16),
            shape((kept, model), BF16),
            shape((kept + rows_dev, sent_width), F32),
        ],
        [SM] + [VM] * (spans + 3),
        (at, *parts, gain, near_weight, dense),
        flops=2 * kept * latent_weight.size,
        moved=2 * latent_weight.size,
        limit=4,
    )
    parts = [sent] + [partner(sent, "span", k) for k in range(1, spans)]
    steps = 8
    row_width = up(latent_width + 2 * experts + 1)
    query, cosine, sine, live, near_kv, near_moe = call(
        functools.partial(query_kernel, heads, raw_rows),
        "query",
        [
            shape((heads * kept, row_width), BF16),
            shape((kept, rope), F32),
            shape((kept, rope), F32),
            shape((kept, 1), F32),
            shape((1, kv_rank), F32),
            shape((1, model), F32),
        ],
        [SM, VM] + [HBM] * 4,
        (at, normed, query_weight, keep, kv_gain[None], moe_gain[None]),
        scratch=[
            pltpu.VMEM((steps, model // steps, query_weight.shape[1]), BF16),
            pltpu.VMEM(keep.shape, jnp.int32),
            pltpu.SemaphoreType.DMA((steps + 3,)),
        ],
        flops=2 * kept * query_weight.size,
        moved=2 * query_weight.size,
        limit=10,
    )
    cached, sent = call(
        functools.partial(cache_kernel, spans, part_width, experts),
        "cache",
        [shape((kept, latent_width), BF16), shape((kept, row_width), BF16)],
        [SM] + [VM] * (spans + 4),
        (at, *parts, live, near_kv, cosine, sine),
        limit=4,
    )

    mine_keys = jnp.concatenate([sent] + [partner(sent, "context", i) for i in evens[1:]], axis=0)
    their_keys = partner(mine_keys, "context", 1)
    partial = call(
        functools.partial(
            attend_kernel, heads, kv_rank, latent_width + 2 * experts, contexts
        ),
        "attend",
        shape((kept, model), BF16),
        [SM, VM, VM, VM, HBM] + [ANY] * (contexts - 1),
        (at, query, mine_keys, their_keys, *weights_even, *weights_odd),
        scratch=[
            pltpu.VMEM((contexts, *out_weight.shape), BF16),
            pltpu.SemaphoreType.DMA((contexts,)),
        ],
        flops=2 * kept * contexts * out_weight.size,
        moved=2 * contexts * out_weight.size,
        limit=12,
    )

    got = [partner(partial, "span", k) for k in range(1, spans)]
    own, moe_in = call(
        functools.partial(resid_kernel, spans),
        "resid",
        [shape((rows_dev, model), F32), shape((kept, model), BF16)],
        [SM] + [VM] * (spans + 2),
        (at, partial, *got, compact, near_moe),
        scratch=[pltpu.VMEM((kept, model), F32)],
        limit=6,
    )

    mine = jnp.concatenate([moe_in] + [partner(moe_in, "context", i) for i in evens[1:]], axis=0)
    theirs = partner(mine, "context", 1)
    half = mine.shape[0]
    cuts, start = [], 0
    while start < hidden:
        size = min(2 * LANES, hidden - start)
        cuts.append((start, size))
        start += size
    near, far = call(
        functools.partial(expert_kernel, latent_width - kv_rank, kv_rank, experts, cuts, 4),
        "expert",
        [shape((half, model), BF16), shape((half, model), BF16)],
        [SM] + [VM] * 6,
        (at, mine, theirs, mine_keys, their_keys, jnp.swapaxes(expert_in[0], 1, 2), expert_out[0]),
        scratch=[pltpu.VMEM((2 * half, hidden), BF16)],
        flops=6 * 2 * half * hidden * model,
        moved=6 * hidden * model,
        limit=24,
    )

    levels = call(
        level_kernel,
        "level",
        [shape((kept, model), F32)] + [shape((kept, model), BF16)] * (len(evens) - 1),
        [VM, VM],
        (near, partner(far, "context", 1)),
        limit=6,
    )
    got = [partner(level, "context", i) for level, i in zip(levels[1:], evens[1:])]
    rows = call(
        functools.partial(rows_kernel, spans),
        "rows",
        [shape((rows_dev, model), F32)] + [shape((rows_dev, model), BF16)] * (spans - 1),
        [SM] + [VM] * len(levels),
        (at, levels[0], *got),
        scratch=[pltpu.VMEM((kept, model), F32)],
        limit=6,
    )
    got = [partner(rows[k], "span", k) for k in range(1, spans)]
    layer_out = call(
        functools.partial(last_kernel, spans),
        "last",
        shape((rows_dev, model), BF16),
        [SM] + [VM] * (spans + 2),
        (at, rows[0], *got, own, live),
        limit=4,
    )
    return (layer_out, cached)


def solution(mesh):
    placed = (
        P(("groups", "context"), "span"),
        P(("groups", "context"), None),
        P(),
        P(None, "span"),
        P(None, "span"),
        P(),
        P("span", "context"),
        P(),
        P(("groups", "context", "span"), None),
        P(("groups", "context", "span"), None),
        P(),
        P(("context", "span"), None, None, None),
        P(("context", "span"), None, None),
    )
    return jax.shard_map(
        per_device,
        mesh=mesh,
        in_specs=placed,
        out_specs=(P(("groups", "context", "span"), None), P(("groups", "context"), None)),
        check_vma=False,
    )
```

```python
import functools
import math

import jax
import jax.numpy as jnp
from jax import lax
from jax.experimental import pallas as pl
from jax.experimental.pallas import tpu as pltpu
from jax.sharding import PartitionSpec as P


EPS = 1e-06
THETA = 50000.0
SCALE = 192.0 ** (-0.5)
NEGATIVE = -1e30
LANES = 128
F32 = jnp.float32
BF16 = jnp.bfloat16
MIB = 1 << 20


VM = pl.BlockSpec(memory_space=pltpu.VMEM)
ANY = pl.BlockSpec(memory_space=pl.ANY)
HBM = pl.BlockSpec(memory_space=pltpu.HBM)


def up(count, unit=LANES):
    return -(-count // unit) * unit


def shape(dims, dtype):
    return jax.ShapeDtypeStruct(tuple(dims), dtype)


def call(kernel, outs, in_specs, args, scratch=(), flops=0, moved=0, limit=16):
    single = not isinstance(outs, (list, tuple))
    args = [
        pltpu.with_memory_space_constraint(value, pltpu.HBM) if spec is HBM else value
        for spec, value in zip(in_specs, args)
    ]
    return pl.pallas_call(
        kernel,
        out_shape=outs,
        in_specs=in_specs,
        out_specs=VM if single else [VM] * len(outs),
        scratch_shapes=list(scratch),
        compiler_params=pltpu.CompilerParams(vmem_limit_bytes=limit * MIB),
        cost_estimate=pl.CostEstimate(flops=flops, bytes_accessed=moved, transcendentals=0),
    )(*args)


def nt(left, right):
    return lax.dot_general(left, right, (((1,), (1,)), ((), ())), preferred_element_type=F32)


def nn(left, right):
    return jnp.dot(left, right, preferred_element_type=F32)


def here():
    return lax.axis_index("context"), lax.axis_index("span")


def partner(values, axis, mask):
    count = lax.axis_size(axis)
    return lax.ppermute(values, axis, [(i, i ^ mask) for i in range(count)])


def gathered(values, axis, masks):
    parts = [values]
    for mask in masks:
        parts.append(partner(values, axis, mask))
    return parts


def natural(parts, index):
    bit = 1
    while bit < len(parts):
        swap = (index & bit) != 0
        parts = [jnp.where(swap, parts[k ^ bit], parts[k]) for k in range(len(parts))]
        bit *= 2
    return parts


def pick_kernel(
    keep_hbm,
    raw_hbm,
    weight_hbm,
    gain_hbm,
    ids_hbm,
    gates_hbm,
    slot_hbm,
    out_ref,
    weight_ref,
    gain_ref,
    dense_ref,
    keep_ref,
    raw_ref,
    ids_ref,
    gates_ref,
    slot_ref,
    sem,
):
    pairs = [
        (keep_hbm, keep_ref),
        (raw_hbm, raw_ref),
        (ids_hbm, ids_ref),
        (gates_hbm, gates_ref),
        (slot_hbm, slot_ref),
        (gain_hbm, gain_ref),
        (weight_hbm, weight_ref),
    ]
    copies = [pltpu.make_async_copy(a, b, sem.at[n]) for n, (a, b) in enumerate(pairs)]
    for copy in copies:
        copy.start()
    copies[0].wait()
    copies[1].wait()
    rows = lax.broadcasted_iota(jnp.int32, (raw_ref.shape[0], keep_ref.shape[1]), 0)
    hits = jnp.where(rows == keep_ref[...], 1.0, 0.0).astype(BF16)
    out_ref[...] = lax.dot_general(
        hits, raw_ref[...], (((0,), (0,)), ((), ())), preferred_element_type=F32
    ).astype(BF16)
    for copy in copies[2:]:
        copy.wait()
    ids = ids_ref[...]
    slots = jnp.zeros_like(ids)
    for e in range(slot_ref.shape[0]):
        slots = jnp.where(ids == e, slot_ref[e], slots)
    lane = lax.broadcasted_iota(jnp.int32, dense_ref.shape, 1)
    gates = jnp.zeros(dense_ref.shape, F32)
    for t in range(ids.shape[1]):
        gates = gates + jnp.where(lane == slots[:, t : t + 1], gates_ref[:, t : t + 1], 0.0)
    dense_ref[...] = gates


def latent_kernel(spans, *refs):
    parts = refs[:spans]
    gain_ref, weight_ref, dense_ref, compact_ref, normed_ref, sent_ref = refs[spans:]
    index = here()[1]
    rows, block = parts[0].shape
    values = [p[...].astype(F32) for p in parts]
    square = sum(jnp.sum(v * v, axis=1, keepdims=True) for v in values)
    factor = lax.rsqrt(square / (spans * block) + EPS)
    for k in range(spans):
        at = pl.ds(pl.multiple_of((index ^ k) * block, block), block)
        compact_ref[:, at] = parts[k][...]
        normed_ref[:, at] = (values[k] * factor * gain_ref[:, at]).astype(BF16)
    sent_ref[0:rows, :] = jnp.zeros((rows, sent_ref.shape[1]), F32)
    sent_ref[0:rows, 0 : weight_ref.shape[0]] = nt(normed_ref[...], weight_ref[...])
    sent_ref[rows:, :] = dense_ref[...]


def rotated(values, cosine, sine):
    half = values.shape[1] // 2
    swapped = jnp.concatenate([values[:, half:], values[:, :half]], axis=1)
    return values * cosine + swapped * sine


def query_kernel(
    heads,
    raw_rows,
    normed_ref,
    weight_ref,
    keep_hbm,
    kv_hbm,
    moe_hbm,
    out_ref,
    cos_ref,
    sin_ref,
    live_ref,
    kv_ref,
    moe_ref,
    buf,
    keep_ref,
    sem,
):
    rows = normed_ref.shape[0]
    latent = weight_ref.shape[1] // heads
    steps = buf.shape[0]
    deep = buf.shape[1]
    small = [(keep_hbm, keep_ref), (kv_hbm, kv_ref), (moe_hbm, moe_ref)]
    small = [pltpu.make_async_copy(a, b, sem.at[steps + n]) for n, (a, b) in enumerate(small)]
    copies = [
        pltpu.make_async_copy(weight_ref.at[pl.ds(n * deep, deep), :], buf.at[n], sem.at[n])
        for n in range(steps)
    ]
    for copy in small + copies:
        copy.start()
    small[0].wait()
    diagonal = lax.broadcasted_iota(jnp.int32, (rows, rows), 0) == lax.broadcasted_iota(
        jnp.int32, (rows, rows), 1
    )
    listing = jnp.sum(
        jnp.where(diagonal, keep_ref[...].astype(F32), 0.0), axis=1, keepdims=True
    )
    live_ref[...] = jnp.where(listing >= 0, 1.0, 0.0)
    positions = (here()[0] * raw_rows).astype(F32) + jnp.maximum(listing, 0.0)
    rope = cos_ref.shape[1]
    half = rope // 2
    lane = lax.broadcasted_iota(jnp.int32, (rows, rope), 1)
    first = lane < half
    place = jnp.where(first, lane, lane - half).astype(F32)
    angles = positions * jnp.exp(place * (-2.0 / rope * math.log(THETA)))
    cos_ref[...] = jnp.cos(angles)
    sine = jnp.sin(angles)
    sin_ref[...] = jnp.where(first, -sine, sine)
    total = jnp.zeros((rows, weight_ref.shape[1]), F32)
    for n in range(steps):
        copies[n].wait()
        total = total + nn(normed_ref[:, n * deep : (n + 1) * deep], buf[n])
    kv_rank = latent - rope
    out_ref[...] = jnp.zeros(out_ref.shape, BF16)
    for h in range(heads):
        one = total[:, h * latent : (h + 1) * latent]
        out_ref[h * rows : (h + 1) * rows, 0:kv_rank] = one[:, :kv_rank].astype(BF16)
        out_ref[h * rows : (h + 1) * rows, kv_rank:latent] = rotated(
            one[:, kv_rank:], cos_ref[...], sin_ref[...]
        ).astype(BF16)
    for copy in small[1:]:
        copy.wait()


def cache_kernel(spans, width, experts, *refs):
    parts = refs[:spans]
    live_ref, gain_ref, cos_ref, sin_ref, cached_ref, sent_ref = refs[spans:]
    rows = live_ref.shape[0]
    kv_rank = gain_ref.shape[1]
    values = natural([p[...] for p in parts], here()[1])
    latent = jnp.concatenate([v[:rows, :width] for v in values], axis=1)
    gates = jnp.concatenate([v[rows:, :experts] for v in values], axis=0)
    nope = latent[:, :kv_rank]
    factor = lax.rsqrt(jnp.mean(nope * nope, axis=1, keepdims=True) + EPS)
    nope = nope * factor * gain_ref[...]
    rope = rotated(latent[:, kv_rank:], cos_ref[...], sin_ref[...])
    cached_ref[:, :kv_rank] = nope.astype(BF16)
    cached_ref[:, kv_rank:] = rope.astype(BF16)
    high = gates.astype(BF16).astype(F32)
    used = rope.shape[1] + 2 * experts + 1
    tail = [rope, high, gates - high, live_ref[...]]
    rest = sent_ref.shape[1] - kv_rank - used
    if rest:
        tail.append(jnp.zeros((rows, rest), F32))
    sent_ref[:, :kv_rank] = nope.astype(BF16)
    sent_ref[:, kv_rank:] = jnp.concatenate(tail, axis=1).astype(BF16)


def attend_kernel(heads, kv_rank, flag_lane, blocks, query_ref, mine_ref, theirs_ref, *refs):
    weights = refs[:blocks]
    out_ref, buf, sem = refs[blocks:]
    copies = [pltpu.make_async_copy(weights[n], buf.at[n], sem.at[n]) for n in range(blocks)]
    for copy in copies:
        copy.start()
    count = query_ref.shape[0] // heads
    index = here()[0]
    keys = jnp.concatenate([mine_ref[...], theirs_ref[...]], axis=0)
    total = keys.shape[0]
    width = keys.shape[1]
    lane = lax.broadcasted_iota(jnp.int32, (8, width), 1)
    flags = nt(jnp.where(lane == flag_lane, 1.0, 0.0).astype(BF16), keys)[0:1, :]
    row = lax.broadcasted_iota(jnp.int32, (count, total), 0)
    col = lax.broadcasted_iota(jnp.int32, (count, total), 1)
    half = blocks // 2
    at = col // count
    which = jnp.where(at < half, 2 * at, 2 * (at - half) + 1)
    key_ids = (which ^ index) * count + col % count
    allowed = (key_ids <= index * count + row) & (flags > 0)
    mixed = []
    for h in range(heads):
        scores = nt(query_ref[h * count : (h + 1) * count, :], keys) * SCALE
        scores = jnp.where(allowed, scores, NEGATIVE)
        highest = jnp.max(scores, axis=1, keepdims=True)
        weight = jnp.where(allowed, jnp.exp(scores - highest), 0.0)
        denominator = jnp.sum(weight, axis=1, keepdims=True)
        summed = nn(weight.astype(BF16), keys[:, :kv_rank])
        mixed.append((summed / denominator).astype(BF16))
    mixed = jnp.concatenate(mixed, axis=1)
    block = buf.shape[2]
    for n in range(blocks):
        i = 2 * n if n < half else 2 * (n - half) + 1
        copies[n].wait()
        place = pl.ds(pl.multiple_of((index ^ i) * block, block), block)
        out_ref[:, place] = nn(mixed, buf[n]).astype(BF16)


def resid_kernel(spans, *refs):
    parts = refs[:spans]
    compact_ref, gain_ref, own_ref, out_ref, buf = refs[spans:]
    resid = compact_ref[...].astype(F32) + sum(p[...].astype(F32) for p in parts)
    factor = lax.rsqrt(jnp.mean(resid * resid, axis=1, keepdims=True) + EPS)
    out_ref[...] = (resid * factor * gain_ref[...]).astype(BF16)
    buf[...] = resid
    count = own_ref.shape[0]
    own_ref[...] = buf[pl.ds(pl.multiple_of(here()[1] * count, count), count), :]


def expert_kernel(
    first_lane,
    tail_at,
    experts,
    cuts,
    columns,
    mine_ref,
    theirs_ref,
    mine_tail_ref,
    theirs_tail_ref,
    in_ref,
    out_weight_ref,
    near_ref,
    far_ref,
    act_ref,
):
    rows = jnp.concatenate([mine_ref[...], theirs_ref[...]], axis=0)
    tail = jnp.concatenate([mine_tail_ref[:, tail_at:], theirs_tail_ref[:, tail_at:]], axis=0)
    tail = tail.astype(F32)
    lane = lax.broadcasted_iota(jnp.int32, tail.shape, 1) - first_lane
    index = here()
    slot = lax.div(index[0] * lax.axis_size("span") + index[1], 2)
    scale = jnp.sum(
        jnp.where((lane == slot) | (lane == slot + experts), tail, 0.0), axis=1, keepdims=True
    )
    for start, size in cuts:
        gate = nt(rows, in_ref[0, start : start + size, :])
        upper = nt(rows, in_ref[1, start : start + size, :])
        act_ref[:, start : start + size] = (gate / (1.0 + jnp.exp(-gate)) * upper).astype(BF16)
    half = mine_ref.shape[0]
    width = out_weight_ref.shape[1] // columns
    for n in range(columns):
        span = slice(n * width, (n + 1) * width)
        done = nn(act_ref[...], out_weight_ref[:, span])
        done = jnp.where(scale > 0, done * scale, 0.0).astype(BF16)
        near_ref[:, span] = done[:half]
        far_ref[:, span] = done[half:]


def level_kernel(near_ref, back_ref, *outs):
    rows = outs[0].shape[0]
    for n, out in enumerate(outs):
        at = slice(n * rows, (n + 1) * rows)
        out[...] = (near_ref[at, :].astype(F32) + back_ref[at, :].astype(F32)).astype(out.dtype)


def rows_kernel(spans, *refs):
    parts, outs, buf = refs[: -spans - 1], refs[-spans - 1 : -1], refs[-1]
    index = here()[1]
    total = parts[0][...]
    for p in parts[1:]:
        total = total + p[...].astype(F32)
    buf[...] = total
    count = outs[0].shape[0]
    for k, out in enumerate(outs):
        at = pl.ds(pl.multiple_of((index ^ k) * count, count), count)
        out[...] = buf[at, :].astype(out.dtype)


def last_kernel(spans, *refs):
    parts = refs[:spans]
    own_ref, live_ref, out_ref = refs[spans:]
    count = out_ref.shape[0]
    routed = sum(p[...].astype(F32) for p in parts)
    at = pl.ds(pl.multiple_of(here()[1] * count, count), count)
    total = own_ref[...] + routed
    out_ref[...] = jnp.where(live_ref[at, :] > 0, total, 0.0).astype(BF16)


def per_device(
    raw_tokens,
    keep,
    attn_gain,
    query_weight,
    latent_weight,
    kv_gain,
    out_weight,
    moe_gain,
    expert_ids,
    gate_values,
    expert_slot,
    expert_in,
    expert_out,
):
    kv_rank = kv_gain.shape[0]
    spans = lax.axis_size("span")
    contexts = lax.axis_size("context")
    part_width = latent_weight.shape[1]
    latent_width = part_width * spans
    rope = latent_width - kv_rank
    model = attn_gain.shape[0]
    kept = keep.shape[1]
    raw_rows = raw_tokens.shape[0]
    heads = query_weight.shape[1] // latent_width
    rows_dev = expert_ids.shape[0]
    experts = expert_slot.shape[0]
    hidden = expert_in.shape[3]
    evens = list(range(0, contexts, 2))

    sent_width = up(max(part_width, experts))
    picked, near_weight, gain, dense = call(
        pick_kernel,
        [
            shape((kept, raw_tokens.shape[1]), BF16),
            shape((part_width, model), BF16),
            shape((1, model), F32),
            shape((rows_dev, sent_width), F32),
        ],
        [HBM] * 7,
        (keep, raw_tokens, latent_weight.T, attn_gain[None], expert_ids, gate_values, expert_slot),
        scratch=[
            pltpu.VMEM(keep.shape, jnp.int32),
            pltpu.VMEM(raw_tokens.shape, BF16),
            pltpu.VMEM(expert_ids.shape, jnp.int32),
            pltpu.VMEM(gate_values.shape, F32),
            pltpu.SMEM(expert_slot.shape, jnp.int32),
            pltpu.SemaphoreType.DMA((7,)),
        ],
        limit=4,
    )
    parts = gathered(picked, "span", range(1, spans))
    weights_even = gathered(out_weight, "context", evens[1:])
    weights_odd = [partner(w, "context", 1) for w in weights_even]

    compact, normed, sent = call(
        functools.partial(latent_kernel, spans),
        [
            shape((kept, model), BF16),
            shape((kept, model), BF16),
            shape((kept + rows_dev, sent_width), F32),
        ],
        [VM] * (spans + 3),
        (*parts, gain, near_weight, dense),
        flops=2 * kept * latent_weight.size,
        moved=2 * latent_weight.size,
        limit=4,
    )
    parts = gathered(sent, "span", range(1, spans))
    steps = 8
    row_width = up(latent_width + 2 * experts + 1)
    query, cosine, sine, live, near_kv, near_moe = call(
        functools.partial(query_kernel, heads, raw_rows),
        [
            shape((heads * kept, row_width), BF16),
            shape((kept, rope), F32),
            shape((kept, rope), F32),
            shape((kept, 1), F32),
            shape((1, kv_rank), F32),
            shape((1, model), F32),
        ],
        [VM] + [HBM] * 4,
        (normed, query_weight, keep, kv_gain[None], moe_gain[None]),
        scratch=[
            pltpu.VMEM((steps, model // steps, query_weight.shape[1]), BF16),
            pltpu.VMEM(keep.shape, jnp.int32),
            pltpu.SemaphoreType.DMA((steps + 3,)),
        ],
        flops=2 * kept * query_weight.size,
        moved=2 * query_weight.size,
        limit=10,
    )
    cached, sent = call(
        functools.partial(cache_kernel, spans, part_width, experts),
        [shape((kept, latent_width), BF16), shape((kept, row_width), BF16)],
        [VM] * (spans + 4),
        (*parts, live, near_kv, cosine, sine),
        limit=4,
    )

    mine_keys = jnp.concatenate(gathered(sent, "context", evens[1:]), axis=0)
    their_keys = partner(mine_keys, "context", 1)
    partial = call(
        functools.partial(
            attend_kernel, heads, kv_rank, latent_width + 2 * experts, contexts
        ),
        shape((kept, model), BF16),
        [VM, VM, VM, HBM] + [ANY] * (contexts - 1),
        (query, mine_keys, their_keys, *weights_even, *weights_odd),
        scratch=[
            pltpu.VMEM((contexts, *out_weight.shape), BF16),
            pltpu.SemaphoreType.DMA((contexts,)),
        ],
        flops=2 * kept * contexts * out_weight.size,
        moved=2 * contexts * out_weight.size,
        limit=12,
    )

    got = gathered(partial, "span", range(1, spans))
    own, moe_in = call(
        functools.partial(resid_kernel, spans),
        [shape((rows_dev, model), F32), shape((kept, model), BF16)],
        [VM] * (spans + 2),
        (*got, compact, near_moe),
        scratch=[pltpu.VMEM((kept, model), F32)],
        limit=6,
    )

    mine = jnp.concatenate(gathered(moe_in, "context", evens[1:]), axis=0)
    theirs = partner(mine, "context", 1)
    half = mine.shape[0]
    cuts, start = [], 0
    while start < hidden:
        size = min(2 * LANES, hidden - start)
        cuts.append((start, size))
        start += size
    near, far = call(
        functools.partial(expert_kernel, latent_width - kv_rank, kv_rank, experts, cuts, 4),
        [shape((half, model), BF16), shape((half, model), BF16)],
        [VM] * 6,
        (mine, theirs, mine_keys, their_keys, jnp.swapaxes(expert_in[0], 1, 2), expert_out[0]),
        scratch=[pltpu.VMEM((2 * half, hidden), BF16)],
        flops=6 * 2 * half * hidden * model,
        moved=6 * hidden * model,
        limit=24,
    )

    levels = call(
        level_kernel,
        [shape((kept, model), F32)] + [shape((kept, model), BF16)] * (len(evens) - 1),
        [VM, VM],
        (near, partner(far, "context", 1)),
        limit=6,
    )
    got = [partner(level, "context", i) for level, i in zip(levels[1:], evens[1:])]
    rows = call(
        functools.partial(rows_kernel, spans),
        [shape((rows_dev, model), F32)] + [shape((rows_dev, model), BF16)] * (spans - 1),
        [VM] * len(levels),
        (levels[0], *got),
        scratch=[pltpu.VMEM((kept, model), F32)],
        limit=6,
    )
    got = []
    for k in range(1, spans):
        got.append(partner(rows[k], "span", k))
    layer_out = call(
        functools.partial(last_kernel, spans),
        shape((rows_dev, model), BF16),
        [VM] * (spans + 2),
        (rows[0], *got, own, live),
        limit=4,
    )
    return (layer_out, cached)


def solution(mesh):
    placed = (
        P(("groups", "context"), "span"),
        P(("groups", "context"), None),
        P(),
        P(None, "span"),
        P(None, "span"),
        P(),
        P("span", "context"),
        P(),
        P(("groups", "context", "span"), None),
        P(("groups", "context", "span"), None),
        P(),
        P(("context", "span"), None, None, None),
        P(("context", "span"), None, None),
    )
    return jax.shard_map(
        per_device,
        mesh=mesh,
        in_specs=placed,
        out_specs=(P(("groups", "context", "span"), None), P(("groups", "context"), None)),
        check_vma=False,
    )
```

```python
import functools
import math

import jax
import jax.numpy as jnp
from jax import lax
from jax.experimental import pallas as pl
from jax.experimental.pallas import tpu as pltpu
from jax.sharding import PartitionSpec as P


EPS = 1e-06
THETA = 50000.0
SCALE = 192.0 ** (-0.5)
NEGATIVE = -1e30
LANES = 128
F32 = jnp.float32
BF16 = jnp.bfloat16
MIB = 1 << 20


VM = pl.BlockSpec(memory_space=pltpu.VMEM)
HBM = pl.BlockSpec(memory_space=pltpu.HBM)


def up(count, unit=LANES):
    return -(-count // unit) * unit


def shape(dims, dtype):
    return jax.ShapeDtypeStruct(tuple(dims), dtype)


def call(kernel, outs, in_specs, args, scratch=(), flops=0, moved=0, limit=16):
    single = not isinstance(outs, (list, tuple))
    args = [
        pltpu.with_memory_space_constraint(value, pltpu.HBM) if spec is HBM else value
        for spec, value in zip(in_specs, args)
    ]
    return pl.pallas_call(
        kernel,
        out_shape=outs,
        in_specs=in_specs,
        out_specs=VM if single else [VM] * len(outs),
        scratch_shapes=list(scratch),
        compiler_params=pltpu.CompilerParams(vmem_limit_bytes=limit * MIB),
        cost_estimate=pl.CostEstimate(flops=flops, bytes_accessed=moved, transcendentals=0),
    )(*args)


def nt(left, right):
    return lax.dot_general(left, right, (((1,), (1,)), ((), ())), preferred_element_type=F32)


def nn(left, right):
    return jnp.dot(left, right, preferred_element_type=F32)


def here():
    return lax.axis_index("context"), lax.axis_index("span")


def partner(values, axis, mask):
    count = lax.axis_size(axis)
    return lax.ppermute(values, axis, [(i, i ^ mask) for i in range(count)])


def gathered(values, axis, masks):
    parts = [values]
    for mask in masks:
        parts.append(partner(values, axis, mask))
    return parts


def natural(parts, index):
    bit = 1
    while bit < len(parts):
        swap = (index & bit) != 0
        parts = [jnp.where(swap, parts[k ^ bit], parts[k]) for k in range(len(parts))]
        bit *= 2
    return parts


def pick_kernel(
    keep_hbm,
    raw_hbm,
    weight_hbm,
    gain_hbm,
    ids_hbm,
    gates_hbm,
    slot_hbm,
    out_ref,
    weight_ref,
    gain_ref,
    dense_ref,
    keep_ref,
    raw_ref,
    ids_ref,
    gates_ref,
    slot_ref,
    sem,
):
    pairs = [
        (keep_hbm, keep_ref),
        (raw_hbm, raw_ref),
        (ids_hbm, ids_ref),
        (gates_hbm, gates_ref),
        (slot_hbm, slot_ref),
        (gain_hbm, gain_ref),
        (weight_hbm, weight_ref),
    ]
    copies = [pltpu.make_async_copy(a, b, sem.at[n]) for n, (a, b) in enumerate(pairs)]
    for copy in copies:
        copy.start()
    copies[0].wait()
    copies[1].wait()
    rows = lax.broadcasted_iota(jnp.int32, (raw_ref.shape[0], keep_ref.shape[1]), 0)
    hits = jnp.where(rows == keep_ref[...], 1.0, 0.0).astype(BF16)
    out_ref[...] = lax.dot_general(
        hits, raw_ref[...], (((0,), (0,)), ((), ())), preferred_element_type=F32
    ).astype(BF16)
    for copy in copies[2:]:
        copy.wait()
    ids = ids_ref[...]
    slots = jnp.zeros_like(ids)
    for e in range(slot_ref.shape[0]):
        slots = jnp.where(ids == e, slot_ref[e], slots)
    lane = lax.broadcasted_iota(jnp.int32, dense_ref.shape, 1)
    gates = jnp.zeros(dense_ref.shape, F32)
    for t in range(ids.shape[1]):
        gates = gates + jnp.where(lane == slots[:, t : t + 1], gates_ref[:, t : t + 1], 0.0)
    dense_ref[...] = gates


def latent_kernel(spans, *refs):
    parts = refs[:spans]
    gain_ref, weight_ref, dense_ref, compact_ref, normed_ref, sent_ref = refs[spans:]
    index = here()[1]
    rows, block = parts[0].shape
    values = [p[...].astype(F32) for p in parts]
    square = sum(jnp.sum(v * v, axis=1, keepdims=True) for v in values)
    factor = lax.rsqrt(square / (spans * block) + EPS)
    for k in range(spans):
        at = pl.ds(pl.multiple_of((index ^ k) * block, block), block)
        compact_ref[:, at] = parts[k][...]
        normed_ref[:, at] = (values[k] * factor * gain_ref[:, at]).astype(BF16)
    sent_ref[0:rows, :] = jnp.zeros((rows, sent_ref.shape[1]), F32)
    sent_ref[0:rows, 0 : weight_ref.shape[0]] = nt(normed_ref[...], weight_ref[...])
    sent_ref[rows:, :] = dense_ref[...]


def rotated(values, cosine, sine):
    half = values.shape[1] // 2
    swapped = jnp.concatenate([values[:, half:], values[:, :half]], axis=1)
    return values * cosine + swapped * sine


def query_kernel(
    heads,
    raw_rows,
    normed_ref,
    weight_ref,
    keep_hbm,
    kv_hbm,
    moe_hbm,
    out_ref,
    cos_ref,
    sin_ref,
    live_ref,
    kv_ref,
    moe_ref,
    buf,
    keep_ref,
    sem,
):
    rows = normed_ref.shape[0]
    latent = weight_ref.shape[1] // heads
    steps = buf.shape[0]
    deep = buf.shape[1]
    small = [(keep_hbm, keep_ref), (kv_hbm, kv_ref), (moe_hbm, moe_ref)]
    small = [pltpu.make_async_copy(a, b, sem.at[steps + n]) for n, (a, b) in enumerate(small)]
    copies = [
        pltpu.make_async_copy(weight_ref.at[pl.ds(n * deep, deep), :], buf.at[n], sem.at[n])
        for n in range(steps)
    ]
    for copy in small + copies:
        copy.start()
    small[0].wait()
    diagonal = lax.broadcasted_iota(jnp.int32, (rows, rows), 0) == lax.broadcasted_iota(
        jnp.int32, (rows, rows), 1
    )
    listing = jnp.sum(
        jnp.where(diagonal, keep_ref[...].astype(F32), 0.0), axis=1, keepdims=True
    )
    live_ref[...] = jnp.where(listing >= 0, 1.0, 0.0)
    positions = (here()[0] * raw_rows).astype(F32) + jnp.maximum(listing, 0.0)
    rope = cos_ref.shape[1]
    half = rope // 2
    lane = lax.broadcasted_iota(jnp.int32, (rows, rope), 1)
    first = lane < half
    place = jnp.where(first, lane, lane - half).astype(F32)
    angles = positions * jnp.exp(place * (-2.0 / rope * math.log(THETA)))
    cos_ref[...] = jnp.cos(angles)
    sine = jnp.sin(angles)
    sin_ref[...] = jnp.where(first, -sine, sine)
    total = jnp.zeros((rows, weight_ref.shape[1]), F32)
    for n in range(steps):
        copies[n].wait()
        total = total + nn(normed_ref[:, n * deep : (n + 1) * deep], buf[n])
    kv_rank = latent - rope
    out_ref[...] = jnp.zeros(out_ref.shape, BF16)
    for h in range(heads):
        one = total[:, h * latent : (h + 1) * latent]
        out_ref[h * rows : (h + 1) * rows, 0:kv_rank] = one[:, :kv_rank].astype(BF16)
        out_ref[h * rows : (h + 1) * rows, kv_rank:latent] = rotated(
            one[:, kv_rank:], cos_ref[...], sin_ref[...]
        ).astype(BF16)
    for copy in small[1:]:
        copy.wait()


def cache_kernel(spans, width, experts, *refs):
    parts = refs[:spans]
    live_ref, gain_ref, cos_ref, sin_ref, query_ref, cached_ref, sent_ref = refs[spans:]
    rows = live_ref.shape[0]
    kv_rank = gain_ref.shape[1]
    values = natural([p[...] for p in parts], here()[1])
    latent = jnp.concatenate([v[:rows, :width] for v in values], axis=1)
    gates = jnp.concatenate([v[rows:, :experts] for v in values], axis=0)
    nope = latent[:, :kv_rank]
    factor = lax.rsqrt(jnp.mean(nope * nope, axis=1, keepdims=True) + EPS)
    nope = nope * factor * gain_ref[...]
    rope = rotated(latent[:, kv_rank:], cos_ref[...], sin_ref[...])
    cached_ref[:, :kv_rank] = nope.astype(BF16)
    cached_ref[:, kv_rank:] = rope.astype(BF16)
    high = gates.astype(BF16).astype(F32)
    used = rope.shape[1] + 2 * experts + 1
    tail = [rope, high, gates - high, live_ref[...]]
    rest = sent_ref.shape[1] - kv_rank - used
    if rest:
        tail.append(jnp.zeros((rows, rest), F32))
    sent_ref[:rows, :kv_rank] = nope.astype(BF16)
    sent_ref[:rows, kv_rank:] = jnp.concatenate(tail, axis=1).astype(BF16)
    sent_ref[rows:, :] = query_ref[...]


def places(blocks):
    return list(range(0, blocks, 2)) + list(range(1, blocks, 2))


def attend_kernel(
    heads, kv_rank, flag_lane, blocks, mine_ref, theirs_ref, weight_hbm, out_ref, weight_ref, sem
):
    copy = pltpu.make_async_copy(weight_hbm, weight_ref, sem)
    copy.start()
    count = mine_ref.shape[1] // (1 + heads)
    index = here()[0]
    half = blocks // 2
    pieces = [(mine_ref, n) for n in range(half)] + [(theirs_ref, n) for n in range(half)]

    def gather(n):
        return jnp.concatenate(
            [ref[p, n * count : (n + 1) * count, :] for ref, p in pieces], axis=0
        )

    keys = gather(0)
    total, width = keys.shape
    lane = lax.broadcasted_iota(jnp.int32, (8, width), 1)
    flags = nt(jnp.where(lane == flag_lane, 1.0, 0.0).astype(BF16), keys)[0:1, :]

    def slot(dims, axis):
        line = lax.broadcasted_iota(jnp.int32, dims, axis)
        at = line // count
        which = jnp.where(at < half, 2 * at, 2 * (at - half) + 1)
        return (which ^ index) * count + line % count

    allowed = (slot((1, total), 1) <= slot((total, 1), 0)) & (flags > 0)
    result = jnp.zeros(out_ref.shape, F32)
    for h in range(heads):
        scores = nt(gather(1 + h), keys) * SCALE
        scores = jnp.where(allowed, scores, NEGATIVE)
        highest = jnp.max(scores, axis=1, keepdims=True)
        weight = jnp.where(allowed, jnp.exp(scores - highest), 0.0)
        denominator = jnp.sum(weight, axis=1, keepdims=True)
        summed = nn(weight.astype(BF16), keys[:, :kv_rank])
        mixed = (summed / denominator).astype(BF16)
        if h == 0:
            copy.wait()
        result = result + nn(mixed, weight_ref[h * kv_rank : (h + 1) * kv_rank, :])
    out_ref[...] = result.astype(BF16)


def sum_kernel(*refs):
    refs[-1][...] = sum(ref[...].astype(F32) for ref in refs[:-1]).astype(BF16)


def resid_kernel(blocks, *refs):
    mine_ref, theirs_ref, mine_rows, their_rows, gain_ref, own_ref, out_ref, buf = refs
    order = places(blocks)
    half = blocks // 2
    index = here()
    count, width = mine_rows.shape[1], mine_ref.shape[2]
    for n, i in enumerate(order):
        ref, p = (mine_ref, n) if n < half else (theirs_ref, n - half)
        lanes = pl.ds(pl.multiple_of((index[0] ^ i) * width, width), width)
        for at, j in enumerate(order):
            to = order.index(i ^ j)
            buf[to * count : (to + 1) * count, lanes] = ref[
                p, at * count : (at + 1) * count, :
            ].astype(F32)
    for n in range(blocks):
        rows, p = (mine_rows, n) if n < half else (their_rows, n - half)
        at = slice(n * count, (n + 1) * count)
        resid = rows[p].astype(F32) + buf[at, :]
        factor = lax.rsqrt(jnp.mean(resid * resid, axis=1, keepdims=True) + EPS)
        out_ref[at, :] = (resid * factor * gain_ref[...]).astype(BF16)
        if n == 0:
            buf[at, :] = resid
    size = own_ref.shape[0]
    own_ref[...] = buf[pl.ds(pl.multiple_of(index[1] * size, size), size), :]


def expert_kernel(
    first_lane,
    tail_at,
    experts,
    cuts,
    columns,
    rows_ref,
    mine_tail_ref,
    theirs_tail_ref,
    in_ref,
    out_weight_ref,
    near_ref,
    far_ref,
    act_ref,
):
    rows = rows_ref[...]
    pieces = mine_tail_ref.shape[0]
    count = rows.shape[0] // (2 * pieces)
    tail = jnp.concatenate(
        [ref[p, :count, tail_at:] for ref in (mine_tail_ref, theirs_tail_ref) for p in range(pieces)],
        axis=0,
    )
    tail = tail.astype(F32)
    lane = lax.broadcasted_iota(jnp.int32, tail.shape, 1) - first_lane
    index = here()
    slot = lax.div(index[0] * lax.axis_size("span") + index[1], 2)
    scale = jnp.sum(
        jnp.where((lane == slot) | (lane == slot + experts), tail, 0.0), axis=1, keepdims=True
    )
    for start, size in cuts:
        gate = nt(rows, in_ref[0, start : start + size, :])
        upper = nt(rows, in_ref[1, start : start + size, :])
        act_ref[:, start : start + size] = (gate / (1.0 + jnp.exp(-gate)) * upper).astype(BF16)
    half = near_ref.shape[0]
    width = out_weight_ref.shape[1] // columns
    for n in range(columns):
        span = slice(n * width, (n + 1) * width)
        done = nn(act_ref[...], out_weight_ref[:, span])
        done = jnp.where(scale > 0, done * scale, 0.0).astype(BF16)
        near_ref[:, span] = done[:half]
        far_ref[:, span] = done[half:]


def level_kernel(near_ref, back_ref, *outs):
    rows = outs[0].shape[0]
    for n, out in enumerate(outs):
        at = slice(n * rows, (n + 1) * rows)
        out[...] = (near_ref[at, :].astype(F32) + back_ref[at, :].astype(F32)).astype(out.dtype)


def rows_kernel(spans, *refs):
    parts, outs, buf = refs[: -spans - 1], refs[-spans - 1 : -1], refs[-1]
    index = here()[1]
    total = parts[0][...]
    for p in parts[1:]:
        total = total + p[...].astype(F32)
    buf[...] = total
    count = outs[0].shape[0]
    for k, out in enumerate(outs):
        at = pl.ds(pl.multiple_of((index ^ k) * count, count), count)
        out[...] = buf[at, :].astype(out.dtype)


def last_kernel(spans, *refs):
    parts = refs[:spans]
    own_ref, live_ref, out_ref = refs[spans:]
    count = out_ref.shape[0]
    routed = sum(p[...].astype(F32) for p in parts)
    at = pl.ds(pl.multiple_of(here()[1] * count, count), count)
    total = own_ref[...] + routed
    out_ref[...] = jnp.where(live_ref[at, :] > 0, total, 0.0).astype(BF16)


def per_device(
    raw_tokens,
    keep,
    attn_gain,
    query_weight,
    latent_weight,
    kv_gain,
    out_weight,
    moe_gain,
    expert_ids,
    gate_values,
    expert_slot,
    expert_in,
    expert_out,
):
    kv_rank = kv_gain.shape[0]
    spans = lax.axis_size("span")
    contexts = lax.axis_size("context")
    part_width = latent_weight.shape[1]
    latent_width = part_width * spans
    rope = latent_width - kv_rank
    model = attn_gain.shape[0]
    kept = keep.shape[1]
    raw_rows = raw_tokens.shape[0]
    heads = query_weight.shape[1] // latent_width
    rows_dev = expert_ids.shape[0]
    experts = expert_slot.shape[0]
    hidden = expert_in.shape[3]
    evens = list(range(0, contexts, 2))

    sent_width = up(max(part_width, experts))
    picked, near_weight, gain, dense = call(
        pick_kernel,
        [
            shape((kept, raw_tokens.shape[1]), BF16),
            shape((part_width, model), BF16),
            shape((1, model), F32),
            shape((rows_dev, sent_width), F32),
        ],
        [HBM] * 7,
        (keep, raw_tokens, latent_weight.T, attn_gain[None], expert_ids, gate_values, expert_slot),
        scratch=[
            pltpu.VMEM(keep.shape, jnp.int32),
            pltpu.VMEM(raw_tokens.shape, BF16),
            pltpu.VMEM(expert_ids.shape, jnp.int32),
            pltpu.VMEM(gate_values.shape, F32),
            pltpu.SMEM(expert_slot.shape, jnp.int32),
            pltpu.SemaphoreType.DMA((7,)),
        ],
        limit=4,
    )
    parts = gathered(picked, "span", range(1, spans))
    compact, normed, sent = call(
        functools.partial(latent_kernel, spans),
        [
            shape((kept, model), BF16),
            shape((kept, model), BF16),
            shape((kept + rows_dev, sent_width), F32),
        ],
        [VM] * (spans + 3),
        (*parts, gain, near_weight, dense),
        flops=2 * kept * latent_weight.size,
        moved=2 * latent_weight.size,
        limit=4,
    )
    parts = gathered(sent, "span", range(1, spans))
    steps = 8
    row_width = up(latent_width + 2 * experts + 1)
    query, cosine, sine, live, near_kv, near_moe = call(
        functools.partial(query_kernel, heads, raw_rows),
        [
            shape((heads * kept, row_width), BF16),
            shape((kept, rope), F32),
            shape((kept, rope), F32),
            shape((kept, 1), F32),
            shape((1, kv_rank), F32),
            shape((1, model), F32),
        ],
        [VM] + [HBM] * 4,
        (normed, query_weight, keep, kv_gain[None], moe_gain[None]),
        scratch=[
            pltpu.VMEM((steps, model // steps, query_weight.shape[1]), BF16),
            pltpu.VMEM(keep.shape, jnp.int32),
            pltpu.SemaphoreType.DMA((steps + 3,)),
        ],
        flops=2 * kept * query_weight.size,
        moved=2 * query_weight.size,
        limit=10,
    )
    cached, sent = call(
        functools.partial(cache_kernel, spans, part_width, experts),
        [shape((kept, latent_width), BF16), shape(((1 + heads) * kept, row_width), BF16)],
        [VM] * (spans + 5),
        (*parts, live, near_kv, cosine, sine, query),
        limit=4,
    )

    mine_keys = jnp.stack(gathered(sent, "context", evens[1:]))
    their_keys = partner(mine_keys, "context", 1)
    partial = call(
        functools.partial(attend_kernel, heads, kv_rank, latent_width + 2 * experts, contexts),
        shape((contexts * kept, out_weight.shape[1]), BF16),
        [VM, VM, HBM],
        (mine_keys, their_keys, out_weight),
        scratch=[pltpu.VMEM(out_weight.shape, BF16), pltpu.SemaphoreType.DMA],
        flops=2 * kept * contexts * out_weight.size,
        moved=2 * out_weight.size,
        limit=12,
    )

    column = call(
        sum_kernel,
        shape(partial.shape, BF16),
        [VM] * spans,
        gathered(partial, "span", range(1, spans)),
        limit=4,
    )
    mine_rows = jnp.stack(gathered(compact, "context", evens[1:]))
    their_rows = partner(mine_rows, "context", 1)

    mine = jnp.stack(gathered(column, "context", evens[1:]))
    theirs = partner(mine, "context", 1)
    half = mine.shape[0] * kept
    own, moe_in = call(
        functools.partial(resid_kernel, contexts),
        [shape((rows_dev, model), F32), shape((2 * half, model), BF16)],
        [VM] * 5,
        (mine, theirs, mine_rows, their_rows, near_moe),
        scratch=[pltpu.VMEM((2 * half, model), F32)],
        limit=16,
    )
    cuts, start = [], 0
    while start < hidden:
        size = min(2 * LANES, hidden - start)
        cuts.append((start, size))
        start += size
    near, far = call(
        functools.partial(expert_kernel, latent_width - kv_rank, kv_rank, experts, cuts, 4),
        [shape((half, model), BF16), shape((half, model), BF16)],
        [VM] * 5,
        (moe_in, mine_keys, their_keys, jnp.swapaxes(expert_in[0], 1, 2), expert_out[0]),
        scratch=[pltpu.VMEM((2 * half, hidden), BF16)],
        flops=6 * 2 * half * hidden * model,
        moved=6 * hidden * model,
        limit=24,
    )

    levels = call(
        level_kernel,
        [shape((kept, model), F32)] + [shape((kept, model), BF16)] * (len(evens) - 1),
        [VM, VM],
        (near, partner(far, "context", 1)),
        limit=6,
    )
    got = [partner(level, "context", i) for level, i in zip(levels[1:], evens[1:])]
    rows = call(
        functools.partial(rows_kernel, spans),
        [shape((rows_dev, model), F32)] + [shape((rows_dev, model), BF16)] * (spans - 1),
        [VM] * len(levels),
        (levels[0], *got),
        scratch=[pltpu.VMEM((kept, model), F32)],
        limit=6,
    )
    got = []
    for k in range(1, spans):
        got.append(partner(rows[k], "span", k))
    layer_out = call(
        functools.partial(last_kernel, spans),
        shape((rows_dev, model), BF16),
        [VM] * (spans + 2),
        (rows[0], *got, own, live),
        limit=4,
    )
    return (layer_out, cached)


def solution(mesh):
    placed = (
        P(("groups", "context"), "span"),
        P(("groups", "context"), None),
        P(),
        P(None, "span"),
        P(None, "span"),
        P(),
        P("span", "context"),
        P(),
        P(("groups", "context", "span"), None),
        P(("groups", "context", "span"), None),
        P(),
        P(("context", "span"), None, None, None),
        P(("context", "span"), None, None),
    )
    return jax.shard_map(
        per_device,
        mesh=mesh,
        in_specs=placed,
        out_specs=(P(("groups", "context", "span"), None), P(("groups", "context"), None)),
        check_vma=False,
    )
```

```python
import functools
import math

import jax
import jax.numpy as jnp
from jax import lax
from jax.experimental import pallas as pl
from jax.experimental.pallas import tpu as pltpu
from jax.sharding import PartitionSpec as P


EPS = 1e-06
THETA = 50000.0
SCALE = 192.0 ** (-0.5)
NEGATIVE = -1e30
LANES = 128
F32 = jnp.float32
BF16 = jnp.bfloat16
MIB = 1 << 20


VM = pl.BlockSpec(memory_space=pltpu.VMEM)
HBM = pl.BlockSpec(memory_space=pltpu.HBM)


def up(count, unit=LANES):
    return -(-count // unit) * unit


def shape(dims, dtype):
    return jax.ShapeDtypeStruct(tuple(dims), dtype)


def call(kernel, outs, in_specs, args, scratch=(), flops=0, moved=0, limit=16):
    single = not isinstance(outs, (list, tuple))
    args = [
        pltpu.with_memory_space_constraint(value, pltpu.HBM) if spec is HBM else value
        for spec, value in zip(in_specs, args)
    ]
    return pl.pallas_call(
        kernel,
        out_shape=outs,
        in_specs=in_specs,
        out_specs=VM if single else [VM] * len(outs),
        scratch_shapes=list(scratch),
        compiler_params=pltpu.CompilerParams(vmem_limit_bytes=limit * MIB),
        cost_estimate=pl.CostEstimate(flops=flops, bytes_accessed=moved, transcendentals=0),
    )(*args)


def nt(left, right):
    return lax.dot_general(left, right, (((1,), (1,)), ((), ())), preferred_element_type=F32)


def nn(left, right):
    return jnp.dot(left, right, preferred_element_type=F32)


def here():
    return lax.axis_index("context"), lax.axis_index("span")


def partner(values, axis, mask):
    count = lax.axis_size(axis)
    return lax.ppermute(values, axis, [(i, i ^ mask) for i in range(count)])


def gathered(values, axis, masks):
    parts = [values]
    for mask in masks:
        parts.append(partner(values, axis, mask))
    return parts


def natural(parts, index):
    bit = 1
    while bit < len(parts):
        swap = (index & bit) != 0
        parts = [jnp.where(swap, parts[k ^ bit], parts[k]) for k in range(len(parts))]
        bit *= 2
    return parts


def fetch(pairs, sem):
    copies = [pltpu.make_async_copy(a, b, sem.at[n]) for n, (a, b) in enumerate(pairs)]
    for copy in copies:
        copy.start()
    return copies


def pick_kernel(keep_hbm, raw_hbm, out_ref, keep_ref, raw_ref, sem):
    for copy in fetch([(keep_hbm, keep_ref), (raw_hbm, raw_ref)], sem):
        copy.wait()
    rows = lax.broadcasted_iota(jnp.int32, (raw_ref.shape[0], keep_ref.shape[1]), 0)
    hits = jnp.where(rows == keep_ref[...], 1.0, 0.0).astype(BF16)
    out_ref[...] = lax.dot_general(
        hits, raw_ref[...], (((0,), (0,)), ((), ())), preferred_element_type=F32
    ).astype(BF16)


def prepare_kernel(raw_rows, *refs):
    keep_hbm, ids_hbm, gates_hbm, slot_hbm = refs[:4]
    sources = refs[4:9]
    targets = refs[9:14]
    dense_ref, cos_ref, sin_ref, live_ref = refs[14:18]
    keep_ref, ids_ref, gates_ref, slot_ref, sem = refs[18:]
    small = [(keep_hbm, keep_ref), (ids_hbm, ids_ref), (gates_hbm, gates_ref), (slot_hbm, slot_ref)]
    copies = fetch(small + list(zip(sources, targets)), sem)
    for copy in copies[:4]:
        copy.wait()
    ids = ids_ref[...]
    slots = jnp.zeros_like(ids)
    for e in range(slot_ref.shape[0]):
        slots = jnp.where(ids == e, slot_ref[e], slots)
    lane = lax.broadcasted_iota(jnp.int32, dense_ref.shape, 1)
    gates = jnp.zeros(dense_ref.shape, F32)
    for t in range(ids.shape[1]):
        gates = gates + jnp.where(lane == slots[:, t : t + 1], gates_ref[:, t : t + 1], 0.0)
    dense_ref[...] = gates
    rows, rope = cos_ref.shape
    diagonal = lax.broadcasted_iota(jnp.int32, (rows, rows), 0) == lax.broadcasted_iota(
        jnp.int32, (rows, rows), 1
    )
    listing = jnp.sum(
        jnp.where(diagonal, keep_ref[...].astype(F32), 0.0), axis=1, keepdims=True
    )
    live_ref[...] = jnp.where(listing >= 0, 1.0, 0.0)
    positions = (here()[0] * raw_rows).astype(F32) + jnp.maximum(listing, 0.0)
    half = rope // 2
    lane = lax.broadcasted_iota(jnp.int32, (rows, rope), 1)
    first = lane < half
    place = jnp.where(first, lane, lane - half).astype(F32)
    angles = positions * jnp.exp(place * (-2.0 / rope * math.log(THETA)))
    cos_ref[...] = jnp.cos(angles)
    sine = jnp.sin(angles)
    sin_ref[...] = jnp.where(first, -sine, sine)
    for copy in copies[4:]:
        copy.wait()


def latent_kernel(spans, *refs):
    parts = refs[:spans]
    gain_ref, weight_ref, dense_ref, compact_ref, normed_ref, sent_ref = refs[spans:]
    index = here()[1]
    rows, block = parts[0].shape
    values = [p[...].astype(F32) for p in parts]
    square = sum(jnp.sum(v * v, axis=1, keepdims=True) for v in values)
    factor = lax.rsqrt(square / (spans * block) + EPS)
    for k in range(spans):
        at = pl.ds(pl.multiple_of((index ^ k) * block, block), block)
        compact_ref[:, at] = parts[k][...]
        normed_ref[:, at] = (values[k] * factor * gain_ref[:, at]).astype(BF16)
    sent_ref[0:rows, :] = jnp.zeros((rows, sent_ref.shape[1]), F32)
    sent_ref[0:rows, 0 : weight_ref.shape[0]] = nt(normed_ref[...], weight_ref[...])
    sent_ref[rows:, :] = dense_ref[...]


def rotated(values, cosine, sine):
    half = values.shape[1] // 2
    swapped = jnp.concatenate([values[:, half:], values[:, :half]], axis=1)
    return values * cosine + swapped * sine


def query_kernel(heads, normed_ref, weight_ref, cos_ref, sin_ref, out_ref):
    rows = normed_ref.shape[0]
    latent = weight_ref.shape[1] // heads
    total = nn(normed_ref[...], weight_ref[...])
    kv_rank = latent - cos_ref.shape[1]
    out_ref[...] = jnp.zeros(out_ref.shape, BF16)
    for h in range(heads):
        one = total[:, h * latent : (h + 1) * latent]
        out_ref[h * rows : (h + 1) * rows, 0:kv_rank] = one[:, :kv_rank].astype(BF16)
        out_ref[h * rows : (h + 1) * rows, kv_rank:latent] = rotated(
            one[:, kv_rank:], cos_ref[...], sin_ref[...]
        ).astype(BF16)


def cache_kernel(spans, width, experts, *refs):
    parts = refs[:spans]
    live_ref, gain_ref, cos_ref, sin_ref, query_ref, cached_ref, sent_ref = refs[spans:]
    rows = live_ref.shape[0]
    kv_rank = gain_ref.shape[1]
    values = natural([p[...] for p in parts], here()[1])
    latent = jnp.concatenate([v[:rows, :width] for v in values], axis=1)
    gates = jnp.concatenate([v[rows:, :experts] for v in values], axis=0)
    nope = latent[:, :kv_rank]
    factor = lax.rsqrt(jnp.mean(nope * nope, axis=1, keepdims=True) + EPS)
    nope = nope * factor * gain_ref[...]
    rope = rotated(latent[:, kv_rank:], cos_ref[...], sin_ref[...])
    cached_ref[:, :kv_rank] = nope.astype(BF16)
    cached_ref[:, kv_rank:] = rope.astype(BF16)
    high = gates.astype(BF16).astype(F32)
    used = rope.shape[1] + 2 * experts + 1
    tail = [rope, high, gates - high, live_ref[...]]
    rest = sent_ref.shape[1] - kv_rank - used
    if rest:
        tail.append(jnp.zeros((rows, rest), F32))
    sent_ref[:rows, :kv_rank] = nope.astype(BF16)
    sent_ref[:rows, kv_rank:] = jnp.concatenate(tail, axis=1).astype(BF16)
    sent_ref[rows:, :] = query_ref[...]


def places(blocks):
    return list(range(0, blocks, 2)) + list(range(1, blocks, 2))


def attend_kernel(
    heads, kv_rank, flag_lane, blocks, mine_ref, theirs_ref, weight_hbm, out_ref, weight_ref, sem
):
    copy = pltpu.make_async_copy(weight_hbm, weight_ref, sem)
    copy.start()
    count = mine_ref.shape[1] // (1 + heads)
    index = here()[0]
    half = blocks // 2
    pieces = [(mine_ref, n) for n in range(half)] + [(theirs_ref, n) for n in range(half)]

    def gather(n):
        return jnp.concatenate(
            [ref[p, n * count : (n + 1) * count, :] for ref, p in pieces], axis=0
        )

    keys = gather(0)
    total, width = keys.shape
    lane = lax.broadcasted_iota(jnp.int32, (8, width), 1)
    flags = nt(jnp.where(lane == flag_lane, 1.0, 0.0).astype(BF16), keys)[0:1, :]

    def slot(dims, axis):
        line = lax.broadcasted_iota(jnp.int32, dims, axis)
        at = line // count
        which = jnp.where(at < half, 2 * at, 2 * (at - half) + 1)
        return (which ^ index) * count + line % count

    allowed = (slot((1, total), 1) <= slot((total, 1), 0)) & (flags > 0)
    result = jnp.zeros(out_ref.shape, F32)
    for h in range(heads):
        scores = nt(gather(1 + h), keys) * SCALE
        scores = jnp.where(allowed, scores, NEGATIVE)
        highest = jnp.max(scores, axis=1, keepdims=True)
        weight = jnp.where(allowed, jnp.exp(scores - highest), 0.0)
        denominator = jnp.sum(weight, axis=1, keepdims=True)
        summed = nn(weight.astype(BF16), keys[:, :kv_rank])
        mixed = (summed / denominator).astype(BF16)
        if h == 0:
            copy.wait()
        result = result + nn(mixed, weight_ref[h * kv_rank : (h + 1) * kv_rank, :])
    out_ref[...] = result.astype(BF16)


def sum_kernel(*refs):
    refs[-1][...] = sum(ref[...].astype(F32) for ref in refs[:-1]).astype(BF16)


def scaled_rows(blocks, odd, pieces_ref, mine_rows, their_rows, gain_ref, part_ref, rows_ref):
    order = places(blocks)
    half = blocks // 2
    index = here()[0]
    count, width = mine_rows.shape[1], pieces_ref.shape[2]
    squares = [jnp.zeros((count, 1), F32)] * blocks
    for p in range(half):
        i = 2 * p + odd
        lanes = pl.ds(pl.multiple_of((index ^ i) * width, width), width)
        gain = gain_ref[:, lanes]
        for at, j in enumerate(order):
            to = order.index(i ^ j)
            rows = mine_rows if to < half else their_rows
            resid = rows[to % half, :, lanes].astype(F32) + pieces_ref[
                p, at * count : (at + 1) * count, :
            ].astype(F32)
            squares[to] = squares[to] + jnp.sum(resid * resid, axis=1, keepdims=True)
            rows_ref[to * count : (to + 1) * count, p * width : (p + 1) * width] = (
                resid * gain
            ).astype(BF16)
            if to == 0:
                part_ref[:, p * width : (p + 1) * width] = resid
    return jnp.concatenate(squares, axis=0)


def products(blocks, odd, width, rows_ref, in_ref, half, start, size):
    index = here()[0]
    total = jnp.zeros((rows_ref.shape[0], size), F32)
    for p in range(blocks // 2):
        lanes = pl.ds(pl.multiple_of((index ^ (2 * p + odd)) * width, width), width)
        total = total + nt(
            rows_ref[:, p * width : (p + 1) * width], in_ref[half, start : start + size, lanes]
        )
    return total


def begin_kernel(
    blocks,
    cuts,
    mine_ref,
    mine_rows,
    their_rows,
    gain_ref,
    in_ref,
    part_ref,
    square_ref,
    gate_ref,
    upper_ref,
    rows_ref,
):
    square_ref[...] = scaled_rows(
        blocks, 0, mine_ref, mine_rows, their_rows, gain_ref, part_ref, rows_ref
    )
    width = mine_ref.shape[2]
    for start, size in cuts:
        at = slice(start, start + size)
        gate_ref[:, at] = products(blocks, 0, width, rows_ref, in_ref, 0, start, size)
        upper_ref[:, at] = products(blocks, 0, width, rows_ref, in_ref, 1, start, size)


def expert_kernel(
    blocks,
    first_lane,
    tail_at,
    experts,
    cuts,
    columns,
    theirs_ref,
    mine_rows,
    their_rows,
    gain_ref,
    in_ref,
    part_ref,
    square_ref,
    gate_ref,
    upper_ref,
    mine_tail_ref,
    theirs_tail_ref,
    out_weight_ref,
    near_ref,
    far_ref,
    own_ref,
    rows_ref,
    act_ref,
    rest_ref,
    whole_ref,
):
    square = square_ref[...] + scaled_rows(
        blocks, 1, theirs_ref, mine_rows, their_rows, gain_ref, rest_ref, rows_ref
    )
    index = here()
    width = theirs_ref.shape[2]
    for p in range(blocks // 2):
        for odd, ref in enumerate((part_ref, rest_ref)):
            lanes = pl.ds(pl.multiple_of((index[0] ^ (2 * p + odd)) * width, width), width)
            whole_ref[:, lanes] = ref[:, p * width : (p + 1) * width]
    size = own_ref.shape[0]
    own_ref[...] = whole_ref[pl.ds(pl.multiple_of(index[1] * size, size), size), :]
    factor = lax.rsqrt(square / (blocks * width) + EPS)
    for start, size in cuts:
        at = slice(start, start + size)
        gate = factor * (
            gate_ref[:, at] + products(blocks, 1, width, rows_ref, in_ref, 0, start, size)
        )
        upper = factor * (
            upper_ref[:, at] + products(blocks, 1, width, rows_ref, in_ref, 1, start, size)
        )
        act_ref[:, at] = (gate / (1.0 + jnp.exp(-gate)) * upper).astype(BF16)
    half = near_ref.shape[0]
    pieces = mine_tail_ref.shape[0]
    count = half // pieces
    tail = jnp.concatenate(
        [ref[p, :count, tail_at:] for ref in (mine_tail_ref, theirs_tail_ref) for p in range(pieces)],
        axis=0,
    )
    tail = tail.astype(F32)
    lane = lax.broadcasted_iota(jnp.int32, tail.shape, 1) - first_lane
    slot = lax.div(index[0] * lax.axis_size("span") + index[1], 2)
    scale = jnp.sum(
        jnp.where((lane == slot) | (lane == slot + experts), tail, 0.0), axis=1, keepdims=True
    )
    wide = out_weight_ref.shape[1] // columns
    for n in range(columns):
        span = slice(n * wide, (n + 1) * wide)
        done = nn(act_ref[...], out_weight_ref[:, span])
        done = jnp.where(scale > 0, done * scale, 0.0).astype(BF16)
        near_ref[:, span] = done[:half]
        far_ref[:, span] = done[half:]


def level_kernel(near_ref, back_ref, *outs):
    rows = outs[0].shape[0]
    for n, out in enumerate(outs):
        at = slice(n * rows, (n + 1) * rows)
        out[...] = (near_ref[at, :].astype(F32) + back_ref[at, :].astype(F32)).astype(out.dtype)


def rows_kernel(spans, *refs):
    parts, outs, buf = refs[: -spans - 1], refs[-spans - 1 : -1], refs[-1]
    index = here()[1]
    total = parts[0][...]
    for p in parts[1:]:
        total = total + p[...].astype(F32)
    buf[...] = total
    count = outs[0].shape[0]
    for k, out in enumerate(outs):
        at = pl.ds(pl.multiple_of((index ^ k) * count, count), count)
        out[...] = buf[at, :].astype(out.dtype)


def last_kernel(spans, *refs):
    parts = refs[:spans]
    own_ref, live_ref, out_ref = refs[spans:]
    count = out_ref.shape[0]
    routed = sum(p[...].astype(F32) for p in parts)
    at = pl.ds(pl.multiple_of(here()[1] * count, count), count)
    total = own_ref[...] + routed
    out_ref[...] = jnp.where(live_ref[at, :] > 0, total, 0.0).astype(BF16)


def per_device(
    raw_tokens,
    keep,
    attn_gain,
    query_weight,
    latent_weight,
    kv_gain,
    out_weight,
    moe_gain,
    expert_ids,
    gate_values,
    expert_slot,
    expert_in,
    expert_out,
):
    kv_rank = kv_gain.shape[0]
    spans = lax.axis_size("span")
    contexts = lax.axis_size("context")
    part_width = latent_weight.shape[1]
    latent_width = part_width * spans
    rope = latent_width - kv_rank
    model = attn_gain.shape[0]
    kept = keep.shape[1]
    raw_rows = raw_tokens.shape[0]
    heads = query_weight.shape[1] // latent_width
    rows_dev = expert_ids.shape[0]
    experts = expert_slot.shape[0]
    hidden = expert_in.shape[3]
    evens = list(range(0, contexts, 2))

    picked = call(
        pick_kernel,
        shape((kept, raw_tokens.shape[1]), BF16),
        [HBM] * 2,
        (keep, raw_tokens),
        scratch=[
            pltpu.VMEM(keep.shape, jnp.int32),
            pltpu.VMEM(raw_tokens.shape, BF16),
            pltpu.SemaphoreType.DMA((2,)),
        ],
        limit=4,
    )
    parts = gathered(picked, "span", range(1, spans))

    sent_width = up(max(part_width, experts))
    moved = (latent_weight.T, attn_gain[None], kv_gain[None], moe_gain[None], query_weight)
    near_weight, gain, near_kv, near_moe, near_query, dense, cosine, sine, live = call(
        functools.partial(prepare_kernel, raw_rows),
        [shape(value.shape, value.dtype) for value in moved]
        + [
            shape((rows_dev, sent_width), F32),
            shape((kept, rope), F32),
            shape((kept, rope), F32),
            shape((kept, 1), F32),
        ],
        [HBM] * 9,
        (keep, expert_ids, gate_values, expert_slot, *moved),
        scratch=[
            pltpu.VMEM(keep.shape, jnp.int32),
            pltpu.VMEM(expert_ids.shape, jnp.int32),
            pltpu.VMEM(gate_values.shape, F32),
            pltpu.SMEM(expert_slot.shape, jnp.int32),
            pltpu.SemaphoreType.DMA((9,)),
        ],
        moved=2 * query_weight.size,
        limit=12,
    )

    compact, normed, sent = call(
        functools.partial(latent_kernel, spans),
        [
            shape((kept, model), BF16),
            shape((kept, model), BF16),
            shape((kept + rows_dev, sent_width), F32),
        ],
        [VM] * (spans + 3),
        (*parts, gain, near_weight, dense),
        flops=2 * kept * latent_weight.size,
        moved=2 * latent_weight.size,
        limit=4,
    )
    parts = gathered(sent, "span", range(1, spans))
    row_width = up(latent_width + 2 * experts + 1)
    query = call(
        functools.partial(query_kernel, heads),
        shape((heads * kept, row_width), BF16),
        [VM] * 4,
        (normed, near_query, cosine, sine),
        flops=2 * kept * query_weight.size,
        moved=2 * query_weight.size,
        limit=10,
    )
    cached, sent = call(
        functools.partial(cache_kernel, spans, part_width, experts),
        [shape((kept, latent_width), BF16), shape(((1 + heads) * kept, row_width), BF16)],
        [VM] * (spans + 5),
        (*parts, live, near_kv, cosine, sine, query),
        limit=4,
    )

    mine_keys = jnp.stack(gathered(sent, "context", evens[1:]))
    their_keys = partner(mine_keys, "context", 1)
    partial = call(
        functools.partial(attend_kernel, heads, kv_rank, latent_width + 2 * experts, contexts),
        shape((contexts * kept, out_weight.shape[1]), BF16),
        [VM, VM, HBM],
        (mine_keys, their_keys, out_weight),
        scratch=[pltpu.VMEM(out_weight.shape, BF16), pltpu.SemaphoreType.DMA],
        flops=2 * kept * contexts * out_weight.size,
        moved=2 * out_weight.size,
        limit=12,
    )

    column = call(
        sum_kernel,
        shape(partial.shape, BF16),
        [VM] * spans,
        gathered(partial, "span", range(1, spans)),
        limit=4,
    )
    mine_rows = jnp.stack(gathered(compact, "context", evens[1:]))
    their_rows = partner(mine_rows, "context", 1)

    mine = jnp.stack(gathered(column, "context", evens[1:]))
    theirs = partner(mine, "context", 1)
    half = mine.shape[0] * kept
    cuts, start = [], 0
    while start < hidden:
        size = min(2 * LANES, hidden - start)
        cuts.append((start, size))
        start += size
    weights_in = jnp.swapaxes(expert_in[0], 1, 2)
    begun = call(
        functools.partial(begin_kernel, contexts, cuts),
        [
            shape((kept, model // 2), F32),
            shape((2 * half, 1), F32),
            shape((2 * half, hidden), F32),
            shape((2 * half, hidden), F32),
        ],
        [VM] * 5,
        (mine, mine_rows, their_rows, near_moe, weights_in),
        scratch=[pltpu.VMEM((2 * half, model // 2), BF16)],
        flops=2 * 2 * half * hidden * model,
        moved=4 * hidden * model,
        limit=20,
    )
    near, far, own = call(
        functools.partial(
            expert_kernel, contexts, latent_width - kv_rank, kv_rank, experts, cuts, 4
        ),
        [shape((half, model), BF16), shape((half, model), BF16), shape((rows_dev, model), F32)],
        [VM] * 12,
        (
            theirs,
            mine_rows,
            their_rows,
            near_moe,
            weights_in,
            *begun,
            mine_keys,
            their_keys,
            expert_out[0],
        ),
        scratch=[
            pltpu.VMEM((2 * half, model // 2), BF16),
            pltpu.VMEM((2 * half, hidden), BF16),
            pltpu.VMEM((kept, model // 2), F32),
            pltpu.VMEM((kept, model), F32),
        ],
        flops=4 * 2 * half * hidden * model,
        moved=4 * hidden * model,
        limit=20,
    )

    levels = call(
        level_kernel,
        [shape((kept, model), F32)] + [shape((kept, model), BF16)] * (len(evens) - 1),
        [VM, VM],
        (near, partner(far, "context", 1)),
        limit=6,
    )
    got = [partner(level, "context", i) for level, i in zip(levels[1:], evens[1:])]
    rows = call(
        functools.partial(rows_kernel, spans),
        [shape((rows_dev, model), F32)] + [shape((rows_dev, model), BF16)] * (spans - 1),
        [VM] * len(levels),
        (levels[0], *got),
        scratch=[pltpu.VMEM((kept, model), F32)],
        limit=6,
    )
    got = []
    for k in range(1, spans):
        got.append(partner(rows[k], "span", k))
    layer_out = call(
        functools.partial(last_kernel, spans),
        shape((rows_dev, model), BF16),
        [VM] * (spans + 2),
        (rows[0], *got, own, live),
        limit=4,
    )
    return (layer_out, cached)


def solution(mesh):
    placed = (
        P(("groups", "context"), "span"),
        P(("groups", "context"), None),
        P(),
        P(None, "span"),
        P(None, "span"),
        P(),
        P("span", "context"),
        P(),
        P(("groups", "context", "span"), None),
        P(("groups", "context", "span"), None),
        P(),
        P(("context", "span"), None, None, None),
        P(("context", "span"), None, None),
    )
    return jax.shard_map(
        per_device,
        mesh=mesh,
        in_specs=placed,
        out_specs=(P(("groups", "context", "span"), None), P(("groups", "context"), None)),
        check_vma=False,
    )
```

```python
import functools
import math

import jax
import jax.numpy as jnp
from jax import lax
from jax.experimental import pallas as pl
from jax.experimental.pallas import tpu as pltpu
from jax.sharding import PartitionSpec as P


EPS = 1e-06
THETA = 50000.0
SCALE = 192.0 ** (-0.5)
NEGATIVE = -1e30
LANES = 128
F32 = jnp.float32
BF16 = jnp.bfloat16
MIB = 1 << 20


VM = pl.BlockSpec(memory_space=pltpu.VMEM)
HBM = pl.BlockSpec(memory_space=pltpu.HBM)
ANY = pl.BlockSpec(memory_space=pl.ANY)


def up(count, unit=LANES):
    return -(-count // unit) * unit


def shape(dims, dtype):
    return jax.ShapeDtypeStruct(tuple(dims), dtype)


def call(kernel, outs, in_specs, args, scratch=(), flops=0, moved=0, limit=16):
    single = not isinstance(outs, (list, tuple))
    args = [
        pltpu.with_memory_space_constraint(value, pltpu.HBM) if spec is HBM else value
        for spec, value in zip(in_specs, args)
    ]
    return pl.pallas_call(
        kernel,
        out_shape=outs,
        in_specs=in_specs,
        out_specs=VM if single else [VM] * len(outs),
        scratch_shapes=list(scratch),
        compiler_params=pltpu.CompilerParams(vmem_limit_bytes=limit * MIB),
        cost_estimate=pl.CostEstimate(flops=flops, bytes_accessed=moved, transcendentals=0),
    )(*args)


def nt(left, right):
    return lax.dot_general(left, right, (((1,), (1,)), ((), ())), preferred_element_type=F32)


def nn(left, right):
    return jnp.dot(left, right, preferred_element_type=F32)


def here():
    return lax.axis_index("context"), lax.axis_index("span")


def partner(values, axis, mask):
    count = lax.axis_size(axis)
    return lax.ppermute(values, axis, [(i, i ^ mask) for i in range(count)])


def gathered(values, axis, masks):
    parts = [values]
    for mask in masks:
        parts.append(partner(values, axis, mask))
    return parts


def natural(parts, index):
    bit = 1
    while bit < len(parts):
        swap = (index & bit) != 0
        parts = [jnp.where(swap, parts[k ^ bit], parts[k]) for k in range(len(parts))]
        bit *= 2
    return parts


def fetch(pairs, sem):
    copies = [pltpu.make_async_copy(a, b, sem.at[n]) for n, (a, b) in enumerate(pairs)]
    for copy in copies:
        copy.start()
    return copies


def pick_kernel(keep_hbm, raw_hbm, out_ref, keep_ref, raw_ref, sem):
    for copy in fetch([(keep_hbm, keep_ref), (raw_hbm, raw_ref)], sem):
        copy.wait()
    rows = lax.broadcasted_iota(jnp.int32, (raw_ref.shape[0], keep_ref.shape[1]), 0)
    hits = jnp.where(rows == keep_ref[...], 1.0, 0.0).astype(BF16)
    out_ref[...] = lax.dot_general(
        hits, raw_ref[...], (((0,), (0,)), ((), ())), preferred_element_type=F32
    ).astype(BF16)


def prepare_kernel(raw_rows, *refs):
    keep_hbm, ids_hbm, gates_hbm, slot_hbm = refs[:4]
    sources = refs[4:9]
    targets = refs[9:14]
    dense_ref, cos_ref, sin_ref, live_ref = refs[14:18]
    keep_ref, ids_ref, gates_ref, slot_ref, sem = refs[18:]
    small = [(keep_hbm, keep_ref), (ids_hbm, ids_ref), (gates_hbm, gates_ref), (slot_hbm, slot_ref)]
    copies = fetch(small + list(zip(sources, targets)), sem)
    for copy in copies[:4]:
        copy.wait()
    ids = ids_ref[...]
    slots = jnp.zeros_like(ids)
    for e in range(slot_ref.shape[0]):
        slots = jnp.where(ids == e, slot_ref[e], slots)
    lane = lax.broadcasted_iota(jnp.int32, dense_ref.shape, 1)
    gates = jnp.zeros(dense_ref.shape, F32)
    for t in range(ids.shape[1]):
        gates = gates + jnp.where(lane == slots[:, t : t + 1], gates_ref[:, t : t + 1], 0.0)
    dense_ref[...] = gates
    rows, rope = cos_ref.shape
    diagonal = lax.broadcasted_iota(jnp.int32, (rows, rows), 0) == lax.broadcasted_iota(
        jnp.int32, (rows, rows), 1
    )
    listing = jnp.sum(
        jnp.where(diagonal, keep_ref[...].astype(F32), 0.0), axis=1, keepdims=True
    )
    live_ref[...] = jnp.where(listing >= 0, 1.0, 0.0)
    positions = (here()[0] * raw_rows).astype(F32) + jnp.maximum(listing, 0.0)
    half = rope // 2
    lane = lax.broadcasted_iota(jnp.int32, (rows, rope), 1)
    first = lane < half
    place = jnp.where(first, lane, lane - half).astype(F32)
    angles = positions * jnp.exp(place * (-2.0 / rope * math.log(THETA)))
    cos_ref[...] = jnp.cos(angles)
    sine = jnp.sin(angles)
    sin_ref[...] = jnp.where(first, -sine, sine)
    for copy in copies[4:]:
        copy.wait()


def latent_kernel(spans, *refs):
    parts = refs[:spans]
    gain_ref, weight_ref, dense_ref, compact_ref, normed_ref, sent_ref = refs[spans:]
    index = here()[1]
    rows, block = parts[0].shape
    values = [p[...].astype(F32) for p in parts]
    square = sum(jnp.sum(v * v, axis=1, keepdims=True) for v in values)
    factor = lax.rsqrt(square / (spans * block) + EPS)
    for k in range(spans):
        at = pl.ds(pl.multiple_of((index ^ k) * block, block), block)
        compact_ref[:, at] = parts[k][...]
        normed_ref[:, at] = (values[k] * factor * gain_ref[:, at]).astype(BF16)
    sent_ref[0:rows, :] = jnp.zeros((rows, sent_ref.shape[1]), F32)
    sent_ref[0:rows, 0 : weight_ref.shape[0]] = nt(normed_ref[...], weight_ref[...])
    sent_ref[rows:, :] = dense_ref[...]


def rotated(values, cosine, sine):
    half = values.shape[1] // 2
    swapped = jnp.concatenate([values[:, half:], values[:, :half]], axis=1)
    return values * cosine + swapped * sine


def query_kernel(heads, normed_ref, weight_ref, cos_ref, sin_ref, out_ref):
    rows = normed_ref.shape[0]
    latent = weight_ref.shape[1] // heads
    total = nn(normed_ref[...], weight_ref[...])
    kv_rank = latent - cos_ref.shape[1]
    out_ref[...] = jnp.zeros(out_ref.shape, BF16)
    for h in range(heads):
        one = total[:, h * latent : (h + 1) * latent]
        out_ref[h * rows : (h + 1) * rows, 0:kv_rank] = one[:, :kv_rank].astype(BF16)
        out_ref[h * rows : (h + 1) * rows, kv_rank:latent] = rotated(
            one[:, kv_rank:], cos_ref[...], sin_ref[...]
        ).astype(BF16)


def cache_kernel(spans, width, experts, *refs):
    parts = refs[:spans]
    live_ref, gain_ref, cos_ref, sin_ref, query_ref, sent_ref = refs[spans:]
    rows = live_ref.shape[0]
    kv_rank = gain_ref.shape[1]
    values = natural([p[...] for p in parts], here()[1])
    latent = jnp.concatenate([v[:rows, :width] for v in values], axis=1)
    gates = jnp.concatenate([v[rows:, :experts] for v in values], axis=0)
    nope = latent[:, :kv_rank]
    factor = lax.rsqrt(jnp.mean(nope * nope, axis=1, keepdims=True) + EPS)
    nope = nope * factor * gain_ref[...]
    rope = rotated(latent[:, kv_rank:], cos_ref[...], sin_ref[...])
    high = gates.astype(BF16).astype(F32)
    used = rope.shape[1] + 2 * experts + 1
    tail = [rope, high, gates - high, live_ref[...]]
    rest = sent_ref.shape[1] - kv_rank - used
    if rest:
        tail.append(jnp.zeros((rows, rest), F32))
    sent_ref[:rows, :kv_rank] = nope.astype(BF16)
    sent_ref[:rows, kv_rank:] = jnp.concatenate(tail, axis=1).astype(BF16)
    sent_ref[rows:, :] = query_ref[...]


def emit_kernel(sent_ref, out_ref):
    out_ref[...] = sent_ref[: out_ref.shape[0], : out_ref.shape[1]]


def attend_kernel(
    heads, kv_rank, flag_lane, mine_ref, theirs_ref, weight_hbm, other_hbm, out_ref, buf, sem
):
    copies = fetch([(weight_hbm, buf.at[0]), (other_hbm, buf.at[1])], sem)
    pieces = mine_ref.shape[0]
    count = theirs_ref.shape[1]
    index = here()[0]

    def gather(ref, n):
        return [ref[p, n * count : (n + 1) * count, :] for p in range(pieces)]

    keys = jnp.concatenate(gather(mine_ref, 0) + gather(theirs_ref, 0), axis=0)
    total, width = keys.shape
    lane = lax.broadcasted_iota(jnp.int32, (8, width), 1)
    flags = nt(jnp.where(lane == flag_lane, 1.0, 0.0).astype(BF16), keys)[0:1, :]

    def slot(dims, axis):
        line = lax.broadcasted_iota(jnp.int32, dims, axis)
        at = line // count
        which = jnp.where(at < pieces, 2 * at, 2 * (at - pieces) + 1)
        return (which ^ index) * count + line % count

    allowed = (slot((1, total), 1) <= slot((pieces * count, 1), 0)) & (flags > 0)
    results = [0.0, 0.0]
    for h in range(heads):
        scores = nt(jnp.concatenate(gather(mine_ref, 1 + h), axis=0), keys) * SCALE
        scores = jnp.where(allowed, scores, NEGATIVE)
        highest = jnp.max(scores, axis=1, keepdims=True)
        weight = jnp.where(allowed, jnp.exp(scores - highest), 0.0)
        denominator = jnp.sum(weight, axis=1, keepdims=True)
        summed = nn(weight.astype(BF16), keys[:, :kv_rank])
        mixed = (summed / denominator).astype(BF16)
        for n in range(2):
            if h == 0:
                copies[n].wait()
            results[n] = results[n] + nn(mixed, buf[n, h * kv_rank : (h + 1) * kv_rank, :])
    block = buf.shape[2]
    for n in range(2):
        lanes = pl.ds(pl.multiple_of(((index ^ n) & 1) * block, block), block)
        out_ref[:, lanes] = results[n].astype(BF16)


def sum_kernel(*refs):
    refs[-1][...] = sum(ref[...].astype(F32) for ref in refs[:-1]).astype(BF16)


def resid_kernel(pieces_ref, rows_ref, gain_ref, out_ref, own_ref, buf):
    pieces, count = rows_ref.shape[:2]
    width = pieces_ref.shape[2]
    index = here()
    for p in range(pieces):
        place = lax.div(index[0] ^ (2 * p), 2)
        lanes = pl.ds(pl.multiple_of(place * width, width), width)
        for at in range(pieces):
            to = p ^ at
            buf[to * count : (to + 1) * count, lanes] = rows_ref[to, :, lanes].astype(
                F32
            ) + pieces_ref[p, at * count : (at + 1) * count, :].astype(F32)
    for n in range(pieces):
        at = slice(n * count, (n + 1) * count)
        resid = buf[at, :]
        factor = lax.rsqrt(jnp.mean(resid * resid, axis=1, keepdims=True) + EPS)
        out_ref[at, :] = (resid * factor * gain_ref[...]).astype(BF16)
    size = own_ref.shape[0]
    own_ref[...] = buf[pl.ds(pl.multiple_of(index[1] * size, size), size), :]


def expert_kernel(
    first_lane,
    tail_at,
    experts,
    cuts,
    columns,
    rows_ref,
    tail_ref,
    in_ref,
    out_weight_ref,
    out_ref,
    act_ref,
):
    rows = rows_ref[...]
    pieces = tail_ref.shape[0]
    count = rows.shape[0] // pieces
    tail = jnp.concatenate([tail_ref[p, :count, tail_at:] for p in range(pieces)], axis=0)
    tail = tail.astype(F32)
    lane = lax.broadcasted_iota(jnp.int32, tail.shape, 1) - first_lane
    index = here()
    slot = lax.div(index[0] * lax.axis_size("span") + index[1], 2)
    scale = jnp.sum(
        jnp.where((lane == slot) | (lane == slot + experts), tail, 0.0), axis=1, keepdims=True
    )
    for start, size in cuts:
        gate = nt(rows, in_ref[0, start : start + size, :])
        upper = nt(rows, in_ref[1, start : start + size, :])
        act_ref[:, start : start + size] = (gate / (1.0 + jnp.exp(-gate)) * upper).astype(BF16)
    wide = out_weight_ref.shape[1] // columns
    for n in range(columns):
        span = slice(n * wide, (n + 1) * wide)
        done = nn(act_ref[...], out_weight_ref[:, span])
        out_ref[:, span] = jnp.where(scale > 0, done * scale, 0.0).astype(BF16)


def level_kernel(near_ref, back_ref, *outs):
    rows = outs[0].shape[0]
    for n, out in enumerate(outs):
        at = slice(n * rows, (n + 1) * rows)
        out[...] = (near_ref[at, :].astype(F32) + back_ref[at, :].astype(F32)).astype(out.dtype)


def rows_kernel(spans, *refs):
    parts, outs, buf = refs[: -spans - 1], refs[-spans - 1 : -1], refs[-1]
    index = here()[1]
    total = parts[0][...]
    for p in parts[1:]:
        total = total + p[...].astype(F32)
    buf[...] = total
    count = outs[0].shape[0]
    for k, out in enumerate(outs):
        at = pl.ds(pl.multiple_of((index ^ k) * count, count), count)
        out[...] = buf[at, :].astype(out.dtype)


def last_kernel(spans, *refs):
    parts = refs[:spans]
    own_ref, live_ref, out_ref = refs[spans:]
    count = out_ref.shape[0]
    routed = sum(p[...].astype(F32) for p in parts)
    at = pl.ds(pl.multiple_of(here()[1] * count, count), count)
    total = own_ref[...] + routed
    out_ref[...] = jnp.where(live_ref[at, :] > 0, total, 0.0).astype(BF16)


def per_device(
    raw_tokens,
    keep,
    attn_gain,
    query_weight,
    latent_weight,
    kv_gain,
    out_weight,
    moe_gain,
    expert_ids,
    gate_values,
    expert_slot,
    expert_in,
    expert_out,
):
    kv_rank = kv_gain.shape[0]
    spans = lax.axis_size("span")
    contexts = lax.axis_size("context")
    part_width = latent_weight.shape[1]
    latent_width = part_width * spans
    rope = latent_width - kv_rank
    model = attn_gain.shape[0]
    kept = keep.shape[1]
    raw_rows = raw_tokens.shape[0]
    heads = query_weight.shape[1] // latent_width
    rows_dev = expert_ids.shape[0]
    experts = expert_slot.shape[0]
    hidden = expert_in.shape[3]
    evens = list(range(0, contexts, 2))

    picked = call(
        pick_kernel,
        shape((kept, raw_tokens.shape[1]), BF16),
        [HBM] * 2,
        (keep, raw_tokens),
        scratch=[
            pltpu.VMEM(keep.shape, jnp.int32),
            pltpu.VMEM(raw_tokens.shape, BF16),
            pltpu.SemaphoreType.DMA((2,)),
        ],
        limit=4,
    )
    parts = gathered(picked, "span", range(1, spans))
    other_weight = partner(out_weight, "context", 1)

    sent_width = up(max(part_width, experts))
    moved = (latent_weight.T, attn_gain[None], kv_gain[None], moe_gain[None], query_weight)
    near_weight, gain, near_kv, near_moe, near_query, dense, cosine, sine, live = call(
        functools.partial(prepare_kernel, raw_rows),
        [shape(value.shape, value.dtype) for value in moved]
        + [
            shape((rows_dev, sent_width), F32),
            shape((kept, rope), F32),
            shape((kept, rope), F32),
            shape((kept, 1), F32),
        ],
        [HBM] * 9,
        (keep, expert_ids, gate_values, expert_slot, *moved),
        scratch=[
            pltpu.VMEM(keep.shape, jnp.int32),
            pltpu.VMEM(expert_ids.shape, jnp.int32),
            pltpu.VMEM(gate_values.shape, F32),
            pltpu.SMEM(expert_slot.shape, jnp.int32),
            pltpu.SemaphoreType.DMA((9,)),
        ],
        moved=2 * query_weight.size,
        limit=12,
    )

    compact, normed, sent = call(
        functools.partial(latent_kernel, spans),
        [
            shape((kept, model), BF16),
            shape((kept, model), BF16),
            shape((kept + rows_dev, sent_width), F32),
        ],
        [VM] * (spans + 3),
        (*parts, gain, near_weight, dense),
        flops=2 * kept * latent_weight.size,
        moved=2 * latent_weight.size,
        limit=4,
    )
    parts = gathered(sent, "span", range(1, spans))
    row_width = up(latent_width + 2 * experts + 1)
    query = call(
        functools.partial(query_kernel, heads),
        shape((heads * kept, row_width), BF16),
        [VM] * 4,
        (normed, near_query, cosine, sine),
        flops=2 * kept * query_weight.size,
        moved=2 * query_weight.size,
        limit=10,
    )
    sent = call(
        functools.partial(cache_kernel, spans, part_width, experts),
        shape(((1 + heads) * kept, row_width), BF16),
        [VM] * (spans + 5),
        (*parts, live, near_kv, cosine, sine, query),
        limit=4,
    )
    cached = call(emit_kernel, shape((kept, latent_width), BF16), [VM], (sent,), limit=4)

    mine_keys = gathered(sent, "context", evens[1:])
    their_keys = partner(jnp.stack([part[:kept] for part in mine_keys]), "context", 1)
    mine_keys = jnp.stack(mine_keys)
    half = mine_keys.shape[0] * kept
    partial = call(
        functools.partial(attend_kernel, heads, kv_rank, latent_width + 2 * experts),
        shape((half, 2 * out_weight.shape[1]), BF16),
        [VM, VM, HBM, ANY],
        (mine_keys, their_keys, out_weight, other_weight),
        scratch=[pltpu.VMEM((2, *out_weight.shape), BF16), pltpu.SemaphoreType.DMA((2,))],
        flops=2 * kept * contexts * out_weight.size,
        moved=4 * out_weight.size,
        limit=12,
    )

    column = call(
        sum_kernel,
        shape(partial.shape, BF16),
        [VM] * spans,
        gathered(partial, "span", range(1, spans)),
        limit=4,
    )
    mine_rows = jnp.stack(gathered(compact, "context", evens[1:]))

    pieces = jnp.stack(gathered(column, "context", evens[1:]))
    moe_in, own = call(
        resid_kernel,
        [shape((half, model), BF16), shape((rows_dev, model), F32)],
        [VM] * 3,
        (pieces, mine_rows, near_moe),
        scratch=[pltpu.VMEM((half, model), F32)],
        limit=8,
    )
    theirs = partner(moe_in, "context", 1)
    cuts, start = [], 0
    while start < hidden:
        size = min(2 * LANES, hidden - start)
        cuts.append((start, size))
        start += size
    weights_in = jnp.swapaxes(expert_in[0], 1, 2)
    near, far = [
        call(
            functools.partial(
                expert_kernel, latent_width - kv_rank, kv_rank, experts, cuts, 4
            ),
            shape((half, model), BF16),
            [VM] * 4,
            (rows, tails, weights_in, expert_out[0]),
            scratch=[pltpu.VMEM((half, hidden), BF16)],
            flops=6 * half * hidden * model,
            moved=6 * hidden * model,
            limit=12,
        )
        for rows, tails in ((moe_in, mine_keys), (theirs, their_keys))
    ]

    levels = call(
        level_kernel,
        [shape((kept, model), F32)] + [shape((kept, model), BF16)] * (len(evens) - 1),
        [VM, VM],
        (near, partner(far, "context", 1)),
        limit=6,
    )
    got = [partner(level, "context", i) for level, i in zip(levels[1:], evens[1:])]
    rows = call(
        functools.partial(rows_kernel, spans),
        [shape((rows_dev, model), F32)] + [shape((rows_dev, model), BF16)] * (spans - 1),
        [VM] * len(levels),
        (levels[0], *got),
        scratch=[pltpu.VMEM((kept, model), F32)],
        limit=6,
    )
    got = []
    for k in range(1, spans):
        got.append(partner(rows[k], "span", k))
    layer_out = call(
        functools.partial(last_kernel, spans),
        shape((rows_dev, model), BF16),
        [VM] * (spans + 2),
        (rows[0], *got, own, live),
        limit=4,
    )
    return (layer_out, cached)


def solution(mesh):
    placed = (
        P(("groups", "context"), "span"),
        P(("groups", "context"), None),
        P(),
        P(None, "span"),
        P(None, "span"),
        P(),
        P("span", "context"),
        P(),
        P(("groups", "context", "span"), None),
        P(("groups", "context", "span"), None),
        P(),
        P(("context", "span"), None, None, None),
        P(("context", "span"), None, None),
    )
    return jax.shard_map(
        per_device,
        mesh=mesh,
        in_specs=placed,
        out_specs=(P(("groups", "context", "span"), None), P(("groups", "context"), None)),
        check_vma=False,
    )
```

```python
import functools
import math

import jax
import jax.numpy as jnp
from jax import lax
from jax.experimental import pallas as pl
from jax.experimental.pallas import tpu as pltpu
from jax.sharding import PartitionSpec as P


EPS = 1e-06
THETA = 50000.0
SCALE = 192.0 ** (-0.5)
NEGATIVE = -1e30
LANES = 128
EARLY = 4
F32 = jnp.float32
BF16 = jnp.bfloat16
MIB = 1 << 20


VM = pl.BlockSpec(memory_space=pltpu.VMEM)
HBM = pl.BlockSpec(memory_space=pltpu.HBM)


def up(count, unit=LANES):
    return -(-count // unit) * unit


def shape(dims, dtype):
    return jax.ShapeDtypeStruct(tuple(dims), dtype)


def call(kernel, outs, in_specs, args, scratch=(), flops=0, moved=0, limit=16):
    single = not isinstance(outs, (list, tuple))
    args = [
        pltpu.with_memory_space_constraint(value, pltpu.HBM) if spec is HBM else value
        for spec, value in zip(in_specs, args)
    ]
    return pl.pallas_call(
        kernel,
        out_shape=outs,
        in_specs=in_specs,
        out_specs=VM if single else [VM] * len(outs),
        scratch_shapes=list(scratch),
        compiler_params=pltpu.CompilerParams(vmem_limit_bytes=limit * MIB),
        cost_estimate=pl.CostEstimate(flops=flops, bytes_accessed=moved, transcendentals=0),
    )(*args)


def nt(left, right):
    return lax.dot_general(left, right, (((1,), (1,)), ((), ())), preferred_element_type=F32)


def nn(left, right):
    return jnp.dot(left, right, preferred_element_type=F32)


def here():
    return lax.axis_index("context"), lax.axis_index("span")


def partner(values, axis, mask):
    count = lax.axis_size(axis)
    return lax.ppermute(values, axis, [(i, i ^ mask) for i in range(count)])


def gathered(values, axis, masks):
    parts = [values]
    for mask in masks:
        parts.append(partner(values, axis, mask))
    return parts


def natural(parts, index):
    bit = 1
    while bit < len(parts):
        swap = (index & bit) != 0
        parts = [jnp.where(swap, parts[k ^ bit], parts[k]) for k in range(len(parts))]
        bit *= 2
    return parts


def fetch(pairs, sem):
    copies = [pltpu.make_async_copy(a, b, sem.at[n]) for n, (a, b) in enumerate(pairs)]
    for copy in copies:
        copy.start()
    return copies


def pick_kernel(keep_hbm, raw_hbm, out_ref, keep_ref, raw_ref, sem):
    for copy in fetch([(keep_hbm, keep_ref), (raw_hbm, raw_ref)], sem):
        copy.wait()
    rows = lax.broadcasted_iota(jnp.int32, (raw_ref.shape[0], keep_ref.shape[1]), 0)
    hits = jnp.where(rows == keep_ref[...], 1.0, 0.0).astype(BF16)
    out_ref[...] = lax.dot_general(
        hits, raw_ref[...], (((0,), (0,)), ((), ())), preferred_element_type=F32
    ).astype(BF16)


def prepare_kernel(
    ids_hbm,
    gates_hbm,
    slot_hbm,
    weight_hbm,
    gain_hbm,
    query_hbm,
    weight_ref,
    gain_ref,
    query_ref,
    dense_ref,
    ids_ref,
    gates_ref,
    slot_ref,
    sem,
):
    early = query_hbm.at[pl.ds(0, query_ref.shape[0]), :]
    small = [(ids_hbm, ids_ref), (gates_hbm, gates_ref), (slot_hbm, slot_ref)]
    large = [(weight_hbm, weight_ref), (gain_hbm, gain_ref), (early, query_ref)]
    copies = fetch(small + large, sem)
    for copy in copies[:3]:
        copy.wait()
    ids = ids_ref[...]
    slots = jnp.zeros_like(ids)
    for e in range(slot_ref.shape[0]):
        slots = jnp.where(ids == e, slot_ref[e], slots)
    lane = lax.broadcasted_iota(jnp.int32, dense_ref.shape, 1)
    gates = jnp.zeros(dense_ref.shape, F32)
    for t in range(ids.shape[1]):
        gates = gates + jnp.where(lane == slots[:, t : t + 1], gates_ref[:, t : t + 1], 0.0)
    dense_ref[...] = gates
    for copy in copies[3:]:
        copy.wait()


def latent_kernel(spans, *refs):
    parts = refs[:spans]
    gain_ref, weight_ref, dense_ref, compact_ref, normed_ref, sent_ref = refs[spans:]
    index = here()[1]
    rows, block = parts[0].shape
    values = [p[...].astype(F32) for p in parts]
    square = sum(jnp.sum(v * v, axis=1, keepdims=True) for v in values)
    factor = lax.rsqrt(square / (spans * block) + EPS)
    for k in range(spans):
        at = pl.ds(pl.multiple_of((index ^ k) * block, block), block)
        compact_ref[:, at] = parts[k][...]
        normed_ref[:, at] = (values[k] * factor * gain_ref[:, at]).astype(BF16)
    sent_ref[0:rows, :] = jnp.zeros((rows, sent_ref.shape[1]), F32)
    sent_ref[0:rows, 0 : weight_ref.shape[0]] = nt(normed_ref[...], weight_ref[...])
    sent_ref[rows:, :] = dense_ref[...]


def rotated(values, cosine, sine):
    half = values.shape[1] // 2
    swapped = jnp.concatenate([values[:, half:], values[:, :half]], axis=1)
    return values * cosine + swapped * sine


def query_kernel(
    heads,
    raw_rows,
    normed_ref,
    early_ref,
    weight_hbm,
    keep_hbm,
    kv_hbm,
    moe_hbm,
    out_ref,
    cos_ref,
    sin_ref,
    live_ref,
    kv_ref,
    moe_ref,
    buf,
    keep_ref,
    sem,
):
    begun = early_ref.shape[0]
    steps, deep = buf.shape[:2]
    small = [(keep_hbm, keep_ref), (kv_hbm, kv_ref), (moe_hbm, moe_ref)]
    late = [(weight_hbm.at[pl.ds(begun + n * deep, deep), :], buf.at[n]) for n in range(steps)]
    copies = fetch(small + late, sem)
    copies[0].wait()
    rows, rope = cos_ref.shape
    diagonal = lax.broadcasted_iota(jnp.int32, (rows, rows), 0) == lax.broadcasted_iota(
        jnp.int32, (rows, rows), 1
    )
    listing = jnp.sum(
        jnp.where(diagonal, keep_ref[...].astype(F32), 0.0), axis=1, keepdims=True
    )
    live_ref[...] = jnp.where(listing >= 0, 1.0, 0.0)
    positions = (here()[0] * raw_rows).astype(F32) + jnp.maximum(listing, 0.0)
    half = rope // 2
    lane = lax.broadcasted_iota(jnp.int32, (rows, rope), 1)
    first = lane < half
    place = jnp.where(first, lane, lane - half).astype(F32)
    angles = positions * jnp.exp(place * (-2.0 / rope * math.log(THETA)))
    cos_ref[...] = jnp.cos(angles)
    sine = jnp.sin(angles)
    sin_ref[...] = jnp.where(first, -sine, sine)
    latent = early_ref.shape[1] // heads
    total = nn(normed_ref[:, :begun], early_ref[...])
    for n in range(steps):
        copies[3 + n].wait()
        at = begun + n * deep
        total = total + nn(normed_ref[:, at : at + deep], buf[n])
    kv_rank = latent - rope
    out_ref[...] = jnp.zeros(out_ref.shape, BF16)
    for h in range(heads):
        one = total[:, h * latent : (h + 1) * latent]
        out_ref[h * rows : (h + 1) * rows, 0:kv_rank] = one[:, :kv_rank].astype(BF16)
        out_ref[h * rows : (h + 1) * rows, kv_rank:latent] = rotated(
            one[:, kv_rank:], cos_ref[...], sin_ref[...]
        ).astype(BF16)
    for copy in copies[1:3]:
        copy.wait()


def cache_kernel(spans, width, experts, *refs):
    parts = refs[:spans]
    live_ref, gain_ref, cos_ref, sin_ref, query_ref, sent_ref = refs[spans:]
    rows = live_ref.shape[0]
    kv_rank = gain_ref.shape[1]
    values = natural([p[...] for p in parts], here()[1])
    latent = jnp.concatenate([v[:rows, :width] for v in values], axis=1)
    gates = jnp.concatenate([v[rows:, :experts] for v in values], axis=0)
    nope = latent[:, :kv_rank]
    factor = lax.rsqrt(jnp.mean(nope * nope, axis=1, keepdims=True) + EPS)
    nope = nope * factor * gain_ref[...]
    rope = rotated(latent[:, kv_rank:], cos_ref[...], sin_ref[...])
    high = gates.astype(BF16).astype(F32)
    used = rope.shape[1] + 2 * experts + 1
    tail = [rope, high, gates - high, live_ref[...]]
    rest = sent_ref.shape[1] - kv_rank - used
    if rest:
        tail.append(jnp.zeros((rows, rest), F32))
    sent_ref[:rows, :kv_rank] = nope.astype(BF16)
    sent_ref[:rows, kv_rank:] = jnp.concatenate(tail, axis=1).astype(BF16)
    sent_ref[rows:, :] = query_ref[...]


def emit_kernel(sent_ref, out_ref):
    out_ref[...] = sent_ref[: out_ref.shape[0], : out_ref.shape[1]]


def places(blocks):
    return list(range(0, blocks, 2)) + list(range(1, blocks, 2))


def attend_kernel(
    heads, kv_rank, flag_lane, blocks, mine_ref, theirs_ref, weight_hbm, out_ref, weight_ref, sem
):
    copy = pltpu.make_async_copy(weight_hbm, weight_ref, sem)
    copy.start()
    count = mine_ref.shape[1] // (1 + heads)
    index = here()[0]
    half = blocks // 2
    pieces = [(mine_ref, n) for n in range(half)] + [(theirs_ref, n) for n in range(half)]

    def gather(n):
        return jnp.concatenate(
            [ref[p, n * count : (n + 1) * count, :] for ref, p in pieces], axis=0
        )

    keys = gather(0)
    total, width = keys.shape
    lane = lax.broadcasted_iota(jnp.int32, (8, width), 1)
    flags = nt(jnp.where(lane == flag_lane, 1.0, 0.0).astype(BF16), keys)[0:1, :]

    def slot(dims, axis):
        line = lax.broadcasted_iota(jnp.int32, dims, axis)
        at = line // count
        which = jnp.where(at < half, 2 * at, 2 * (at - half) + 1)
        return (which ^ index) * count + line % count

    allowed = (slot((1, total), 1) <= slot((total, 1), 0)) & (flags > 0)
    result = jnp.zeros(out_ref.shape, F32)
    for h in range(heads):
        scores = nt(gather(1 + h), keys) * SCALE
        scores = jnp.where(allowed, scores, NEGATIVE)
        highest = jnp.max(scores, axis=1, keepdims=True)
        weight = jnp.where(allowed, jnp.exp(scores - highest), 0.0)
        denominator = jnp.sum(weight, axis=1, keepdims=True)
        summed = nn(weight.astype(BF16), keys[:, :kv_rank])
        mixed = (summed / denominator).astype(BF16)
        if h == 0:
            copy.wait()
        result = result + nn(mixed, weight_ref[h * kv_rank : (h + 1) * kv_rank, :])
    out_ref[...] = result.astype(BF16)


def sum_kernel(*refs):
    refs[-1][...] = sum(ref[...].astype(F32) for ref in refs[:-1]).astype(BF16)


def scaled_rows(blocks, odd, pieces_ref, mine_rows, their_rows, gain_ref, part_ref, rows_ref):
    order = places(blocks)
    half = blocks // 2
    index = here()[0]
    count, width = mine_rows.shape[1], pieces_ref.shape[2]
    squares = [jnp.zeros((count, 1), F32)] * blocks
    for p in range(half):
        i = 2 * p + odd
        lanes = pl.ds(pl.multiple_of((index ^ i) * width, width), width)
        gain = gain_ref[:, lanes]
        for at, j in enumerate(order):
            to = order.index(i ^ j)
            rows = mine_rows if to < half else their_rows
            resid = rows[to % half, :, lanes].astype(F32) + pieces_ref[
                p, at * count : (at + 1) * count, :
            ].astype(F32)
            squares[to] = squares[to] + jnp.sum(resid * resid, axis=1, keepdims=True)
            rows_ref[to * count : (to + 1) * count, p * width : (p + 1) * width] = (
                resid * gain
            ).astype(BF16)
            if to == 0:
                part_ref[:, p * width : (p + 1) * width] = resid
    return jnp.concatenate(squares, axis=0)


def products(blocks, odd, width, rows_ref, in_ref, half, start, size):
    index = here()[0]
    total = jnp.zeros((rows_ref.shape[0], size), F32)
    for p in range(blocks // 2):
        lanes = pl.ds(pl.multiple_of((index ^ (2 * p + odd)) * width, width), width)
        total = total + nt(
            rows_ref[:, p * width : (p + 1) * width], in_ref[half, start : start + size, lanes]
        )
    return total


def begin_kernel(
    blocks,
    cuts,
    mine_ref,
    mine_rows,
    their_rows,
    gain_ref,
    in_ref,
    part_ref,
    square_ref,
    gate_ref,
    upper_ref,
    rows_ref,
):
    square_ref[...] = scaled_rows(
        blocks, 0, mine_ref, mine_rows, their_rows, gain_ref, part_ref, rows_ref
    )
    width = mine_ref.shape[2]
    for start, size in cuts:
        at = slice(start, start + size)
        gate_ref[:, at] = products(blocks, 0, width, rows_ref, in_ref, 0, start, size)
        upper_ref[:, at] = products(blocks, 0, width, rows_ref, in_ref, 1, start, size)


def expert_kernel(
    blocks,
    first_lane,
    tail_at,
    experts,
    cuts,
    columns,
    theirs_ref,
    mine_rows,
    their_rows,
    gain_ref,
    in_ref,
    part_ref,
    square_ref,
    gate_ref,
    upper_ref,
    mine_tail_ref,
    theirs_tail_ref,
    out_weight_ref,
    near_ref,
    far_ref,
    own_ref,
    rows_ref,
    act_ref,
    rest_ref,
    whole_ref,
):
    square = square_ref[...] + scaled_rows(
        blocks, 1, theirs_ref, mine_rows, their_rows, gain_ref, rest_ref, rows_ref
    )
    index = here()
    width = theirs_ref.shape[2]
    for p in range(blocks // 2):
        for odd, ref in enumerate((part_ref, rest_ref)):
            lanes = pl.ds(pl.multiple_of((index[0] ^ (2 * p + odd)) * width, width), width)
            whole_ref[:, lanes] = ref[:, p * width : (p + 1) * width]
    size = own_ref.shape[0]
    own_ref[...] = whole_ref[pl.ds(pl.multiple_of(index[1] * size, size), size), :]
    factor = lax.rsqrt(square / (blocks * width) + EPS)
    for start, size in cuts:
        at = slice(start, start + size)
        gate = factor * (
            gate_ref[:, at] + products(blocks, 1, width, rows_ref, in_ref, 0, start, size)
        )
        upper = factor * (
            upper_ref[:, at] + products(blocks, 1, width, rows_ref, in_ref, 1, start, size)
        )
        act_ref[:, at] = (gate / (1.0 + jnp.exp(-gate)) * upper).astype(BF16)
    half = near_ref.shape[0]
    pieces = mine_tail_ref.shape[0]
    count = half // pieces
    tail = jnp.concatenate(
        [ref[p, :count, tail_at:] for ref in (mine_tail_ref, theirs_tail_ref) for p in range(pieces)],
        axis=0,
    )
    tail = tail.astype(F32)
    lane = lax.broadcasted_iota(jnp.int32, tail.shape, 1) - first_lane
    slot = lax.div(index[0] * lax.axis_size("span") + index[1], 2)
    scale = jnp.sum(
        jnp.where((lane == slot) | (lane == slot + experts), tail, 0.0), axis=1, keepdims=True
    )
    wide = out_weight_ref.shape[1] // columns
    for n in range(columns):
        span = slice(n * wide, (n + 1) * wide)
        done = nn(act_ref[...], out_weight_ref[:, span])
        done = jnp.where(scale > 0, done * scale, 0.0).astype(BF16)
        near_ref[:, span] = done[:half]
        far_ref[:, span] = done[half:]


def level_kernel(near_ref, back_ref, *outs):
    rows = outs[0].shape[0]
    for n, out in enumerate(outs):
        at = slice(n * rows, (n + 1) * rows)
        out[...] = (near_ref[at, :].astype(F32) + back_ref[at, :].astype(F32)).astype(out.dtype)


def rows_kernel(spans, *refs):
    parts, outs, buf = refs[: -spans - 1], refs[-spans - 1 : -1], refs[-1]
    index = here()[1]
    total = parts[0][...]
    for p in parts[1:]:
        total = total + p[...].astype(F32)
    buf[...] = total
    count = outs[0].shape[0]
    for k, out in enumerate(outs):
        at = pl.ds(pl.multiple_of((index ^ k) * count, count), count)
        out[...] = buf[at, :].astype(out.dtype)


def last_kernel(spans, *refs):
    parts = refs[:spans]
    own_ref, live_ref, out_ref = refs[spans:]
    count = out_ref.shape[0]
    routed = sum(p[...].astype(F32) for p in parts)
    at = pl.ds(pl.multiple_of(here()[1] * count, count), count)
    total = own_ref[...] + routed
    out_ref[...] = jnp.where(live_ref[at, :] > 0, total, 0.0).astype(BF16)


def per_device(
    raw_tokens,
    keep,
    attn_gain,
    query_weight,
    latent_weight,
    kv_gain,
    out_weight,
    moe_gain,
    expert_ids,
    gate_values,
    expert_slot,
    expert_in,
    expert_out,
):
    kv_rank = kv_gain.shape[0]
    spans = lax.axis_size("span")
    contexts = lax.axis_size("context")
    part_width = latent_weight.shape[1]
    latent_width = part_width * spans
    rope = latent_width - kv_rank
    model = attn_gain.shape[0]
    kept = keep.shape[1]
    raw_rows = raw_tokens.shape[0]
    heads = query_weight.shape[1] // latent_width
    rows_dev = expert_ids.shape[0]
    experts = expert_slot.shape[0]
    hidden = expert_in.shape[3]
    evens = list(range(0, contexts, 2))

    picked = call(
        pick_kernel,
        shape((kept, raw_tokens.shape[1]), BF16),
        [HBM] * 2,
        (keep, raw_tokens),
        scratch=[
            pltpu.VMEM(keep.shape, jnp.int32),
            pltpu.VMEM(raw_tokens.shape, BF16),
            pltpu.SemaphoreType.DMA((2,)),
        ],
        limit=4,
    )
    parts = gathered(picked, "span", range(1, spans))

    sent_width = up(max(part_width, experts))
    begun = model // EARLY
    near_weight, gain, early_query, dense = call(
        prepare_kernel,
        [
            shape((part_width, model), BF16),
            shape((1, model), F32),
            shape((begun, query_weight.shape[1]), BF16),
            shape((rows_dev, sent_width), F32),
        ],
        [HBM] * 6,
        (expert_ids, gate_values, expert_slot, latent_weight.T, attn_gain[None], query_weight),
        scratch=[
            pltpu.VMEM(expert_ids.shape, jnp.int32),
            pltpu.VMEM(gate_values.shape, F32),
            pltpu.SMEM(expert_slot.shape, jnp.int32),
            pltpu.SemaphoreType.DMA((6,)),
        ],
        moved=query_weight.size,
        limit=8,
    )

    compact, normed, sent = call(
        functools.partial(latent_kernel, spans),
        [
            shape((kept, model), BF16),
            shape((kept, model), BF16),
            shape((kept + rows_dev, sent_width), F32),
        ],
        [VM] * (spans + 3),
        (*parts, gain, near_weight, dense),
        flops=2 * kept * latent_weight.size,
        moved=2 * latent_weight.size,
        limit=4,
    )
    parts = gathered(sent, "span", range(1, spans))
    row_width = up(latent_width + 2 * experts + 1)
    steps = 3
    query, cosine, sine, live, near_kv, near_moe = call(
        functools.partial(query_kernel, heads, raw_rows),
        [
            shape((heads * kept, row_width), BF16),
            shape((kept, rope), F32),
            shape((kept, rope), F32),
            shape((kept, 1), F32),
            shape((1, kv_rank), F32),
            shape((1, model), F32),
        ],
        [VM, VM] + [HBM] * 4,
        (normed, early_query, query_weight, keep, kv_gain[None], moe_gain[None]),
        scratch=[
            pltpu.VMEM((steps, (model - begun) // steps, query_weight.shape[1]), BF16),
            pltpu.VMEM(keep.shape, jnp.int32),
            pltpu.SemaphoreType.DMA((steps + 3,)),
        ],
        flops=2 * kept * query_weight.size,
        moved=query_weight.size,
        limit=10,
    )
    sent = call(
        functools.partial(cache_kernel, spans, part_width, experts),
        shape(((1 + heads) * kept, row_width), BF16),
        [VM] * (spans + 5),
        (*parts, live, near_kv, cosine, sine, query),
        limit=4,
    )

    cached = call(emit_kernel, shape((kept, latent_width), BF16), [VM], (sent,), limit=4)

    mine_keys = jnp.stack(gathered(sent, "context", evens[1:]))
    their_keys = partner(mine_keys, "context", 1)
    partial = call(
        functools.partial(attend_kernel, heads, kv_rank, latent_width + 2 * experts, contexts),
        shape((contexts * kept, out_weight.shape[1]), BF16),
        [VM, VM, HBM],
        (mine_keys, their_keys, out_weight),
        scratch=[pltpu.VMEM(out_weight.shape, BF16), pltpu.SemaphoreType.DMA],
        flops=2 * kept * contexts * out_weight.size,
        moved=2 * out_weight.size,
        limit=12,
    )

    column = call(
        sum_kernel,
        shape(partial.shape, BF16),
        [VM] * spans,
        gathered(partial, "span", range(1, spans)),
        limit=4,
    )
    mine_rows = jnp.stack(gathered(compact, "context", evens[1:]))
    their_rows = partner(mine_rows, "context", 1)

    mine = jnp.stack(gathered(column, "context", evens[1:]))
    theirs = partner(mine, "context", 1)
    half = mine.shape[0] * kept
    cuts, start = [], 0
    while start < hidden:
        size = min(2 * LANES, hidden - start)
        cuts.append((start, size))
        start += size
    weights_in = jnp.swapaxes(expert_in[0], 1, 2)
    begun = call(
        functools.partial(begin_kernel, contexts, cuts),
        [
            shape((kept, model // 2), F32),
            shape((2 * half, 1), F32),
            shape((2 * half, hidden), F32),
            shape((2 * half, hidden), F32),
        ],
        [VM] * 5,
        (mine, mine_rows, their_rows, near_moe, weights_in),
        scratch=[pltpu.VMEM((2 * half, model // 2), BF16)],
        flops=2 * 2 * half * hidden * model,
        moved=4 * hidden * model,
        limit=20,
    )
    near, far, own = call(
        functools.partial(
            expert_kernel, contexts, latent_width - kv_rank, kv_rank, experts, cuts, 4
        ),
        [shape((half, model), BF16), shape((half, model), BF16), shape((rows_dev, model), F32)],
        [VM] * 12,
        (
            theirs,
            mine_rows,
            their_rows,
            near_moe,
            weights_in,
            *begun,
            mine_keys,
            their_keys,
            expert_out[0],
        ),
        scratch=[
            pltpu.VMEM((2 * half, model // 2), BF16),
            pltpu.VMEM((2 * half, hidden), BF16),
            pltpu.VMEM((kept, model // 2), F32),
            pltpu.VMEM((kept, model), F32),
        ],
        flops=4 * 2 * half * hidden * model,
        moved=4 * hidden * model,
        limit=20,
    )

    levels = call(
        level_kernel,
        [shape((kept, model), F32)] + [shape((kept, model), BF16)] * (len(evens) - 1),
        [VM, VM],
        (near, partner(far, "context", 1)),
        limit=6,
    )
    got = [partner(level, "context", i) for level, i in zip(levels[1:], evens[1:])]
    rows = call(
        functools.partial(rows_kernel, spans),
        [shape((rows_dev, model), F32)] + [shape((rows_dev, model), BF16)] * (spans - 1),
        [VM] * len(levels),
        (levels[0], *got),
        scratch=[pltpu.VMEM((kept, model), F32)],
        limit=6,
    )
    got = []
    for k in range(1, spans):
        got.append(partner(rows[k], "span", k))
    layer_out = call(
        functools.partial(last_kernel, spans),
        shape((rows_dev, model), BF16),
        [VM] * (spans + 2),
        (rows[0], *got, own, live),
        limit=4,
    )
    return (layer_out, cached)


def solution(mesh):
    placed = (
        P(("groups", "context"), "span"),
        P(("groups", "context"), None),
        P(),
        P(None, "span"),
        P(None, "span"),
        P(),
        P("span", "context"),
        P(),
        P(("groups", "context", "span"), None),
        P(("groups", "context", "span"), None),
        P(),
        P(("context", "span"), None, None, None),
        P(("context", "span"), None, None),
    )
    return jax.shard_map(
        per_device,
        mesh=mesh,
        in_specs=placed,
        out_specs=(P(("groups", "context", "span"), None), P(("groups", "context"), None)),
        check_vma=False,
    )
```

```python
import functools
import math

import jax
import jax.numpy as jnp
from jax import lax
from jax.experimental import pallas as pl
from jax.experimental.pallas import tpu as pltpu
from jax.sharding import PartitionSpec as P


EPS = 1e-06
THETA = 50000.0
SCALE = 192.0 ** (-0.5)
NEGATIVE = -1e30
LANES = 128
EARLY = 4
F32 = jnp.float32
BF16 = jnp.bfloat16
MIB = 1 << 20


VM = pl.BlockSpec(memory_space=pltpu.VMEM)
HBM = pl.BlockSpec(memory_space=pltpu.HBM)


def up(count, unit=LANES):
    return -(-count // unit) * unit


def shape(dims, dtype):
    return jax.ShapeDtypeStruct(tuple(dims), dtype)


def call(kernel, outs, in_specs, args, scratch=(), flops=0, moved=0, limit=16):
    single = not isinstance(outs, (list, tuple))
    args = [
        pltpu.with_memory_space_constraint(value, pltpu.HBM) if spec is HBM else value
        for spec, value in zip(in_specs, args)
    ]
    return pl.pallas_call(
        kernel,
        out_shape=outs,
        in_specs=in_specs,
        out_specs=VM if single else [VM] * len(outs),
        scratch_shapes=list(scratch),
        compiler_params=pltpu.CompilerParams(vmem_limit_bytes=limit * MIB),
        cost_estimate=pl.CostEstimate(flops=flops, bytes_accessed=moved, transcendentals=0),
    )(*args)


def nt(left, right):
    return lax.dot_general(left, right, (((1,), (1,)), ((), ())), preferred_element_type=F32)


def nn(left, right):
    return jnp.dot(left, right, preferred_element_type=F32)


def here():
    return lax.axis_index("context"), lax.axis_index("span")


def partner(values, axis, mask):
    count = lax.axis_size(axis)
    return lax.ppermute(values, axis, [(i, i ^ mask) for i in range(count)])


def gathered(values, axis, masks):
    parts = [values]
    for mask in masks:
        parts.append(partner(values, axis, mask))
    return parts


def natural(parts, index):
    bit = 1
    while bit < len(parts):
        swap = (index & bit) != 0
        parts = [jnp.where(swap, parts[k ^ bit], parts[k]) for k in range(len(parts))]
        bit *= 2
    return parts


def fetch(pairs, sem):
    copies = [pltpu.make_async_copy(a, b, sem.at[n]) for n, (a, b) in enumerate(pairs)]
    for copy in copies:
        copy.start()
    return copies


def pick_kernel(keep_hbm, raw_hbm, out_ref, keep_ref, raw_ref, sem):
    for copy in fetch([(keep_hbm, keep_ref), (raw_hbm, raw_ref)], sem):
        copy.wait()
    rows = lax.broadcasted_iota(jnp.int32, (raw_ref.shape[0], keep_ref.shape[1]), 0)
    hits = jnp.where(rows == keep_ref[...], 1.0, 0.0).astype(BF16)
    out_ref[...] = lax.dot_general(
        hits, raw_ref[...], (((0,), (0,)), ((), ())), preferred_element_type=F32
    ).astype(BF16)


def prepare_kernel(
    ids_hbm,
    gates_hbm,
    slot_hbm,
    weight_hbm,
    gain_hbm,
    query_hbm,
    weight_ref,
    gain_ref,
    query_ref,
    dense_ref,
    ids_ref,
    gates_ref,
    slot_ref,
    sem,
):
    early = query_hbm.at[pl.ds(0, query_ref.shape[0]), :]
    small = [(ids_hbm, ids_ref), (gates_hbm, gates_ref), (slot_hbm, slot_ref)]
    large = [(weight_hbm, weight_ref), (gain_hbm, gain_ref), (early, query_ref)]
    copies = fetch(small + large, sem)
    for copy in copies[:3]:
        copy.wait()
    ids = ids_ref[...]
    slots = jnp.zeros_like(ids)
    for e in range(slot_ref.shape[0]):
        slots = jnp.where(ids == e, slot_ref[e], slots)
    lane = lax.broadcasted_iota(jnp.int32, dense_ref.shape, 1)
    gates = jnp.zeros(dense_ref.shape, F32)
    for t in range(ids.shape[1]):
        gates = gates + jnp.where(lane == slots[:, t : t + 1], gates_ref[:, t : t + 1], 0.0)
    dense_ref[...] = gates
    for copy in copies[3:]:
        copy.wait()


def latent_kernel(spans, *refs):
    parts = refs[:spans]
    gain_ref, weight_ref, dense_ref, compact_ref, normed_ref, sent_ref = refs[spans:]
    index = here()[1]
    rows, block = parts[0].shape
    values = [p[...].astype(F32) for p in parts]
    square = sum(jnp.sum(v * v, axis=1, keepdims=True) for v in values)
    factor = lax.rsqrt(square / (spans * block) + EPS)
    for k in range(spans):
        at = pl.ds(pl.multiple_of((index ^ k) * block, block), block)
        compact_ref[:, at] = parts[k][...]
        normed_ref[:, at] = (values[k] * factor * gain_ref[:, at]).astype(BF16)
    sent_ref[0:rows, :] = jnp.zeros((rows, sent_ref.shape[1]), F32)
    sent_ref[0:rows, 0 : weight_ref.shape[0]] = nt(normed_ref[...], weight_ref[...])
    sent_ref[rows:, :] = dense_ref[...]


def rotated(values, cosine, sine):
    half = values.shape[1] // 2
    swapped = jnp.concatenate([values[:, half:], values[:, :half]], axis=1)
    return values * cosine + swapped * sine


def query_kernel(
    heads,
    raw_rows,
    normed_ref,
    early_ref,
    weight_hbm,
    keep_hbm,
    kv_hbm,
    moe_hbm,
    out_ref,
    cos_ref,
    sin_ref,
    live_ref,
    kv_ref,
    moe_ref,
    buf,
    keep_ref,
    sem,
):
    begun = early_ref.shape[0]
    steps, deep = buf.shape[:2]
    small = [(keep_hbm, keep_ref), (kv_hbm, kv_ref), (moe_hbm, moe_ref)]
    late = [(weight_hbm.at[pl.ds(begun + n * deep, deep), :], buf.at[n]) for n in range(steps)]
    copies = fetch(small + late, sem)
    copies[0].wait()
    rows, rope = cos_ref.shape
    diagonal = lax.broadcasted_iota(jnp.int32, (rows, rows), 0) == lax.broadcasted_iota(
        jnp.int32, (rows, rows), 1
    )
    listing = jnp.sum(
        jnp.where(diagonal, keep_ref[...].astype(F32), 0.0), axis=1, keepdims=True
    )
    live_ref[...] = jnp.where(listing >= 0, 1.0, 0.0)
    positions = (here()[0] * raw_rows).astype(F32) + jnp.maximum(listing, 0.0)
    half = rope // 2
    lane = lax.broadcasted_iota(jnp.int32, (rows, rope), 1)
    first = lane < half
    place = jnp.where(first, lane, lane - half).astype(F32)
    angles = positions * jnp.exp(place * (-2.0 / rope * math.log(THETA)))
    cos_ref[...] = jnp.cos(angles)
    sine = jnp.sin(angles)
    sin_ref[...] = jnp.where(first, -sine, sine)
    latent = early_ref.shape[1] // heads
    total = nn(normed_ref[:, :begun], early_ref[...])
    for n in range(steps):
        copies[3 + n].wait()
        at = begun + n * deep
        total = total + nn(normed_ref[:, at : at + deep], buf[n])
    kv_rank = latent - rope
    out_ref[...] = jnp.zeros(out_ref.shape, BF16)
    for h in range(heads):
        one = total[:, h * latent : (h + 1) * latent]
        out_ref[h * rows : (h + 1) * rows, 0:kv_rank] = one[:, :kv_rank].astype(BF16)
        out_ref[h * rows : (h + 1) * rows, kv_rank:latent] = rotated(
            one[:, kv_rank:], cos_ref[...], sin_ref[...]
        ).astype(BF16)
    for copy in copies[1:3]:
        copy.wait()


def cache_kernel(spans, width, experts, *refs):
    parts = refs[:spans]
    live_ref, gain_ref, cos_ref, sin_ref, query_ref, sent_ref = refs[spans:]
    rows = live_ref.shape[0]
    kv_rank = gain_ref.shape[1]
    values = natural([p[...] for p in parts], here()[1])
    latent = jnp.concatenate([v[:rows, :width] for v in values], axis=1)
    gates = jnp.concatenate([v[rows:, :experts] for v in values], axis=0)
    nope = latent[:, :kv_rank]
    factor = lax.rsqrt(jnp.mean(nope * nope, axis=1, keepdims=True) + EPS)
    nope = nope * factor * gain_ref[...]
    rope = rotated(latent[:, kv_rank:], cos_ref[...], sin_ref[...])
    high = gates.astype(BF16).astype(F32)
    used = rope.shape[1] + 2 * experts + 1
    tail = [rope, high, gates - high, live_ref[...]]
    rest = sent_ref.shape[1] - kv_rank - used
    if rest:
        tail.append(jnp.zeros((rows, rest), F32))
    sent_ref[:rows, :kv_rank] = nope.astype(BF16)
    sent_ref[:rows, kv_rank:] = jnp.concatenate(tail, axis=1).astype(BF16)
    sent_ref[rows:, :] = query_ref[...]


def emit_kernel(sent_ref, out_ref):
    out_ref[...] = sent_ref[: out_ref.shape[0], : out_ref.shape[1]]


def places(blocks):
    return list(range(0, blocks, 2)) + list(range(1, blocks, 2))


def attend_kernel(
    heads, kv_rank, flag_lane, blocks, mine_ref, theirs_ref, weight_hbm, out_ref, weight_ref, sem
):
    copy = pltpu.make_async_copy(weight_hbm, weight_ref, sem)
    copy.start()
    count = mine_ref.shape[1] // (1 + heads)
    index = here()[0]
    half = blocks // 2
    pieces = [(mine_ref, n) for n in range(half)] + [(theirs_ref, n) for n in range(half)]

    def gather(n):
        return [ref[p, n * count : (n + 1) * count, :] for ref, p in pieces]

    keys = jnp.concatenate(gather(0), axis=0)
    total, width = keys.shape
    lane = lax.broadcasted_iota(jnp.int32, (16, width), 1)
    flag_rows = jnp.where(lane == flag_lane, 1.0, 0.0).astype(BF16)
    queries = sum([gather(1 + h) for h in range(heads)], [])
    both = nt(jnp.concatenate(queries + [flag_rows], axis=0), keys)
    flags = both[heads * total : heads * total + 1, :]
    shift = count.bit_length() - 1

    def slot(dims, axis):
        line = lax.broadcasted_iota(jnp.int32, dims, axis)
        if count == 1 << shift:
            at, rest = line >> shift, line & (count - 1)
        else:
            at, rest = line // count, line % count
        which = jnp.where(at < half, 2 * at, 2 * (at - half) + 1)
        return (which ^ index) * count + rest

    allowed = (slot((1, total), 1) <= slot((total, 1), 0)) & (flags > 0)
    weights, shares = [], []
    for h in range(heads):
        scores = both[h * total : (h + 1) * total, :] * SCALE
        scores = jnp.where(allowed, scores, NEGATIVE)
        highest = jnp.max(scores, axis=1, keepdims=True)
        weight = jnp.where(allowed, jnp.exp(scores - highest), 0.0)
        shares.append(1.0 / jnp.sum(weight, axis=1, keepdims=True))
        weights.append(weight.astype(BF16))
    summed = nn(jnp.concatenate(weights, axis=0), keys[:, :kv_rank])
    copy.wait()
    result = jnp.zeros(out_ref.shape, F32)
    for h in range(heads):
        mixed = (summed[h * total : (h + 1) * total] * shares[h]).astype(BF16)
        result = result + nn(mixed, weight_ref[h * kv_rank : (h + 1) * kv_rank, :])
    out_ref[...] = result.astype(BF16)


def sum_kernel(*refs):
    refs[-1][...] = sum(ref[...].astype(F32) for ref in refs[:-1]).astype(BF16)


def scaled_rows(blocks, odd, pieces_ref, mine_rows, their_rows, gain_ref, part_ref, rows_ref):
    order = places(blocks)
    half = blocks // 2
    index = here()[0]
    count, width = mine_rows.shape[1], pieces_ref.shape[2]
    squares = [jnp.zeros((count, 1), F32)] * blocks
    for p in range(half):
        i = 2 * p + odd
        lanes = pl.ds(pl.multiple_of((index ^ i) * width, width), width)
        gain = gain_ref[:, lanes]
        for at, j in enumerate(order):
            to = order.index(i ^ j)
            rows = mine_rows if to < half else their_rows
            resid = rows[to % half, :, lanes].astype(F32) + pieces_ref[
                p, at * count : (at + 1) * count, :
            ].astype(F32)
            squares[to] = squares[to] + jnp.sum(resid * resid, axis=1, keepdims=True)
            rows_ref[to * count : (to + 1) * count, p * width : (p + 1) * width] = (
                resid * gain
            ).astype(BF16)
            if to == 0:
                part_ref[:, p * width : (p + 1) * width] = resid
    return jnp.concatenate(squares, axis=0)


def products(blocks, odd, width, rows_ref, in_ref, half, start, size):
    index = here()[0]
    total = jnp.zeros((rows_ref.shape[0], size), F32)
    for p in range(blocks // 2):
        lanes = pl.ds(pl.multiple_of((index ^ (2 * p + odd)) * width, width), width)
        total = total + nt(
            rows_ref[:, p * width : (p + 1) * width], in_ref[half, start : start + size, lanes]
        )
    return total


def begin_kernel(
    blocks,
    cuts,
    mine_ref,
    mine_rows,
    their_rows,
    gain_ref,
    in_ref,
    part_ref,
    square_ref,
    gate_ref,
    upper_ref,
    rows_ref,
):
    square_ref[...] = scaled_rows(
        blocks, 0, mine_ref, mine_rows, their_rows, gain_ref, part_ref, rows_ref
    )
    width = mine_ref.shape[2]
    for start, size in cuts:
        at = slice(start, start + size)
        gate_ref[:, at] = products(blocks, 0, width, rows_ref, in_ref, 0, start, size)
        upper_ref[:, at] = products(blocks, 0, width, rows_ref, in_ref, 1, start, size)


def expert_kernel(
    blocks,
    first_lane,
    tail_at,
    experts,
    cuts,
    columns,
    theirs_ref,
    mine_rows,
    their_rows,
    gain_ref,
    in_ref,
    part_ref,
    square_ref,
    gate_ref,
    upper_ref,
    mine_tail_ref,
    theirs_tail_ref,
    out_weight_ref,
    near_ref,
    far_ref,
    own_ref,
    rows_ref,
    act_ref,
    rest_ref,
    whole_ref,
):
    square = square_ref[...] + scaled_rows(
        blocks, 1, theirs_ref, mine_rows, their_rows, gain_ref, rest_ref, rows_ref
    )
    index = here()
    width = theirs_ref.shape[2]
    for p in range(blocks // 2):
        for odd, ref in enumerate((part_ref, rest_ref)):
            lanes = pl.ds(pl.multiple_of((index[0] ^ (2 * p + odd)) * width, width), width)
            whole_ref[:, lanes] = ref[:, p * width : (p + 1) * width]
    size = own_ref.shape[0]
    own_ref[...] = whole_ref[pl.ds(pl.multiple_of(index[1] * size, size), size), :]
    factor = lax.rsqrt(square / (blocks * width) + EPS)
    for start, size in cuts:
        at = slice(start, start + size)
        gate = factor * (
            gate_ref[:, at] + products(blocks, 1, width, rows_ref, in_ref, 0, start, size)
        )
        upper = factor * (
            upper_ref[:, at] + products(blocks, 1, width, rows_ref, in_ref, 1, start, size)
        )
        act_ref[:, at] = (gate / (1.0 + jnp.exp(-gate)) * upper).astype(BF16)
    half = near_ref.shape[0]
    pieces = mine_tail_ref.shape[0]
    count = half // pieces
    tail = jnp.concatenate(
        [ref[p, :count, tail_at:] for ref in (mine_tail_ref, theirs_tail_ref) for p in range(pieces)],
        axis=0,
    )
    tail = tail.astype(F32)
    lane = lax.broadcasted_iota(jnp.int32, tail.shape, 1) - first_lane
    slot = lax.div(index[0] * lax.axis_size("span") + index[1], 2)
    scale = jnp.sum(
        jnp.where((lane == slot) | (lane == slot + experts), tail, 0.0), axis=1, keepdims=True
    )
    wide = out_weight_ref.shape[1] // columns
    for n in range(columns):
        span = slice(n * wide, (n + 1) * wide)
        done = nn(act_ref[...], out_weight_ref[:, span])
        done = jnp.where(scale > 0, done * scale, 0.0).astype(BF16)
        near_ref[:, span] = done[:half]
        far_ref[:, span] = done[half:]


def level_kernel(near_ref, back_ref, *outs):
    rows = outs[0].shape[0]
    for n, out in enumerate(outs):
        at = slice(n * rows, (n + 1) * rows)
        out[...] = (near_ref[at, :].astype(F32) + back_ref[at, :].astype(F32)).astype(out.dtype)


def rows_kernel(spans, *refs):
    parts, outs, buf = refs[: -spans - 1], refs[-spans - 1 : -1], refs[-1]
    index = here()[1]
    total = parts[0][...]
    for p in parts[1:]:
        total = total + p[...].astype(F32)
    buf[...] = total
    count = outs[0].shape[0]
    for k, out in enumerate(outs):
        at = pl.ds(pl.multiple_of((index ^ k) * count, count), count)
        out[...] = buf[at, :].astype(out.dtype)


def last_kernel(spans, *refs):
    parts = refs[:spans]
    own_ref, live_ref, out_ref = refs[spans:]
    count = out_ref.shape[0]
    routed = sum(p[...].astype(F32) for p in parts)
    at = pl.ds(pl.multiple_of(here()[1] * count, count), count)
    total = own_ref[...] + routed
    out_ref[...] = jnp.where(live_ref[at, :] > 0, total, 0.0).astype(BF16)


def per_device(
    raw_tokens,
    keep,
    attn_gain,
    query_weight,
    latent_weight,
    kv_gain,
    out_weight,
    moe_gain,
    expert_ids,
    gate_values,
    expert_slot,
    expert_in,
    expert_out,
):
    kv_rank = kv_gain.shape[0]
    spans = lax.axis_size("span")
    contexts = lax.axis_size("context")
    part_width = latent_weight.shape[1]
    latent_width = part_width * spans
    rope = latent_width - kv_rank
    model = attn_gain.shape[0]
    kept = keep.shape[1]
    raw_rows = raw_tokens.shape[0]
    heads = query_weight.shape[1] // latent_width
    rows_dev = expert_ids.shape[0]
    experts = expert_slot.shape[0]
    hidden = expert_in.shape[3]
    evens = list(range(0, contexts, 2))

    picked = call(
        pick_kernel,
        shape((kept, raw_tokens.shape[1]), BF16),
        [HBM] * 2,
        (keep, raw_tokens),
        scratch=[
            pltpu.VMEM(keep.shape, jnp.int32),
            pltpu.VMEM(raw_tokens.shape, BF16),
            pltpu.SemaphoreType.DMA((2,)),
        ],
        limit=4,
    )
    parts = gathered(picked, "span", range(1, spans))

    sent_width = up(max(part_width, experts))
    begun = model // EARLY
    near_weight, gain, early_query, dense = call(
        prepare_kernel,
        [
            shape((part_width, model), BF16),
            shape((1, model), F32),
            shape((begun, query_weight.shape[1]), BF16),
            shape((rows_dev, sent_width), F32),
        ],
        [HBM] * 6,
        (expert_ids, gate_values, expert_slot, latent_weight.T, attn_gain[None], query_weight),
        scratch=[
            pltpu.VMEM(expert_ids.shape, jnp.int32),
            pltpu.VMEM(gate_values.shape, F32),
            pltpu.SMEM(expert_slot.shape, jnp.int32),
            pltpu.SemaphoreType.DMA((6,)),
        ],
        moved=query_weight.size,
        limit=8,
    )

    compact, normed, sent = call(
        functools.partial(latent_kernel, spans),
        [
            shape((kept, model), BF16),
            shape((kept, model), BF16),
            shape((kept + rows_dev, sent_width), F32),
        ],
        [VM] * (spans + 3),
        (*parts, gain, near_weight, dense),
        flops=2 * kept * latent_weight.size,
        moved=2 * latent_weight.size,
        limit=4,
    )
    parts = gathered(sent, "span", range(1, spans))
    row_width = up(latent_width + 2 * experts + 1)
    steps = 3
    query, cosine, sine, live, near_kv, near_moe = call(
        functools.partial(query_kernel, heads, raw_rows),
        [
            shape((heads * kept, row_width), BF16),
            shape((kept, rope), F32),
            shape((kept, rope), F32),
            shape((kept, 1), F32),
            shape((1, kv_rank), F32),
            shape((1, model), F32),
        ],
        [VM, VM] + [HBM] * 4,
        (normed, early_query, query_weight, keep, kv_gain[None], moe_gain[None]),
        scratch=[
            pltpu.VMEM((steps, (model - begun) // steps, query_weight.shape[1]), BF16),
            pltpu.VMEM(keep.shape, jnp.int32),
            pltpu.SemaphoreType.DMA((steps + 3,)),
        ],
        flops=2 * kept * query_weight.size,
        moved=query_weight.size,
        limit=10,
    )
    sent = call(
        functools.partial(cache_kernel, spans, part_width, experts),
        shape(((1 + heads) * kept, row_width), BF16),
        [VM] * (spans + 5),
        (*parts, live, near_kv, cosine, sine, query),
        limit=4,
    )

    cached = call(emit_kernel, shape((kept, latent_width), BF16), [VM], (sent,), limit=4)

    mine_keys = jnp.stack(gathered(sent, "context", evens[1:]))
    their_keys = partner(mine_keys, "context", 1)
    partial = call(
        functools.partial(attend_kernel, heads, kv_rank, latent_width + 2 * experts, contexts),
        shape((contexts * kept, out_weight.shape[1]), BF16),
        [VM, VM, HBM],
        (mine_keys, their_keys, out_weight),
        scratch=[pltpu.VMEM(out_weight.shape, BF16), pltpu.SemaphoreType.DMA],
        flops=2 * kept * contexts * out_weight.size,
        moved=2 * out_weight.size,
        limit=12,
    )

    column, bit = partial, 1
    while bit < spans:
        column = call(
            sum_kernel,
            shape(partial.shape, BF16),
            [VM] * 2,
            gathered(column, "span", [bit]),
            limit=4,
        )
        bit *= 2
    mine_rows = jnp.stack(gathered(compact, "context", evens[1:]))
    their_rows = partner(mine_rows, "context", 1)

    mine = jnp.stack(gathered(column, "context", evens[1:]))
    theirs = partner(mine, "context", 1)
    half = mine.shape[0] * kept
    cuts, start = [], 0
    while start < hidden:
        size = min(2 * LANES, hidden - start)
        cuts.append((start, size))
        start += size
    weights_in = jnp.swapaxes(expert_in[0], 1, 2)
    begun = call(
        functools.partial(begin_kernel, contexts, cuts),
        [
            shape((kept, model // 2), F32),
            shape((2 * half, 1), F32),
            shape((2 * half, hidden), F32),
            shape((2 * half, hidden), F32),
        ],
        [VM] * 5,
        (mine, mine_rows, their_rows, near_moe, weights_in),
        scratch=[pltpu.VMEM((2 * half, model // 2), BF16)],
        flops=2 * 2 * half * hidden * model,
        moved=4 * hidden * model,
        limit=20,
    )
    near, far, own = call(
        functools.partial(
            expert_kernel, contexts, latent_width - kv_rank, kv_rank, experts, cuts, 4
        ),
        [shape((half, model), BF16), shape((half, model), BF16), shape((rows_dev, model), F32)],
        [VM] * 12,
        (
            theirs,
            mine_rows,
            their_rows,
            near_moe,
            weights_in,
            *begun,
            mine_keys,
            their_keys,
            expert_out[0],
        ),
        scratch=[
            pltpu.VMEM((2 * half, model // 2), BF16),
            pltpu.VMEM((2 * half, hidden), BF16),
            pltpu.VMEM((kept, model // 2), F32),
            pltpu.VMEM((kept, model), F32),
        ],
        flops=4 * 2 * half * hidden * model,
        moved=4 * hidden * model,
        limit=20,
    )

    levels = call(
        level_kernel,
        [shape((kept, model), F32)] + [shape((kept, model), BF16)] * (len(evens) - 1),
        [VM, VM],
        (near, partner(far, "context", 1)),
        limit=6,
    )
    got = []
    for level, i in zip(levels[1:], evens[1:]):
        got.append(partner(level, "context", i))
    rows = call(
        functools.partial(rows_kernel, spans),
        [shape((rows_dev, model), F32)] + [shape((rows_dev, model), BF16)] * (spans - 1),
        [VM] * len(levels),
        (levels[0], *got),
        scratch=[pltpu.VMEM((kept, model), F32)],
        limit=6,
    )
    got = []
    for k in range(1, spans):
        got.append(partner(rows[k], "span", k))
    layer_out = call(
        functools.partial(last_kernel, spans),
        shape((rows_dev, model), BF16),
        [VM] * (spans + 2),
        (rows[0], *got, own, live),
        limit=4,
    )
    return (layer_out, cached)


def solution(mesh):
    placed = (
        P(("groups", "context"), "span"),
        P(("groups", "context"), None),
        P(),
        P(None, "span"),
        P(None, "span"),
        P(),
        P("span", "context"),
        P(),
        P(("groups", "context", "span"), None),
        P(("groups", "context", "span"), None),
        P(),
        P(("context", "span"), None, None, None),
        P(("context", "span"), None, None),
    )
    return jax.shard_map(
        per_device,
        mesh=mesh,
        in_specs=placed,
        out_specs=(P(("groups", "context", "span"), None), P(("groups", "context"), None)),
        check_vma=False,
    )
```

```python
import functools
import math

import jax
import jax.numpy as jnp
from jax import lax
from jax.experimental import pallas as pl
from jax.experimental.pallas import tpu as pltpu
from jax.sharding import PartitionSpec as P


EPS = 1e-06
THETA = 50000.0
SCALE = 192.0 ** (-0.5)
NEGATIVE = -1e30
LANES = 128
EARLY = 4
F32 = jnp.float32
BF16 = jnp.bfloat16
MIB = 1 << 20


VM = pl.BlockSpec(memory_space=pltpu.VMEM)
HBM = pl.BlockSpec(memory_space=pltpu.HBM)


def up(count, unit=LANES):
    return -(-count // unit) * unit


def shape(dims, dtype):
    return jax.ShapeDtypeStruct(tuple(dims), dtype)


def call(kernel, outs, in_specs, args, scratch=(), flops=0, moved=0, limit=16):
    single = not isinstance(outs, (list, tuple))
    args = [
        pltpu.with_memory_space_constraint(value, pltpu.HBM) if spec is HBM else value
        for spec, value in zip(in_specs, args)
    ]
    return pl.pallas_call(
        kernel,
        out_shape=outs,
        in_specs=in_specs,
        out_specs=VM if single else [VM] * len(outs),
        scratch_shapes=list(scratch),
        compiler_params=pltpu.CompilerParams(vmem_limit_bytes=limit * MIB),
        cost_estimate=pl.CostEstimate(flops=flops, bytes_accessed=moved, transcendentals=0),
    )(*args)


def nt(left, right):
    return lax.dot_general(left, right, (((1,), (1,)), ((), ())), preferred_element_type=F32)


def nn(left, right):
    return jnp.dot(left, right, preferred_element_type=F32)


def here():
    return lax.axis_index("context"), lax.axis_index("span")


def partner(values, axis, mask):
    count = lax.axis_size(axis)
    return lax.ppermute(values, axis, [(i, i ^ mask) for i in range(count)])


def gathered(values, axis, masks):
    parts = [values]
    for mask in masks:
        parts.append(partner(values, axis, mask))
    return parts


def natural(parts, index):
    bit = 1
    while bit < len(parts):
        swap = (index & bit) != 0
        parts = [jnp.where(swap, parts[k ^ bit], parts[k]) for k in range(len(parts))]
        bit *= 2
    return parts


def fetch(pairs, sem):
    copies = [pltpu.make_async_copy(a, b, sem.at[n]) for n, (a, b) in enumerate(pairs)]
    for copy in copies:
        copy.start()
    return copies


def pick_kernel(keep_hbm, raw_hbm, out_ref, keep_ref, raw_ref, sem):
    for copy in fetch([(keep_hbm, keep_ref), (raw_hbm, raw_ref)], sem):
        copy.wait()
    rows = lax.broadcasted_iota(jnp.int32, (raw_ref.shape[0], keep_ref.shape[1]), 0)
    hits = jnp.where(rows == keep_ref[...], 1.0, 0.0).astype(BF16)
    out_ref[...] = lax.dot_general(
        hits, raw_ref[...], (((0,), (0,)), ((), ())), preferred_element_type=F32
    ).astype(BF16)


def prepare_kernel(
    ids_hbm,
    gates_hbm,
    slot_hbm,
    weight_hbm,
    gain_hbm,
    query_hbm,
    weight_ref,
    gain_ref,
    query_ref,
    dense_ref,
    ids_ref,
    gates_ref,
    slot_ref,
    sem,
):
    early = query_hbm.at[pl.ds(0, query_ref.shape[0]), :]
    small = [(ids_hbm, ids_ref), (gates_hbm, gates_ref), (slot_hbm, slot_ref)]
    large = [(weight_hbm, weight_ref), (gain_hbm, gain_ref), (early, query_ref)]
    copies = fetch(small + large, sem)
    for copy in copies[:3]:
        copy.wait()
    ids = ids_ref[...]
    slots = jnp.zeros_like(ids)
    for e in range(slot_ref.shape[0]):
        slots = jnp.where(ids == e, slot_ref[e], slots)
    lane = lax.broadcasted_iota(jnp.int32, dense_ref.shape, 1)
    gates = jnp.zeros(dense_ref.shape, F32)
    for t in range(ids.shape[1]):
        gates = gates + jnp.where(lane == slots[:, t : t + 1], gates_ref[:, t : t + 1], 0.0)
    dense_ref[...] = gates
    for copy in copies[3:]:
        copy.wait()


def latent_kernel(spans, *refs):
    parts = refs[:spans]
    gain_ref, weight_ref, dense_ref, compact_ref, normed_ref, sent_ref = refs[spans:]
    index = here()[1]
    rows, block = parts[0].shape
    values = [p[...].astype(F32) for p in parts]
    square = sum(jnp.sum(v * v, axis=1, keepdims=True) for v in values)
    factor = lax.rsqrt(square / (spans * block) + EPS)
    for k in range(spans):
        at = pl.ds(pl.multiple_of((index ^ k) * block, block), block)
        compact_ref[:, at] = parts[k][...]
        normed_ref[:, at] = (values[k] * factor * gain_ref[:, at]).astype(BF16)
    sent_ref[0:rows, :] = jnp.zeros((rows, sent_ref.shape[1]), F32)
    sent_ref[0:rows, 0 : weight_ref.shape[0]] = nt(normed_ref[...], weight_ref[...])
    sent_ref[rows:, :] = dense_ref[...]


def rotated(values, cosine, sine):
    half = values.shape[1] // 2
    swapped = jnp.concatenate([values[:, half:], values[:, :half]], axis=1)
    return values * cosine + swapped * sine


def query_kernel(
    heads,
    raw_rows,
    normed_ref,
    early_ref,
    weight_hbm,
    keep_hbm,
    kv_hbm,
    moe_hbm,
    out_ref,
    cos_ref,
    sin_ref,
    live_ref,
    kv_ref,
    moe_ref,
    buf,
    keep_ref,
    sem,
):
    begun = early_ref.shape[0]
    steps, deep = buf.shape[:2]
    small = [(keep_hbm, keep_ref), (kv_hbm, kv_ref), (moe_hbm, moe_ref)]
    late = [(weight_hbm.at[pl.ds(begun + n * deep, deep), :], buf.at[n]) for n in range(steps)]
    copies = fetch(small + late, sem)
    copies[0].wait()
    rows, rope = cos_ref.shape
    diagonal = lax.broadcasted_iota(jnp.int32, (rows, rows), 0) == lax.broadcasted_iota(
        jnp.int32, (rows, rows), 1
    )
    listing = jnp.sum(
        jnp.where(diagonal, keep_ref[...].astype(F32), 0.0), axis=1, keepdims=True
    )
    live_ref[...] = jnp.where(listing >= 0, 1.0, 0.0)
    positions = (here()[0] * raw_rows).astype(F32) + jnp.maximum(listing, 0.0)
    half = rope // 2
    lane = lax.broadcasted_iota(jnp.int32, (rows, rope), 1)
    first = lane < half
    place = jnp.where(first, lane, lane - half).astype(F32)
    angles = positions * jnp.exp(place * (-2.0 / rope * math.log(THETA)))
    cos_ref[...] = jnp.cos(angles)
    sine = jnp.sin(angles)
    sin_ref[...] = jnp.where(first, -sine, sine)
    latent = early_ref.shape[1] // heads
    total = nn(normed_ref[:, :begun], early_ref[...])
    for n in range(steps):
        copies[3 + n].wait()
        at = begun + n * deep
        total = total + nn(normed_ref[:, at : at + deep], buf[n])
    kv_rank = latent - rope
    out_ref[...] = jnp.zeros(out_ref.shape, BF16)
    for h in range(heads):
        one = total[:, h * latent : (h + 1) * latent]
        out_ref[h * rows : (h + 1) * rows, 0:kv_rank] = one[:, :kv_rank].astype(BF16)
        out_ref[h * rows : (h + 1) * rows, kv_rank:latent] = rotated(
            one[:, kv_rank:], cos_ref[...], sin_ref[...]
        ).astype(BF16)
    for copy in copies[1:3]:
        copy.wait()


def cache_kernel(spans, width, experts, *refs):
    parts = refs[:spans]
    live_ref, gain_ref, cos_ref, sin_ref, query_ref, sent_ref = refs[spans:]
    rows = live_ref.shape[0]
    kv_rank = gain_ref.shape[1]
    values = natural([p[...] for p in parts], here()[1])
    latent = jnp.concatenate([v[:rows, :width] for v in values], axis=1)
    gates = jnp.concatenate([v[rows:, :experts] for v in values], axis=0)
    nope = latent[:, :kv_rank]
    factor = lax.rsqrt(jnp.mean(nope * nope, axis=1, keepdims=True) + EPS)
    nope = nope * factor * gain_ref[...]
    rope = rotated(latent[:, kv_rank:], cos_ref[...], sin_ref[...])
    high = gates.astype(BF16).astype(F32)
    used = rope.shape[1] + 2 * experts + 1
    tail = [rope, high, gates - high, live_ref[...]]
    rest = sent_ref.shape[1] - kv_rank - used
    if rest:
        tail.append(jnp.zeros((rows, rest), F32))
    sent_ref[:rows, :kv_rank] = nope.astype(BF16)
    sent_ref[:rows, kv_rank:] = jnp.concatenate(tail, axis=1).astype(BF16)
    sent_ref[rows:, :] = query_ref[...]


def emit_kernel(sent_ref, out_ref):
    out_ref[...] = sent_ref[: out_ref.shape[0], : out_ref.shape[1]]


def places(blocks):
    return list(range(0, blocks, 2)) + list(range(1, blocks, 2))


def attend_kernel(
    heads, kv_rank, flag_lane, blocks, mine_ref, theirs_ref, weight_hbm, out_ref, weight_ref, sem
):
    copy = pltpu.make_async_copy(weight_hbm, weight_ref, sem)
    copy.start()
    count = mine_ref.shape[1] // (1 + heads)
    index = here()[0]
    half = blocks // 2
    pieces = [(mine_ref, n) for n in range(half)] + [(theirs_ref, n) for n in range(half)]

    def gather(n):
        return jnp.concatenate(
            [ref[p, n * count : (n + 1) * count, :] for ref, p in pieces], axis=0
        )

    keys = gather(0)
    total, width = keys.shape
    lane = lax.broadcasted_iota(jnp.int32, (8, width), 1)
    flags = nt(jnp.where(lane == flag_lane, 1.0, 0.0).astype(BF16), keys)[0:1, :]

    shift = count.bit_length() - 1

    def slot(dims, axis):
        line = lax.broadcasted_iota(jnp.int32, dims, axis)
        if count == 1 << shift:
            at, rest = line >> shift, line & (count - 1)
        else:
            at, rest = line // count, line % count
        which = jnp.where(at < half, 2 * at, 2 * (at - half) + 1)
        return (which ^ index) * count + rest

    allowed = (slot((1, total), 1) <= slot((total, 1), 0)) & (flags > 0)
    result = jnp.zeros(out_ref.shape, F32)
    for h in range(heads):
        scores = nt(gather(1 + h), keys) * SCALE
        scores = jnp.where(allowed, scores, NEGATIVE)
        highest = jnp.max(scores, axis=1, keepdims=True)
        weight = jnp.where(allowed, jnp.exp(scores - highest), 0.0)
        share = 1.0 / jnp.sum(weight, axis=1, keepdims=True)
        summed = nn(weight.astype(BF16), keys[:, :kv_rank])
        mixed = (summed * share).astype(BF16)
        if h == 0:
            copy.wait()
        result = result + nn(mixed, weight_ref[h * kv_rank : (h + 1) * kv_rank, :])
    out_ref[...] = result.astype(BF16)


def sum_kernel(*refs):
    refs[-1][...] = sum(ref[...].astype(F32) for ref in refs[:-1]).astype(BF16)


def scaled_rows(blocks, odd, pieces_ref, mine_rows, their_rows, gain_ref, part_ref, rows_ref):
    order = places(blocks)
    half = blocks // 2
    index = here()[0]
    count, width = mine_rows.shape[1], pieces_ref.shape[2]
    squares = [jnp.zeros((count, 1), F32)] * blocks
    for p in range(half):
        i = 2 * p + odd
        lanes = pl.ds(pl.multiple_of((index ^ i) * width, width), width)
        gain = gain_ref[:, lanes]
        for at, j in enumerate(order):
            to = order.index(i ^ j)
            rows = mine_rows if to < half else their_rows
            resid = rows[to % half, :, lanes].astype(F32) + pieces_ref[
                p, at * count : (at + 1) * count, :
            ].astype(F32)
            squares[to] = squares[to] + jnp.sum(resid * resid, axis=1, keepdims=True)
            rows_ref[to * count : (to + 1) * count, p * width : (p + 1) * width] = (
                resid * gain
            ).astype(BF16)
            if to == 0:
                part_ref[:, p * width : (p + 1) * width] = resid
    return jnp.concatenate(squares, axis=0)


def products(blocks, odd, width, rows_ref, in_ref, half, start, size):
    index = here()[0]
    total = jnp.zeros((rows_ref.shape[0], size), F32)
    for p in range(blocks // 2):
        lanes = pl.ds(pl.multiple_of((index ^ (2 * p + odd)) * width, width), width)
        total = total + nt(
            rows_ref[:, p * width : (p + 1) * width], in_ref[half, start : start + size, lanes]
        )
    return total


def begin_kernel(
    blocks,
    cuts,
    mine_ref,
    mine_rows,
    their_rows,
    gain_ref,
    in_ref,
    part_ref,
    square_ref,
    gate_ref,
    upper_ref,
    rows_ref,
):
    square_ref[...] = scaled_rows(
        blocks, 0, mine_ref, mine_rows, their_rows, gain_ref, part_ref, rows_ref
    )
    width = mine_ref.shape[2]
    for start, size in cuts:
        at = slice(start, start + size)
        gate_ref[:, at] = products(blocks, 0, width, rows_ref, in_ref, 0, start, size)
        upper_ref[:, at] = products(blocks, 0, width, rows_ref, in_ref, 1, start, size)


def expert_kernel(
    blocks,
    first_lane,
    tail_at,
    experts,
    cuts,
    columns,
    theirs_ref,
    mine_rows,
    their_rows,
    gain_ref,
    in_ref,
    part_ref,
    square_ref,
    gate_ref,
    upper_ref,
    mine_tail_ref,
    theirs_tail_ref,
    out_weight_ref,
    near_ref,
    far_ref,
    own_ref,
    rows_ref,
    act_ref,
    rest_ref,
    whole_ref,
):
    square = square_ref[...] + scaled_rows(
        blocks, 1, theirs_ref, mine_rows, their_rows, gain_ref, rest_ref, rows_ref
    )
    index = here()
    width = theirs_ref.shape[2]
    for p in range(blocks // 2):
        for odd, ref in enumerate((part_ref, rest_ref)):
            lanes = pl.ds(pl.multiple_of((index[0] ^ (2 * p + odd)) * width, width), width)
            whole_ref[:, lanes] = ref[:, p * width : (p + 1) * width]
    size = own_ref.shape[0]
    own_ref[...] = whole_ref[pl.ds(pl.multiple_of(index[1] * size, size), size), :]
    factor = lax.rsqrt(square / (blocks * width) + EPS)
    for start, size in cuts:
        at = slice(start, start + size)
        gate = factor * (
            gate_ref[:, at] + products(blocks, 1, width, rows_ref, in_ref, 0, start, size)
        )
        upper = factor * (
            upper_ref[:, at] + products(blocks, 1, width, rows_ref, in_ref, 1, start, size)
        )
        act_ref[:, at] = (gate / (1.0 + jnp.exp(-gate)) * upper).astype(BF16)
    half = near_ref.shape[0]
    pieces = mine_tail_ref.shape[0]
    count = half // pieces
    tail = jnp.concatenate(
        [ref[p, :count, tail_at:] for ref in (mine_tail_ref, theirs_tail_ref) for p in range(pieces)],
        axis=0,
    )
    tail = tail.astype(F32)
    lane = lax.broadcasted_iota(jnp.int32, tail.shape, 1) - first_lane
    slot = lax.div(index[0] * lax.axis_size("span") + index[1], 2)
    scale = jnp.sum(
        jnp.where((lane == slot) | (lane == slot + experts), tail, 0.0), axis=1, keepdims=True
    )
    wide = out_weight_ref.shape[1] // columns
    for n in range(columns):
        span = slice(n * wide, (n + 1) * wide)
        done = nn(act_ref[...], out_weight_ref[:, span])
        done = jnp.where(scale > 0, done * scale, 0.0).astype(BF16)
        near_ref[:, span] = done[:half]
        far_ref[:, span] = done[half:]


def level_kernel(near_ref, back_ref, *outs):
    rows = outs[0].shape[0]
    for n, out in enumerate(outs):
        at = slice(n * rows, (n + 1) * rows)
        out[...] = (near_ref[at, :].astype(F32) + back_ref[at, :].astype(F32)).astype(out.dtype)


def rows_kernel(spans, *refs):
    parts, outs, buf = refs[: -spans - 1], refs[-spans - 1 : -1], refs[-1]
    index = here()[1]
    total = parts[0][...]
    for p in parts[1:]:
        total = total + p[...].astype(F32)
    buf[...] = total
    count = outs[0].shape[0]
    for k, out in enumerate(outs):
        at = pl.ds(pl.multiple_of((index ^ k) * count, count), count)
        out[...] = buf[at, :].astype(out.dtype)


def last_kernel(spans, *refs):
    parts = refs[:spans]
    own_ref, live_ref, out_ref = refs[spans:]
    count = out_ref.shape[0]
    routed = sum(p[...].astype(F32) for p in parts)
    at = pl.ds(pl.multiple_of(here()[1] * count, count), count)
    total = own_ref[...] + routed
    out_ref[...] = jnp.where(live_ref[at, :] > 0, total, 0.0).astype(BF16)


def per_device(
    raw_tokens,
    keep,
    attn_gain,
    query_weight,
    latent_weight,
    kv_gain,
    out_weight,
    moe_gain,
    expert_ids,
    gate_values,
    expert_slot,
    expert_in,
    expert_out,
):
    kv_rank = kv_gain.shape[0]
    spans = lax.axis_size("span")
    contexts = lax.axis_size("context")
    part_width = latent_weight.shape[1]
    latent_width = part_width * spans
    rope = latent_width - kv_rank
    model = attn_gain.shape[0]
    kept = keep.shape[1]
    raw_rows = raw_tokens.shape[0]
    heads = query_weight.shape[1] // latent_width
    rows_dev = expert_ids.shape[0]
    experts = expert_slot.shape[0]
    hidden = expert_in.shape[3]
    evens = list(range(0, contexts, 2))

    picked = call(
        pick_kernel,
        shape((kept, raw_tokens.shape[1]), BF16),
        [HBM] * 2,
        (keep, raw_tokens),
        scratch=[
            pltpu.VMEM(keep.shape, jnp.int32),
            pltpu.VMEM(raw_tokens.shape, BF16),
            pltpu.SemaphoreType.DMA((2,)),
        ],
        limit=4,
    )
    parts = gathered(picked, "span", range(1, spans))

    sent_width = up(max(part_width, experts))
    begun = model // EARLY
    near_weight, gain, early_query, dense = call(
        prepare_kernel,
        [
            shape((part_width, model), BF16),
            shape((1, model), F32),
            shape((begun, query_weight.shape[1]), BF16),
            shape((rows_dev, sent_width), F32),
        ],
        [HBM] * 6,
        (expert_ids, gate_values, expert_slot, latent_weight.T, attn_gain[None], query_weight),
        scratch=[
            pltpu.VMEM(expert_ids.shape, jnp.int32),
            pltpu.VMEM(gate_values.shape, F32),
            pltpu.SMEM(expert_slot.shape, jnp.int32),
            pltpu.SemaphoreType.DMA((6,)),
        ],
        moved=query_weight.size,
        limit=8,
    )

    compact, normed, sent = call(
        functools.partial(latent_kernel, spans),
        [
            shape((kept, model), BF16),
            shape((kept, model), BF16),
            shape((kept + rows_dev, sent_width), F32),
        ],
        [VM] * (spans + 3),
        (*parts, gain, near_weight, dense),
        flops=2 * kept * latent_weight.size,
        moved=2 * latent_weight.size,
        limit=4,
    )
    parts = gathered(sent, "span", range(1, spans))
    row_width = up(latent_width + 2 * experts + 1)
    steps = 3
    query, cosine, sine, live, near_kv, near_moe = call(
        functools.partial(query_kernel, heads, raw_rows),
        [
            shape((heads * kept, row_width), BF16),
            shape((kept, rope), F32),
            shape((kept, rope), F32),
            shape((kept, 1), F32),
            shape((1, kv_rank), F32),
            shape((1, model), F32),
        ],
        [VM, VM] + [HBM] * 4,
        (normed, early_query, query_weight, keep, kv_gain[None], moe_gain[None]),
        scratch=[
            pltpu.VMEM((steps, (model - begun) // steps, query_weight.shape[1]), BF16),
            pltpu.VMEM(keep.shape, jnp.int32),
            pltpu.SemaphoreType.DMA((steps + 3,)),
        ],
        flops=2 * kept * query_weight.size,
        moved=query_weight.size,
        limit=10,
    )
    sent = call(
        functools.partial(cache_kernel, spans, part_width, experts),
        shape(((1 + heads) * kept, row_width), BF16),
        [VM] * (spans + 5),
        (*parts, live, near_kv, cosine, sine, query),
        limit=4,
    )

    cached = call(emit_kernel, shape((kept, latent_width), BF16), [VM], (sent,), limit=4)

    mine_keys = jnp.stack(gathered(sent, "context", evens[1:]))
    their_keys = partner(mine_keys, "context", 1)
    partial = call(
        functools.partial(attend_kernel, heads, kv_rank, latent_width + 2 * experts, contexts),
        shape((contexts * kept, out_weight.shape[1]), BF16),
        [VM, VM, HBM],
        (mine_keys, their_keys, out_weight),
        scratch=[pltpu.VMEM(out_weight.shape, BF16), pltpu.SemaphoreType.DMA],
        flops=2 * kept * contexts * out_weight.size,
        moved=2 * out_weight.size,
        limit=12,
    )

    column, bit = partial, 1
    while bit < spans:
        column = call(
            sum_kernel,
            shape(partial.shape, BF16),
            [VM] * 2,
            gathered(column, "span", [bit]),
            limit=4,
        )
        bit *= 2
    mine_rows = jnp.stack(gathered(compact, "context", evens[1:]))
    their_rows = partner(mine_rows, "context", 1)

    mine = jnp.stack(gathered(column, "context", evens[1:]))
    theirs = partner(mine, "context", 1)
    half = mine.shape[0] * kept
    cuts, start = [], 0
    while start < hidden:
        size = min(2 * LANES, hidden - start)
        cuts.append((start, size))
        start += size
    weights_in = jnp.swapaxes(expert_in[0], 1, 2)
    begun = call(
        functools.partial(begin_kernel, contexts, cuts),
        [
            shape((kept, model // 2), F32),
            shape((2 * half, 1), F32),
            shape((2 * half, hidden), F32),
            shape((2 * half, hidden), F32),
        ],
        [VM] * 5,
        (mine, mine_rows, their_rows, near_moe, weights_in),
        scratch=[pltpu.VMEM((2 * half, model // 2), BF16)],
        flops=2 * 2 * half * hidden * model,
        moved=4 * hidden * model,
        limit=20,
    )
    near, far, own = call(
        functools.partial(
            expert_kernel, contexts, latent_width - kv_rank, kv_rank, experts, cuts, 4
        ),
        [shape((half, model), BF16), shape((half, model), BF16), shape((rows_dev, model), F32)],
        [VM] * 12,
        (
            theirs,
            mine_rows,
            their_rows,
            near_moe,
            weights_in,
            *begun,
            mine_keys,
            their_keys,
            expert_out[0],
        ),
        scratch=[
            pltpu.VMEM((2 * half, model // 2), BF16),
            pltpu.VMEM((2 * half, hidden), BF16),
            pltpu.VMEM((kept, model // 2), F32),
            pltpu.VMEM((kept, model), F32),
        ],
        flops=4 * 2 * half * hidden * model,
        moved=4 * hidden * model,
        limit=20,
    )

    levels = call(
        level_kernel,
        [shape((kept, model), F32)] + [shape((kept, model), BF16)] * (len(evens) - 1),
        [VM, VM],
        (near, partner(far, "context", 1)),
        limit=6,
    )
    got = []
    for level, i in zip(levels[1:], evens[1:]):
        got.append(partner(level, "context", i))
    rows = call(
        functools.partial(rows_kernel, spans),
        [shape((rows_dev, model), F32)] + [shape((rows_dev, model), BF16)] * (spans - 1),
        [VM] * len(levels),
        (levels[0], *got),
        scratch=[pltpu.VMEM((kept, model), F32)],
        limit=6,
    )
    got = []
    for k in range(1, spans):
        got.append(partner(rows[k], "span", k))
    layer_out = call(
        functools.partial(last_kernel, spans),
        shape((rows_dev, model), BF16),
        [VM] * (spans + 2),
        (rows[0], *got, own, live),
        limit=4,
    )
    return (layer_out, cached)


def solution(mesh):
    placed = (
        P(("groups", "context"), "span"),
        P(("groups", "context"), None),
        P(),
        P(None, "span"),
        P(None, "span"),
        P(),
        P("span", "context"),
        P(),
        P(("groups", "context", "span"), None),
        P(("groups", "context", "span"), None),
        P(),
        P(("context", "span"), None, None, None),
        P(("context", "span"), None, None),
    )
    return jax.shard_map(
        per_device,
        mesh=mesh,
        in_specs=placed,
        out_specs=(P(("groups", "context", "span"), None), P(("groups", "context"), None)),
        check_vma=False,
    )
```

```python
import functools
import math

import jax
import jax.numpy as jnp
from jax import lax
from jax.experimental import pallas as pl
from jax.experimental.pallas import tpu as pltpu
from jax.sharding import PartitionSpec as P


EPS = 1e-06
THETA = 50000.0
SCALE = 192.0 ** (-0.5)
NEGATIVE = -1e30
LANES = 128
EARLY = 4
F32 = jnp.float32
BF16 = jnp.bfloat16
MIB = 1 << 20


VM = pl.BlockSpec(memory_space=pltpu.VMEM)
HBM = pl.BlockSpec(memory_space=pltpu.HBM)


def up(count, unit=LANES):
    return -(-count // unit) * unit


def shape(dims, dtype):
    return jax.ShapeDtypeStruct(tuple(dims), dtype)


def call(kernel, outs, in_specs, args, scratch=(), flops=0, moved=0, limit=16):
    single = not isinstance(outs, (list, tuple))
    args = [
        pltpu.with_memory_space_constraint(value, pltpu.HBM) if spec is HBM else value
        for spec, value in zip(in_specs, args)
    ]
    return pl.pallas_call(
        kernel,
        out_shape=outs,
        in_specs=in_specs,
        out_specs=VM if single else [VM] * len(outs),
        scratch_shapes=list(scratch),
        compiler_params=pltpu.CompilerParams(vmem_limit_bytes=limit * MIB),
        cost_estimate=pl.CostEstimate(flops=flops, bytes_accessed=moved, transcendentals=0),
    )(*args)


def nt(left, right):
    return lax.dot_general(left, right, (((1,), (1,)), ((), ())), preferred_element_type=F32)


def nn(left, right):
    return jnp.dot(left, right, preferred_element_type=F32)


def here():
    return lax.axis_index("context"), lax.axis_index("span")


def partner(values, axis, mask):
    count = lax.axis_size(axis)
    return lax.ppermute(values, axis, [(i, i ^ mask) for i in range(count)])


def gathered(values, axis, masks):
    parts = [values]
    for mask in masks:
        parts.append(partner(values, axis, mask))
    return parts


def natural(parts, index):
    bit = 1
    while bit < len(parts):
        swap = (index & bit) != 0
        parts = [jnp.where(swap, parts[k ^ bit], parts[k]) for k in range(len(parts))]
        bit *= 2
    return parts


def fetch(pairs, sem):
    copies = [pltpu.make_async_copy(a, b, sem.at[n]) for n, (a, b) in enumerate(pairs)]
    for copy in copies:
        copy.start()
    return copies


def pick_kernel(keep_hbm, raw_hbm, out_ref, keep_ref, raw_ref, sem):
    for copy in fetch([(keep_hbm, keep_ref), (raw_hbm, raw_ref)], sem):
        copy.wait()
    rows = lax.broadcasted_iota(jnp.int32, (raw_ref.shape[0], keep_ref.shape[1]), 0)
    hits = jnp.where(rows == keep_ref[...], 1.0, 0.0).astype(BF16)
    out_ref[...] = lax.dot_general(
        hits, raw_ref[...], (((0,), (0,)), ((), ())), preferred_element_type=F32
    ).astype(BF16)


def prepare_kernel(
    ids_hbm,
    gates_hbm,
    slot_hbm,
    weight_hbm,
    gain_hbm,
    query_hbm,
    weight_ref,
    gain_ref,
    query_ref,
    dense_ref,
    ids_ref,
    gates_ref,
    slot_ref,
    sem,
):
    early = query_hbm.at[pl.ds(0, query_ref.shape[0]), :]
    small = [(ids_hbm, ids_ref), (gates_hbm, gates_ref), (slot_hbm, slot_ref)]
    large = [(weight_hbm, weight_ref), (gain_hbm, gain_ref), (early, query_ref)]
    copies = fetch(small + large, sem)
    for copy in copies[:3]:
        copy.wait()
    ids = ids_ref[...]
    slots = jnp.zeros_like(ids)
    for e in range(slot_ref.shape[0]):
        slots = jnp.where(ids == e, slot_ref[e], slots)
    lane = lax.broadcasted_iota(jnp.int32, dense_ref.shape, 1)
    gates = jnp.zeros(dense_ref.shape, F32)
    for t in range(ids.shape[1]):
        gates = gates + jnp.where(lane == slots[:, t : t + 1], gates_ref[:, t : t + 1], 0.0)
    dense_ref[...] = gates
    for copy in copies[3:]:
        copy.wait()


def latent_kernel(spans, *refs):
    parts = refs[:spans]
    gain_ref, weight_ref, dense_ref, compact_ref, normed_ref, sent_ref = refs[spans:]
    index = here()[1]
    rows, block = parts[0].shape
    values = [p[...].astype(F32) for p in parts]
    square = sum(jnp.sum(v * v, axis=1, keepdims=True) for v in values)
    factor = lax.rsqrt(square / (spans * block) + EPS)
    for k in range(spans):
        at = pl.ds(pl.multiple_of((index ^ k) * block, block), block)
        compact_ref[:, at] = parts[k][...]
        normed_ref[:, at] = (values[k] * factor * gain_ref[:, at]).astype(BF16)
    sent_ref[0:rows, :] = jnp.zeros((rows, sent_ref.shape[1]), F32)
    sent_ref[0:rows, 0 : weight_ref.shape[0]] = nt(normed_ref[...], weight_ref[...])
    sent_ref[rows:, :] = dense_ref[...]


def rotated(values, cosine, sine):
    half = values.shape[1] // 2
    swapped = jnp.concatenate([values[:, half:], values[:, :half]], axis=1)
    return values * cosine + swapped * sine


def query_kernel(
    heads,
    raw_rows,
    normed_ref,
    early_ref,
    weight_hbm,
    keep_hbm,
    kv_hbm,
    moe_hbm,
    out_ref,
    cos_ref,
    sin_ref,
    live_ref,
    kv_ref,
    moe_ref,
    buf,
    keep_ref,
    sem,
):
    begun = early_ref.shape[0]
    steps, deep = buf.shape[:2]
    small = [(keep_hbm, keep_ref), (kv_hbm, kv_ref), (moe_hbm, moe_ref)]
    late = [(weight_hbm.at[pl.ds(begun + n * deep, deep), :], buf.at[n]) for n in range(steps)]
    copies = fetch(small + late, sem)
    copies[0].wait()
    rows, rope = cos_ref.shape
    diagonal = lax.broadcasted_iota(jnp.int32, (rows, rows), 0) == lax.broadcasted_iota(
        jnp.int32, (rows, rows), 1
    )
    listing = jnp.sum(
        jnp.where(diagonal, keep_ref[...].astype(F32), 0.0), axis=1, keepdims=True
    )
    live_ref[...] = jnp.where(listing >= 0, 1.0, 0.0)
    positions = (here()[0] * raw_rows).astype(F32) + jnp.maximum(listing, 0.0)
    half = rope // 2
    lane = lax.broadcasted_iota(jnp.int32, (rows, rope), 1)
    first = lane < half
    place = jnp.where(first, lane, lane - half).astype(F32)
    angles = positions * jnp.exp(place * (-2.0 / rope * math.log(THETA)))
    cos_ref[...] = jnp.cos(angles)
    sine = jnp.sin(angles)
    sin_ref[...] = jnp.where(first, -sine, sine)
    latent = early_ref.shape[1] // heads
    total = nn(normed_ref[:, :begun], early_ref[...])
    for n in range(steps):
        copies[3 + n].wait()
        at = begun + n * deep
        total = total + nn(normed_ref[:, at : at + deep], buf[n])
    kv_rank = latent - rope
    out_ref[...] = jnp.zeros(out_ref.shape, BF16)
    for h in range(heads):
        one = total[:, h * latent : (h + 1) * latent]
        out_ref[h * rows : (h + 1) * rows, 0:kv_rank] = one[:, :kv_rank].astype(BF16)
        out_ref[h * rows : (h + 1) * rows, kv_rank:latent] = rotated(
            one[:, kv_rank:], cos_ref[...], sin_ref[...]
        ).astype(BF16)
    for copy in copies[1:3]:
        copy.wait()


def cache_kernel(spans, width, experts, *refs):
    parts = refs[:spans]
    live_ref, gain_ref, cos_ref, sin_ref, query_ref, sent_ref = refs[spans:]
    rows = live_ref.shape[0]
    kv_rank = gain_ref.shape[1]
    values = natural([p[...] for p in parts], here()[1])
    latent = jnp.concatenate([v[:rows, :width] for v in values], axis=1)
    gates = jnp.concatenate([v[rows:, :experts] for v in values], axis=0)
    nope = latent[:, :kv_rank]
    factor = lax.rsqrt(jnp.mean(nope * nope, axis=1, keepdims=True) + EPS)
    nope = nope * factor * gain_ref[...]
    rope = rotated(latent[:, kv_rank:], cos_ref[...], sin_ref[...])
    high = gates.astype(BF16).astype(F32)
    used = rope.shape[1] + 2 * experts + 1
    tail = [rope, high, gates - high, live_ref[...]]
    rest = sent_ref.shape[1] - kv_rank - used
    if rest:
        tail.append(jnp.zeros((rows, rest), F32))
    sent_ref[:rows, :kv_rank] = nope.astype(BF16)
    sent_ref[:rows, kv_rank:] = jnp.concatenate(tail, axis=1).astype(BF16)
    sent_ref[rows:, :] = query_ref[...]


def emit_kernel(sent_ref, out_ref):
    out_ref[...] = sent_ref[: out_ref.shape[0], : out_ref.shape[1]]


def places(blocks):
    return list(range(0, blocks, 2)) + list(range(1, blocks, 2))


def attend_kernel(
    heads, kv_rank, flag_lane, blocks, mine_ref, theirs_ref, weight_hbm, out_ref, weight_ref, sem
):
    copy = pltpu.make_async_copy(weight_hbm, weight_ref, sem)
    copy.start()
    count = mine_ref.shape[1] // (1 + heads)
    index = here()[0]
    half = blocks // 2
    pieces = [(mine_ref, n) for n in range(half)] + [(theirs_ref, n) for n in range(half)]

    def gather(n):
        return jnp.concatenate(
            [ref[p, n * count : (n + 1) * count, :] for ref, p in pieces], axis=0
        )

    keys = gather(0)
    total, width = keys.shape
    lane = lax.broadcasted_iota(jnp.int32, (8, width), 1)
    flags = nt(jnp.where(lane == flag_lane, 1.0, 0.0).astype(BF16), keys)[0:1, :]

    shift = count.bit_length() - 1

    def slot(dims, axis):
        line = lax.broadcasted_iota(jnp.int32, dims, axis)
        if count == 1 << shift:
            at, rest = line >> shift, line & (count - 1)
        else:
            at, rest = line // count, line % count
        which = jnp.where(at < half, 2 * at, 2 * (at - half) + 1)
        return (which ^ index) * count + rest

    allowed = (slot((1, total), 1) <= slot((total, 1), 0)) & (flags > 0)
    result = jnp.zeros(out_ref.shape, F32)
    for h in range(heads):
        scores = nt(gather(1 + h), keys) * SCALE
        scores = jnp.where(allowed, scores, NEGATIVE)
        highest = jnp.max(scores, axis=1, keepdims=True)
        weight = jnp.where(allowed, jnp.exp(scores - highest), 0.0)
        share = 1.0 / jnp.sum(weight, axis=1, keepdims=True)
        summed = nn(weight.astype(BF16), keys[:, :kv_rank])
        mixed = (summed * share).astype(BF16)
        if h == 0:
            copy.wait()
        result = result + nn(mixed, weight_ref[h * kv_rank : (h + 1) * kv_rank, :])
    out_ref[...] = result.astype(BF16)


def sum_kernel(*refs):
    refs[-1][...] = sum(ref[...].astype(F32) for ref in refs[:-1]).astype(BF16)


def scaled_rows(blocks, odd, pieces_ref, mine_rows, their_rows, gain_ref, part_ref, rows_ref):
    order = places(blocks)
    half = blocks // 2
    index = here()[0]
    count, width = mine_rows.shape[1], pieces_ref.shape[2]
    squares = [jnp.zeros((count, 1), F32)] * blocks
    for p in range(half):
        i = 2 * p + odd
        lanes = pl.ds(pl.multiple_of((index ^ i) * width, width), width)
        gain = gain_ref[:, lanes]
        for at, j in enumerate(order):
            to = order.index(i ^ j)
            rows = mine_rows if to < half else their_rows
            resid = rows[to % half, :, lanes].astype(F32) + pieces_ref[
                p, at * count : (at + 1) * count, :
            ].astype(F32)
            squares[to] = squares[to] + jnp.sum(resid * resid, axis=1, keepdims=True)
            rows_ref[to * count : (to + 1) * count, p * width : (p + 1) * width] = (
                resid * gain
            ).astype(BF16)
            if to == 0:
                part_ref[:, p * width : (p + 1) * width] = resid
    return jnp.concatenate(squares, axis=0)


def products(blocks, odd, width, rows_ref, in_ref, half, start, size):
    index = here()[0]
    total = jnp.zeros((rows_ref.shape[0], size), F32)
    for p in range(blocks // 2):
        lanes = pl.ds(pl.multiple_of((index ^ (2 * p + odd)) * width, width), width)
        total = total + nt(
            rows_ref[:, p * width : (p + 1) * width], in_ref[half, start : start + size, lanes]
        )
    return total


def begin_kernel(
    blocks,
    cuts,
    mine_ref,
    mine_rows,
    their_rows,
    gain_ref,
    in_ref,
    part_ref,
    square_ref,
    gate_ref,
    upper_ref,
    rows_ref,
):
    square_ref[...] = scaled_rows(
        blocks, 0, mine_ref, mine_rows, their_rows, gain_ref, part_ref, rows_ref
    )
    width = mine_ref.shape[2]
    for start, size in cuts:
        at = slice(start, start + size)
        gate_ref[:, at] = products(blocks, 0, width, rows_ref, in_ref, 0, start, size)
        upper_ref[:, at] = products(blocks, 0, width, rows_ref, in_ref, 1, start, size)


def expert_kernel(
    blocks,
    first_lane,
    tail_at,
    experts,
    cuts,
    columns,
    theirs_ref,
    mine_rows,
    their_rows,
    gain_ref,
    in_ref,
    part_ref,
    square_ref,
    gate_ref,
    upper_ref,
    mine_tail_ref,
    theirs_tail_ref,
    out_weight_ref,
    near_ref,
    far_ref,
    own_ref,
    act_ref,
    scale_ref,
    rows_ref,
    rest_ref,
    whole_ref,
):
    square = square_ref[...] + scaled_rows(
        blocks, 1, theirs_ref, mine_rows, their_rows, gain_ref, rest_ref, rows_ref
    )
    index = here()
    width = theirs_ref.shape[2]
    for p in range(blocks // 2):
        for odd, ref in enumerate((part_ref, rest_ref)):
            lanes = pl.ds(pl.multiple_of((index[0] ^ (2 * p + odd)) * width, width), width)
            whole_ref[:, lanes] = ref[:, p * width : (p + 1) * width]
    size = own_ref.shape[0]
    own_ref[...] = whole_ref[pl.ds(pl.multiple_of(index[1] * size, size), size), :]
    factor = lax.rsqrt(square / (blocks * width) + EPS)
    for start, size in cuts:
        at = slice(start, start + size)
        gate = factor * (
            gate_ref[:, at] + products(blocks, 1, width, rows_ref, in_ref, 0, start, size)
        )
        upper = factor * (
            upper_ref[:, at] + products(blocks, 1, width, rows_ref, in_ref, 1, start, size)
        )
        act_ref[:, at] = (gate / (1.0 + jnp.exp(-gate)) * upper).astype(BF16)
    half = near_ref.shape[0]
    pieces = mine_tail_ref.shape[0]
    count = half // pieces
    tail = jnp.concatenate(
        [ref[p, :count, tail_at:] for ref in (mine_tail_ref, theirs_tail_ref) for p in range(pieces)],
        axis=0,
    )
    tail = tail.astype(F32)
    lane = lax.broadcasted_iota(jnp.int32, tail.shape, 1) - first_lane
    slot = lax.div(index[0] * lax.axis_size("span") + index[1], 2)
    scale = jnp.sum(
        jnp.where((lane == slot) | (lane == slot + experts), tail, 0.0), axis=1, keepdims=True
    )
    scale_ref[...] = scale
    project(0, columns, scale, act_ref, out_weight_ref, near_ref, far_ref)


def project(first, columns, scale, act_ref, weight_ref, near_ref, far_ref):
    half, width = near_ref.shape
    wide = width // columns
    for n in range(columns):
        span = slice(n * wide, (n + 1) * wide)
        done = nn(act_ref[...], weight_ref[:, first + n * wide : first + (n + 1) * wide])
        done = jnp.where(scale > 0, done * scale, 0.0).astype(BF16)
        near_ref[:, span] = done[:half]
        far_ref[:, span] = done[half:]


def finish_kernel(columns, act_ref, scale_ref, weight_ref, near_ref, far_ref):
    project(near_ref.shape[1], columns, scale_ref[...], act_ref, weight_ref, near_ref, far_ref)


def level_kernel(*refs):
    parts, outs = refs[:4], refs[4:]
    rows = outs[0].shape[0]
    width = parts[0].shape[1]
    for n, out in enumerate(outs):
        at = slice(n * rows, (n + 1) * rows)
        for side in range(2):
            near_ref, back_ref = parts[2 * side : 2 * side + 2]
            out[:, side * width : (side + 1) * width] = (
                near_ref[at, :].astype(F32) + back_ref[at, :].astype(F32)
            ).astype(out.dtype)


def rows_kernel(spans, *refs):
    parts, outs, buf = refs[: -spans - 1], refs[-spans - 1 : -1], refs[-1]
    index = here()[1]
    total = parts[0][...]
    for p in parts[1:]:
        total = total + p[...].astype(F32)
    buf[...] = total
    count = outs[0].shape[0]
    for k, out in enumerate(outs):
        at = pl.ds(pl.multiple_of((index ^ k) * count, count), count)
        out[...] = buf[at, :].astype(out.dtype)


def last_kernel(spans, *refs):
    parts = refs[:spans]
    own_ref, live_ref, out_ref = refs[spans:]
    count = out_ref.shape[0]
    routed = sum(p[...].astype(F32) for p in parts)
    at = pl.ds(pl.multiple_of(here()[1] * count, count), count)
    total = own_ref[...] + routed
    out_ref[...] = jnp.where(live_ref[at, :] > 0, total, 0.0).astype(BF16)


def per_device(
    raw_tokens,
    keep,
    attn_gain,
    query_weight,
    latent_weight,
    kv_gain,
    out_weight,
    moe_gain,
    expert_ids,
    gate_values,
    expert_slot,
    expert_in,
    expert_out,
):
    kv_rank = kv_gain.shape[0]
    spans = lax.axis_size("span")
    contexts = lax.axis_size("context")
    part_width = latent_weight.shape[1]
    latent_width = part_width * spans
    rope = latent_width - kv_rank
    model = attn_gain.shape[0]
    kept = keep.shape[1]
    raw_rows = raw_tokens.shape[0]
    heads = query_weight.shape[1] // latent_width
    rows_dev = expert_ids.shape[0]
    experts = expert_slot.shape[0]
    hidden = expert_in.shape[3]
    evens = list(range(0, contexts, 2))

    picked = call(
        pick_kernel,
        shape((kept, raw_tokens.shape[1]), BF16),
        [HBM] * 2,
        (keep, raw_tokens),
        scratch=[
            pltpu.VMEM(keep.shape, jnp.int32),
            pltpu.VMEM(raw_tokens.shape, BF16),
            pltpu.SemaphoreType.DMA((2,)),
        ],
        limit=4,
    )
    parts = gathered(picked, "span", range(1, spans))

    sent_width = up(max(part_width, experts))
    begun = model // EARLY
    near_weight, gain, early_query, dense = call(
        prepare_kernel,
        [
            shape((part_width, model), BF16),
            shape((1, model), F32),
            shape((begun, query_weight.shape[1]), BF16),
            shape((rows_dev, sent_width), F32),
        ],
        [HBM] * 6,
        (expert_ids, gate_values, expert_slot, latent_weight.T, attn_gain[None], query_weight),
        scratch=[
            pltpu.VMEM(expert_ids.shape, jnp.int32),
            pltpu.VMEM(gate_values.shape, F32),
            pltpu.SMEM(expert_slot.shape, jnp.int32),
            pltpu.SemaphoreType.DMA((6,)),
        ],
        moved=query_weight.size,
        limit=8,
    )

    compact, normed, sent = call(
        functools.partial(latent_kernel, spans),
        [
            shape((kept, model), BF16),
            shape((kept, model), BF16),
            shape((kept + rows_dev, sent_width), F32),
        ],
        [VM] * (spans + 3),
        (*parts, gain, near_weight, dense),
        flops=2 * kept * latent_weight.size,
        moved=2 * latent_weight.size,
        limit=4,
    )
    parts = gathered(sent, "span", range(1, spans))
    row_width = up(latent_width + 2 * experts + 1)
    steps = 3
    query, cosine, sine, live, near_kv, near_moe = call(
        functools.partial(query_kernel, heads, raw_rows),
        [
            shape((heads * kept, row_width), BF16),
            shape((kept, rope), F32),
            shape((kept, rope), F32),
            shape((kept, 1), F32),
            shape((1, kv_rank), F32),
            shape((1, model), F32),
        ],
        [VM, VM] + [HBM] * 4,
        (normed, early_query, query_weight, keep, kv_gain[None], moe_gain[None]),
        scratch=[
            pltpu.VMEM((steps, (model - begun) // steps, query_weight.shape[1]), BF16),
            pltpu.VMEM(keep.shape, jnp.int32),
            pltpu.SemaphoreType.DMA((steps + 3,)),
        ],
        flops=2 * kept * query_weight.size,
        moved=query_weight.size,
        limit=10,
    )
    sent = call(
        functools.partial(cache_kernel, spans, part_width, experts),
        shape(((1 + heads) * kept, row_width), BF16),
        [VM] * (spans + 5),
        (*parts, live, near_kv, cosine, sine, query),
        limit=4,
    )

    cached = call(emit_kernel, shape((kept, latent_width), BF16), [VM], (sent,), limit=4)

    mine_keys = jnp.stack(gathered(sent, "context", evens[1:]))
    their_keys = partner(mine_keys, "context", 1)
    partial = call(
        functools.partial(attend_kernel, heads, kv_rank, latent_width + 2 * experts, contexts),
        shape((contexts * kept, out_weight.shape[1]), BF16),
        [VM, VM, HBM],
        (mine_keys, their_keys, out_weight),
        scratch=[pltpu.VMEM(out_weight.shape, BF16), pltpu.SemaphoreType.DMA],
        flops=2 * kept * contexts * out_weight.size,
        moved=2 * out_weight.size,
        limit=12,
    )

    column, bit = partial, 1
    while bit < spans:
        column = call(
            sum_kernel,
            shape(partial.shape, BF16),
            [VM] * 2,
            gathered(column, "span", [bit]),
            limit=4,
        )
        bit *= 2
    mine_rows = jnp.stack(gathered(compact, "context", evens[1:]))
    their_rows = partner(mine_rows, "context", 1)

    mine = jnp.stack(gathered(column, "context", evens[1:]))
    theirs = partner(mine, "context", 1)
    half = mine.shape[0] * kept
    cuts, start = [], 0
    while start < hidden:
        size = min(2 * LANES, hidden - start)
        cuts.append((start, size))
        start += size
    weights_in = jnp.swapaxes(expert_in[0], 1, 2)
    begun = call(
        functools.partial(begin_kernel, contexts, cuts),
        [
            shape((kept, model // 2), F32),
            shape((2 * half, 1), F32),
            shape((2 * half, hidden), F32),
            shape((2 * half, hidden), F32),
        ],
        [VM] * 5,
        (mine, mine_rows, their_rows, near_moe, weights_in),
        scratch=[pltpu.VMEM((2 * half, model // 2), BF16)],
        flops=2 * 2 * half * hidden * model,
        moved=4 * hidden * model,
        limit=20,
    )
    side = model // 2
    near, far, own, act, scale = call(
        functools.partial(
            expert_kernel, contexts, latent_width - kv_rank, kv_rank, experts, cuts, 2
        ),
        [
            shape((half, side), BF16),
            shape((half, side), BF16),
            shape((rows_dev, model), F32),
            shape((2 * half, hidden), BF16),
            shape((2 * half, 1), F32),
        ],
        [VM] * 12,
        (
            theirs,
            mine_rows,
            their_rows,
            near_moe,
            weights_in,
            *begun,
            mine_keys,
            their_keys,
            expert_out[0],
        ),
        scratch=[
            pltpu.VMEM((2 * half, model // 2), BF16),
            pltpu.VMEM((kept, model // 2), F32),
            pltpu.VMEM((kept, model), F32),
        ],
        flops=4 * 2 * half * hidden * model,
        moved=4 * hidden * model,
        limit=20,
    )

    back = partner(far, "context", 1)
    later, far = call(
        functools.partial(finish_kernel, 2),
        [shape((half, side), BF16), shape((half, side), BF16)],
        [VM] * 3,
        (act, scale, expert_out[0]),
        flops=2 * half * hidden * model,
        moved=hidden * model,
        limit=12,
    )
    later_back = partner(far, "context", 1)

    levels = call(
        level_kernel,
        [shape((kept, model), F32)] + [shape((kept, model), BF16)] * (len(evens) - 1),
        [VM] * 4,
        (near, back, later, later_back),
        limit=6,
    )
    got = []
    for level, i in zip(levels[1:], evens[1:]):
        got.append(partner(level, "context", i))
    rows = call(
        functools.partial(rows_kernel, spans),
        [shape((rows_dev, model), F32)] + [shape((rows_dev, model), BF16)] * (spans - 1),
        [VM] * len(levels),
        (levels[0], *got),
        scratch=[pltpu.VMEM((kept, model), F32)],
        limit=6,
    )
    got = []
    for k in range(1, spans):
        got.append(partner(rows[k], "span", k))
    layer_out = call(
        functools.partial(last_kernel, spans),
        shape((rows_dev, model), BF16),
        [VM] * (spans + 2),
        (rows[0], *got, own, live),
        limit=4,
    )
    return (layer_out, cached)


def solution(mesh):
    placed = (
        P(("groups", "context"), "span"),
        P(("groups", "context"), None),
        P(),
        P(None, "span"),
        P(None, "span"),
        P(),
        P("span", "context"),
        P(),
        P(("groups", "context", "span"), None),
        P(("groups", "context", "span"), None),
        P(),
        P(("context", "span"), None, None, None),
        P(("context", "span"), None, None),
    )
    return jax.shard_map(
        per_device,
        mesh=mesh,
        in_specs=placed,
        out_specs=(P(("groups", "context", "span"), None), P(("groups", "context"), None)),
        check_vma=False,
    )
```
